32 devices in a mesh: rows: 16 (over z, y, core), tm: 2 (over x).
Axes of the slice: x: 2, y: 2, z: 4, core: 2. Of those that a mesh axis runs over, the one named last changes fastest.
Arguments:
- tokens: bfloat16 [16, 1024, 1024], P('rows', 'tm')
- cotangent: float32 [16, 1024, 1024], P('rows', 'tm'), may hold values from -6 to 6
- segment_ids: int32 [16, 1024], P('rows', 'tm'), may hold values from 0 to 5, never falling along the last dimension, each value on 1 to 341 neighbouring positions
- rel_bucket: int32 [513], replicated, may hold values from 0 to 127, as said below
- ffn1_in: bfloat16 [1024, 4096], P('rows'), may hold values from -0.1875 to 0.1875
- ffn1_out: bfloat16 [4096, 1024], P('rows'), may hold values from -0.09375 to 0.09375
- qkv_weight: bfloat16 [1024, 3072], P('rows'), may hold values from -0.1875 to 0.1875
- attn_out: bfloat16 [1024, 1024], P('rows'), may hold values from -0.75 to 0.75
- glu_in: bfloat16 [1024, 2048], P('rows'), may hold values from -0.1875 to 0.1875
- conv_out: bfloat16 [1024, 1024], P('rows'), may hold values from -0.1875 to 0.1875
- ffn2_in: bfloat16 [1024, 4096], P('rows'), may hold values from -0.1875 to 0.1875
- ffn2_out: bfloat16 [4096, 1024], P('rows'), may hold values from -0.09375 to 0.09375
- gains: bfloat16 [6, 1024], P(None, 'rows'), may hold values from 0.5 to 1.5
- shifts: bfloat16 [14, 1024], P(None, 'rows'), may hold values from -2 to 2
- ffn_bias: bfloat16 [2, 4096], P(None, 'rows'), may hold values from -2 to 2
- conv_kernel: bfloat16 [5, 1024], P(None, 'rows'), may hold values from -3 to 3
- rel_table: bfloat16 [1024], P('rows'), may hold values from -4 to 4
Outputs:
- output: float32 [16, 1024, 1024], P('rows', 'tm')
- tokens_grad: float32 [16, 1024, 1024], P('rows', 'tm')
- ffn1_in_grad: float32 [1024, 4096], P('rows')
- ffn1_out_grad: float32 [4096, 1024], P('rows')
- qkv_weight_grad: float32 [1024, 3072], P('rows')
- attn_out_grad: float32 [1024, 1024], P('rows')
- glu_in_grad: float32 [1024, 2048], P('rows')
- conv_out_grad: float32 [1024, 1024], P('rows')
- ffn2_in_grad: float32 [1024, 4096], P('rows')
- ffn2_out_grad: float32 [4096, 1024], P('rows')
- gains_grad: float32 [6, 1024], P(None, 'rows')
- shifts_grad: float32 [14, 1024], P(None, 'rows')
- ffn_bias_grad: float32 [2, 4096], P(None, 'rows')
- conv_kernel_grad: float32 [5, 1024], P(None, 'rows')
- rel_table_grad: float32 [1024], P('rows')
The draws below stay inside these ranges and needn't reach their ends.
Inputs may be any that keep to these rules, and one draw needn't show every extreme that they name: `segment_ids`: within a row the ids never fall; every utterance has 1 to 341 frames, the longest exactly that. `rel_bucket`: never falls from distance -256 to +256; 0 at -256 and 127 at +256.
All inputs are finite; a program needn't handle non-finite values.
Results may differ from the reference program's by a relative error of at most 0.035.
Values may be sent and summed in bfloat16 or wider, within the bound.
A program may use at most 320 MiB of HBM per device.

```python
import math
import jax
import jax.numpy as jnp
import numpy as np
from jax import lax

D = 1024
HEADS = 8
FF = 4096
KSIZE = 5
NB = 128
MAXD = 256
UTTS = 6
FRAMES = 1024
NROWS = 16


def draw_tokens(key, part):
    noise_key, direction_key = jax.random.split(jax.random.fold_in(key, 11))
    ramp = jnp.arange(NROWS, dtype=jnp.float32) / max(NROWS - 1, 1)
    noise = jax.random.normal(noise_key, (NROWS, FRAMES, D), jnp.float32)
    amplitude = 0.4 + 0.8 * ramp
    direction = jax.random.normal(direction_key, (NROWS, 1, D), jnp.float32)
    return (noise + amplitude[:, None, None] * direction).astype(jnp.bfloat16)


def draw_rel_bucket(key, part):
    order = jax.random.permutation(jax.random.fold_in(key, 23), 2 * MAXD)
    steps = jnp.zeros((2 * MAXD,), jnp.int32).at[order[:NB - 1]].set(1)
    return jnp.concatenate([jnp.zeros((1,), jnp.int32), jnp.cumsum(steps).astype(jnp.int32)])


def block_scale(stream_key, shape, shards, smallest, top_value):
    level, own = 1.0, jax.random.fold_in(stream_key, 6)
    for dim, shards_of in shards:
        draws = jnp.exp(jax.random.uniform(jax.random.fold_in(own, dim), (shards_of,), jnp.float32, smallest / len(shards), top_value / len(shards)))
        level = level * jnp.repeat(draws, shape[dim] // shards_of).reshape([-1 if axis == dim else 1 for axis in range(len(shape))])
    return level


def length_profile(count, total, limit, skew):
    portions = [(1 << 20) // math.isqrt(rank ** skew) + 1 for rank in range(2, count + 1)]
    surplus, counts = total - limit - (count - 1), [1] * (count - 1)
    while surplus > 0:
        candidates = [i for i in range(count - 1) if counts[i] < limit]
        mass, budget = sum([portions[i] for i in candidates]), surplus
        for i in candidates:
            more = min(limit - counts[i], max(1, budget * portions[i] // mass), surplus)
            counts[i] = counts[i] + more
            surplus = surplus - more
    return np.array([limit] + counts)


def ragged_sizes(rng, number_of, total, most, slope):
    if number_of == 2:
        one = jax.random.randint(rng, (), max(1, total - most), min(most, total - 1) + 1)
        return jnp.stack([one, total - one])
    tallies = jnp.asarray(length_profile(number_of, total, most, slope), jnp.int32)
    twos = (number_of - 1) // 2
    donor, sink = tallies[1:1 + 2 * twos:2], tallies[2:2 + 2 * twos:2]
    margin = jnp.minimum(donor - 1, most - sink)
    moved = jax.random.randint(jax.random.fold_in(rng, 1), (twos,), 0, 1 << 20) % (margin + 1)
    tallies = tallies.at[1:1 + 2 * twos:2].set(donor - moved).at[2:2 + 2 * twos:2].set(sink + moved)
    return tallies[jax.random.permutation(jax.random.fold_in(rng, 2), number_of)]


def bell_draw(rng, shape, width, reach, pieces=(), kind=jnp.bfloat16):
    drawn = width * jax.random.normal(rng, shape, jnp.float32)
    if pieces:
        drawn = drawn * block_scale(rng, shape, pieces, -0.22, 0.18)
    return jnp.clip(drawn, -reach, reach).astype(kind)


def setup_inputs(seed: int = 0) -> dict:
    key_of = jax.random.split(jax.random.key(seed), 18)
    return {
        "tokens": draw_tokens(jax.random.fold_in(key_of[17], 71), 0),
        "cotangent": bell_draw(key_of[1], (NROWS, FRAMES, D), 1.0, 6.0, ((0, 16), (1, 2)), jnp.float32),
        "segment_ids": jax.vmap(lambda own: jnp.searchsorted(jnp.cumsum(ragged_sizes(own, UTTS, FRAMES, FRAMES // 3, 1)), jnp.arange(FRAMES), side="right"))(jax.random.split(key_of[2], NROWS)).reshape((NROWS, FRAMES)).astype(jnp.int32),
        "rel_bucket": draw_rel_bucket(jax.random.fold_in(key_of[17], 71), 0),
        "ffn1_in": bell_draw(key_of[4], (D, FF), D ** -0.5, 0.1875, ((0, 16),)),
        "ffn1_out": bell_draw(key_of[5], (FF, D), FF ** -0.5, 0.09375, ((0, 16),)),
        "qkv_weight": bell_draw(key_of[6], (D, 3 * D), D ** -0.5, 0.1875, ((0, 16),)),
        "attn_out": bell_draw(key_of[7], (D, D), (D // 16) ** -0.5, 0.75, ((0, 16),)),
        "glu_in": bell_draw(key_of[8], (D, 2 * D), D ** -0.5, 0.1875, ((0, 16),)),
        "conv_out": bell_draw(key_of[9], (D, D), D ** -0.5, 0.1875, ((0, 16),)),
        "ffn2_in": bell_draw(key_of[10], (D, FF), D ** -0.5, 0.1875, ((0, 16),)),
        "ffn2_out": bell_draw(key_of[11], (FF, D), FF ** -0.5, 0.09375, ((0, 16),)),
        "gains": jnp.clip(1.0 + 0.1 * jax.random.normal(key_of[12], (6, D), jnp.float32), 0.5, 1.5).astype(jnp.bfloat16),
        "shifts": bell_draw(key_of[13], (14, D), 0.3, 2.0, ((1, 16),)),
        "ffn_bias": bell_draw(key_of[14], (2, FF), 0.3, 2.0, ((1, 16),)),
        "conv_kernel": bell_draw(key_of[15], (KSIZE, D), 0.5, 3.0, ((1, 16),)),
        "rel_table": bell_draw(key_of[16], (HEADS * NB,), 1.0, 4.0, ((0, 16),)),
    }


@jax.custom_vjp
def low(v):
    return lax.optimization_barrier(v.astype(jnp.bfloat16)).astype(jnp.float32)

@jax.custom_vjp
def low_back(v):
    return v

def low_keep(v):
    return (low(v), None)

def low_pass(kept, grad):
    return (grad,)

def back_keep(v):
    return (v, None)

def back_low(kept, grad):
    return (low(grad),)
low.defvjp(low_keep, low_pass)
low_back.defvjp(back_keep, back_low)
EPS = 1e-05
NEG = -1e+30
HIGH = lax.Precision.HIGHEST

def layer_norm(value, gain, shift):
    batch_mean = lax.optimization_barrier(jnp.mean(value, axis=-1, keepdims=True))
    centred = value - batch_mean
    spread = lax.optimization_barrier(jnp.mean(centred * centred, axis=-1, keepdims=True))
    return centred * lax.rsqrt(spread + EPS) * gain + shift

def dense(value, weight):
    return jnp.dot(value, weight, precision=HIGH)

def feed_forward(resid, gain, shift, w_in, b_in, w_out, b_out):
    normed = low(layer_norm(resid, gain, shift))
    hidden = low_back(dense(normed, w_in) + b_in)
    active = low(jax.nn.silu(hidden))
    return resid + 0.5 * low_back(dense(active, w_out) + b_out)

def attend_row(inputs, table):
    query, keys, values, seg = inputs
    scale = 1.0 / math.sqrt(query.shape[-1])
    scores = jnp.einsum('ihd,jhd->hij', query, keys, precision=HIGH) * scale + table
    scores = low_back(scores)
    same = (seg[:, None] == seg[None, :])[None]
    scores = jnp.where(same, scores, NEG)
    shifted = scores - lax.optimization_barrier(jnp.max(scores, axis=-1, keepdims=True))
    weights = jnp.exp(shifted)
    probs = low(weights / lax.optimization_barrier(jnp.sum(weights, axis=-1, keepdims=True)))
    return jnp.einsum('hij,jhd->ihd', probs, values, precision=HIGH)

def attention(resid, gain, shift, w_qkv, b_query, b_value, w_out, b_out, segment_ids, table):
    normed = low(layer_norm(resid, gain, shift))
    biases = jnp.concatenate([b_query, jnp.zeros_like(b_query), b_value])
    mixed = low(low_back(dense(normed, w_qkv) + biases))
    nrows = resid.shape[0]
    frames = resid.shape[1]
    split = mixed.reshape(nrows, frames, 3, HEADS, D // HEADS)
    attended = lax.map(jax.checkpoint(lambda inputs: attend_row(inputs, table)), (split[:, :, 0], split[:, :, 1], split[:, :, 2], segment_ids))
    attended = low(low_back(attended.reshape(nrows, frames, D)))
    return resid + low_back(dense(attended, w_out) + b_out)

def convolution(resid, gain, shift, w_glu, b_value, b_gate, kernel, bn_gain, bn_shift, w_out, b_out, segment_ids):
    normed = low(layer_norm(resid, gain, shift))
    pre = low_back(dense(normed, w_glu) + jnp.concatenate([b_value, b_gate]))
    gated = low(pre[..., :D] * jax.nn.sigmoid(pre[..., D:]))
    half = (KSIZE - 1) // 2
    frames = segment_ids.shape[1]
    padded = jnp.pad(gated, ((0, 0), (half, half), (0, 0)))
    seg_pad = jnp.pad(segment_ids, ((0, 0), (half, half)), constant_values=-1)
    convolved_rows = jnp.zeros_like(gated)
    for tap in range(KSIZE):
        same = (seg_pad[:, tap:tap + frames] == segment_ids)[..., None]
        convolved_rows = convolved_rows + kernel[tap] * jnp.where(same, padded[:, tap:tap + frames], 0.0)
    convolved_rows = low_back(convolved_rows)
    batch_mean = lax.optimization_barrier(jnp.mean(convolved_rows, axis=(0, 1)))
    spread = lax.optimization_barrier(jnp.mean(jnp.square(convolved_rows - batch_mean), axis=(0, 1)))
    normalized_rows = (convolved_rows - batch_mean) * lax.rsqrt(spread + EPS) * bn_gain + bn_shift
    active = low(jax.nn.silu(normalized_rows))
    return resid + low_back(dense(active, w_out) + b_out)

def reference(tokens, cotangent, segment_ids, rel_bucket, ffn1_in, ffn1_out, qkv_weight, attn_out, glu_in, conv_out, ffn2_in, ffn2_out, gains, shifts, ffn_bias, conv_kernel, rel_table):
    frames = segment_ids.shape[1]
    position = jnp.arange(frames, dtype=jnp.int32)
    distance = jnp.clip(position[None, :] - position[:, None], -MAXD, MAXD) + MAXD
    bucket = rel_bucket[distance]

    def forward(x, w1i, w1o, wqkv, wao, wglu, wco, w2i, w2o, gain_rows, shift_rows, hidden_bias, kernel, table_flat):
        table = table_flat.reshape(HEADS, NB)[:, bucket]
        x = feed_forward(x, gain_rows[0], shift_rows[0], w1i, hidden_bias[0], w1o, shift_rows[6])
        x = attention(x, gain_rows[1], shift_rows[1], wqkv, shift_rows[7], shift_rows[8], wao, shift_rows[9], segment_ids, table)
        x = convolution(x, gain_rows[2], shift_rows[2], wglu, shift_rows[10], shift_rows[11], kernel, gain_rows[5], shift_rows[5], wco, shift_rows[12], segment_ids)
        x = feed_forward(x, gain_rows[3], shift_rows[3], w2i, hidden_bias[1], w2o, shift_rows[13])
        return layer_norm(x, gain_rows[4], shift_rows[4])
    floats = [arr.astype(jnp.float32) for arr in (tokens, ffn1_in, ffn1_out, qkv_weight, attn_out, glu_in, conv_out, ffn2_in, ffn2_out, gains, shifts, ffn_bias, conv_kernel, rel_table)]
    output, pullback = jax.vjp(forward, *floats)
    grads = pullback(cotangent.astype(jnp.float32))
    return (output, grads[0], grads[1], grads[2], grads[3], grads[4], grads[5], grads[6], grads[7], grads[8], grads[9], grads[10], grads[11], grads[12], grads[13])
```

```python
import functools
import math

import jax
import jax.numpy as jnp
import numpy as np
from jax import lax
from jax.experimental import pallas as pl
from jax.experimental.pallas import tpu as pltpu
from jax.sharding import PartitionSpec as P

HEADS = 8
KSIZE = 5
NB = 128
MAXD = 256


EPS = 1e-05
NEG = -1e30
HIGH = lax.Precision.HIGHEST


MESH = pl.DeviceIdType.MESH
ANY = pl.ANY


def place():
    r = lax.axis_index("rows")
    t = lax.axis_index("tm")
    return r, t, lax.rem(r, 2), lax.rem(r // 2, 2), r // 4


def remote(src, dst, send, recv, rows, tm):
    pltpu.make_async_remote_copy(
        src_ref=src, dst_ref=dst, send_sem=send, recv_sem=recv,
        device_id=(rows, tm), device_id_type=MESH,
    ).start()


def landed(ref, sem):
    pltpu.make_async_copy(ref, ref, sem).wait()


def greet(peers):
    barrier = pltpu.get_barrier_semaphore()
    for rows, tm in peers:
        pl.semaphore_signal(barrier, inc=1, device_id=(rows, tm), device_id_type=MESH)
    pl.semaphore_wait(barrier, len(peers))


def link_peers():
    r, t, c, y, z = place()
    return [(r + 1 - 2 * c, t), (r + 2 - 4 * y, t), (lax.rem(r + 4, 16), t), (lax.rem(r + 12, 16), t), (r, 1 - t)]


def loop(n, fn, first=0):
    def one(i, carry):
        fn(i)
        return carry
    lax.fori_loop(first, n, one, 0)


UNIT = 64
EDGE = 24
MIDDLE = UNIT - 2 * EDGE
PLANE = EDGE + MIDDLE


class Gather:
    LEAD = 3
    EVENTS = (("from_z", 1, 0), ("from_y", 0, 0), ("from_z", 2, 1), ("from_y", 1, 1), ("from_x", 0, 1), ("from_z", 3, 2),
              ("from_y", 2, 2), ("from_x", 1, 2), ("from_y", 3, 3), ("from_x", 2, 3), ("from_x", 3, 4))
    LAG = 4

    def __init__(self, full, first, units, sems):
        self.full, self.first, self.units = full, first, units
        self.zr, self.yr, self.xr, self.cr, self.snd = sems
        self.r, self.t, self.c, self.y, self.z = place()
        self.taken = set()

    @staticmethod
    def scratch(units):
        sem = pltpu.SemaphoreType.DMA
        return [sem((units, 4)), sem((units, 4)), sem((units, 8)), sem((units,)), sem((5,))]

    def slot(self, z, y):
        return z * 4 + y * 2 + self.c

    def rows_of(self, unit, start, size):
        return pl.ds(pl.multiple_of((unit + self.first) * UNIT + start, 8), size)

    def inplane(self, slot, unit):
        return self.full.at[slot, self.rows_of(unit, self.t * EDGE, PLANE)]

    def edge(self, slot, unit, tm):
        return self.full.at[slot, self.rows_of(unit, tm * PLANE, EDGE)]

    def to_core(self, ref, unit):
        remote(ref, ref, self.snd.at[4], self.cr.at[unit], self.r + 1 - 2 * self.c, self.t)

    def send_own(self, unit):
        r, t, z = self.r, self.t, self.z
        plane = self.inplane(r, unit)

        @pl.when(z < 3)
        def _():
            remote(plane, plane, self.snd.at[0], self.zr.at[unit, z], r + 4, t)

        @pl.when(z > 0)
        def _():
            remote(plane, plane, self.snd.at[1], self.zr.at[unit, z], r - 4, t)

        remote(plane, plane, self.snd.at[2], self.yr.at[unit, z], self.slot(z, 1 - self.y), t)
        self.to_core(self.full.at[r, self.rows_of(unit, 0, UNIT)], unit)

    def pass_on(self, unit, z, y):
        s = self.slot(z, y)
        part = self.edge(s, unit, self.t)
        remote(part, part, self.snd.at[3], self.xr.at[unit, z * 2 + y], self.r, 1 - self.t)
        self.to_core(self.inplane(s, unit), unit)

    def from_z(self, unit, distance):
        for sign in (-1, 1):
            z = self.z + sign * distance

            @pl.when((z >= 0) & (z <= 3))
            def _(z=z, sign=sign):
                plane = self.inplane(self.slot(z, self.y), unit)
                landed(plane, self.zr.at[unit, z])
                onward = self.z - sign

                @pl.when((onward >= 0) & (onward <= 3))
                def _():
                    remote(plane, plane, self.snd.at[0 if sign < 0 else 1], self.zr.at[unit, z], self.slot(onward, self.y), self.t)

                remote(plane, plane, self.snd.at[2], self.yr.at[unit, z], self.slot(self.z, 1 - self.y), self.t)
                self.pass_on(unit, z, self.y)

    def from_y(self, unit, distance):
        for sign in (-1, 1) if distance else (1,):
            z = self.z + sign * distance

            @pl.when((z >= 0) & (z <= 3))
            def _(z=z):
                landed(self.inplane(self.slot(z, 1 - self.y), unit), self.yr.at[unit, z])
                self.pass_on(unit, z, 1 - self.y)

    def from_x(self, unit, distance):
        for other in (False, True) if distance else (True,):
            y = 1 - self.y if other else self.y
            for sign in (-1, 1) if distance else (1,):
                z = self.z + sign * distance

                @pl.when((z >= 0) & (z <= 3))
                def _(z=z, y=y):
                    part = self.edge(self.slot(z, y), unit, 1 - self.t)
                    landed(part, self.xr.at[unit, z * 2 + y])
                    self.to_core(part, unit)

    def begin(self):
        for unit in range(min(self.LEAD, self.units)):
            self.send_own(unit)

    def tick(self, step):
        for name, distance, lag in self.EVENTS:
            unit = step - lag

            @pl.when((unit >= 0) & (unit < self.units))
            def _(name=name, distance=distance, unit=unit):
                getattr(self, name)(unit, distance)
        unit = step + self.LEAD

        @pl.when(unit < self.units)
        def _():
            self.send_own(unit)

    def run(self, first, last):
        loop(last, self.tick, first)

    def arrived(self, unit):
        self.taken.add(unit)
        landed(self.full.at[0:8, self.rows_of(unit, 0, UNIT)], self.cr.at[unit])

    def finish(self):
        full, units, z = self.full, self.units, self.z
        for unit in range(units):
            if unit not in self.taken:
                self.arrived(unit)
        plane = units * PLANE
        for k in range(4):
            @pl.when(z == k)
            def _(k=k):
                if k < 3:
                    landed(full.at[0:k + 1, 0:plane], self.snd.at[0])
                if k > 0:
                    landed(full.at[0:4 - k, 0:plane], self.snd.at[1])
        landed(full.at[0:4, 0:plane], self.snd.at[2])
        landed(full.at[0:7, 0:units * EDGE], self.snd.at[3])
        landed(full.at[0:8, 0:units * UNIT], self.snd.at[4])


S_EDGE = 16
S_MIDDLE = UNIT - 2 * S_EDGE
S_PLANE = S_EDGE + S_MIDDLE


class Scatter:
    def __init__(self, grads, out, units, bufs, sems):
        self.grads, self.out, self.units = grads, out, units
        self.own, self.obuf, self.cv, self.xv, self.yv, self.zv, self.fv = bufs
        self.load, self.store, self.cr, self.xr, self.yr, self.zr, self.fr, self.snd = sems
        self.r, self.t, self.c, self.y, self.z = place()

    def mine(self):
        return pl.ds(pl.multiple_of(self.t * S_EDGE, 16), S_PLANE)

    def edge(self, tm):
        return pl.ds(pl.multiple_of(tm * S_PLANE, 16), S_EDGE)

    def own_copy(self, unit):
        rows = pl.ds(pl.multiple_of(unit * UNIT, UNIT), UNIT)
        return pltpu.make_async_copy(self.grads.at[:, self.c, rows], self.own.at[lax.rem(unit, 2)], self.load.at[lax.rem(unit, 2)])

    def send_core(self, unit):
        rows = pl.ds(pl.multiple_of(unit * UNIT, UNIT), UNIT)
        remote(self.grads.at[:, 1 - self.c, rows], self.cv.at[unit], self.snd.at[0], self.cr.at[unit], self.r + 1 - 2 * self.c, self.t)

    def add(self, a, b, n):
        def one(i, carry):
            a[i] = (a[i].astype(jnp.float32) + b[i].astype(jnp.float32)).astype(jnp.bfloat16)
            return carry
        lax.fori_loop(0, n, one, 0)

    def sum_core(self, unit):
        cv = self.cv.at[unit]
        landed(cv, self.cr.at[unit])
        self.own_copy(unit).wait()
        self.add(cv, self.own.at[lax.rem(unit, 2)], 8)

        @pl.when(unit + 2 < self.units)
        def _():
            self.own_copy(unit + 2).start()
        remote(cv.at[:, self.edge(1 - self.t)], self.xv.at[unit], self.snd.at[1], self.xr.at[unit], self.r, 1 - self.t)

    def sum_x(self, unit):
        xv, cv = self.xv.at[unit], self.cv.at[unit]
        landed(xv, self.xr.at[unit])
        self.add(cv.at[:, self.edge(self.t)], xv, 8)
        for k in range(4):
            remote(cv.at[k * 2 + 1 - self.y, self.mine()], self.yv.at[unit, k], self.snd.at[2], self.yr.at[unit, k], self.r + 2 - 4 * self.y, self.t)

    def at_z(self, unit, z):
        return self.cv.at[unit, z * 2 + self.y, self.mine()]

    def send_z(self, unit, target, up):
        at = self.at_z(unit, target)
        remote(at, self.zv.at[unit, target + (1 if up else 0)], self.snd.at[3 if up else 4], self.zr.at[unit, target + (1 if up else 0)],
               self.r + (4 if up else -4), self.t)

    def take_z(self, unit, target, below):
        at = self.at_z(unit, target)
        entry = target + (1 if below else 0)
        zv = self.zv.at[unit, entry]
        landed(zv, self.zr.at[unit, entry])
        at[...] = (at[...].astype(jnp.float32) + zv[...].astype(jnp.float32)).astype(jnp.bfloat16)

    def sum_y(self, unit):
        for k in range(4):
            yv = self.yv.at[unit, k]
            landed(yv, self.yr.at[unit, k])
            at = self.at_z(unit, k)
            at[...] = (at[...].astype(jnp.float32) + yv[...].astype(jnp.float32)).astype(jnp.bfloat16)

        @pl.when(self.z == 0)
        def _():
            for target in (3, 2, 1):
                self.send_z(unit, target, True)

        @pl.when(self.z == 3)
        def _():
            for target in (0, 1, 2):
                self.send_z(unit, target, False)

    def hop(self, unit, number):
        for z in range(4):
            @pl.when(self.z == z)
            def _(z=z):
                if number == z:
                    for target in range(3, z - 1, -1):
                        self.take_z(unit, target, True)
                        if target > z:
                            self.send_z(unit, target, True)
                if number == 3 - z:
                    for target in range(0, z + 1):
                        self.take_z(unit, target, False)
                        if target < z:
                            self.send_z(unit, target, False)

    def exchange(self, unit):
        at = self.at_z(unit, self.z)
        remote(at, self.fv.at[unit], self.snd.at[5], self.fr.at[unit], self.r, 1 - self.t)

    def store_copy(self, unit):
        return pltpu.make_async_copy(self.obuf.at[lax.rem(unit, 2)], self.out.at[pl.ds(pl.multiple_of(unit * UNIT, UNIT), UNIT)], self.store.at[lax.rem(unit, 2)])

    def conclude(self, unit):
        fv = self.fv.at[unit]
        landed(fv, self.fr.at[unit])
        at = self.cv.at[unit, self.z * 2 + self.y]

        @pl.when(unit >= 2)
        def _():
            self.store_copy(unit - 2).wait()
        obuf = self.obuf.at[lax.rem(unit, 2)]
        middle = pl.ds(S_EDGE, S_MIDDLE)
        obuf[middle] = at[middle].astype(jnp.float32) + fv[pl.ds(pl.multiple_of(self.t * S_EDGE, 16), S_MIDDLE)].astype(jnp.float32)
        obuf[self.edge(self.t)] = at[self.edge(self.t)].astype(jnp.float32)
        obuf[self.edge(1 - self.t)] = fv[pl.ds(pl.multiple_of((1 - self.t) * S_MIDDLE, 16), S_EDGE)].astype(jnp.float32)
        self.store_copy(unit).start()

    LEAD = 3
    EVENTS = (("sum_core", 0, ()), ("sum_x", 1, ()), ("sum_y", 2, ()), ("hop", 3, (1,)), ("hop", 4, (2,)), ("hop", 5, (3,)), ("exchange", 5, ()), ("conclude", 6, ()))

    def ticks(self):
        return self.units + max(e[1] for e in self.EVENTS)

    def begin(self):
        for unit in range(min(2, self.units)):
            self.own_copy(unit).start()
        for unit in range(min(self.LEAD, self.units)):
            self.send_core(unit)

    def tick(self, step):
        for name, lag, args in self.EVENTS:
            unit = step - lag

            @pl.when((unit >= 0) & (unit < self.units))
            def _(name=name, unit=unit, args=args):
                getattr(self, name)(unit, *args)
        unit = step + self.LEAD

        @pl.when(unit < self.units)
        def _():
            self.send_core(unit)

    def finish(self):
        units, z, grads = self.units, self.z, self.grads
        for unit in range(max(0, units - 2), units):
            self.store_copy(unit).wait()
        landed(grads.at[:, 0, 0:units * UNIT], self.snd.at[0])
        landed(grads.at[:, 0, 0:units * S_EDGE], self.snd.at[1])
        landed(grads.at[0:4, 0, 0:units * S_PLANE], self.snd.at[2])
        for k in range(4):
            @pl.when(z == k)
            def _(k=k):
                if k < 3:
                    landed(grads.at[0:3 - k, 0, 0:units * S_PLANE], self.snd.at[3])
                if k > 0:
                    landed(grads.at[0:k, 0, 0:units * S_PLANE], self.snd.at[4])
        landed(grads.at[0, 0, 0:units * S_PLANE], self.snd.at[5])


def scatter_kernel(units, grads, small, out, small_out, own, obuf, cv, xv, yv, zv, fv, sown, sv, sx, load, store, cr, xr, yr, zr, fr, snd, sload, ssend, srecv, sxsem):
    r, t, c, y, z = place()
    R = lax.axis_size("rows")
    cs = pltpu.make_async_copy(small, sown, sload.at[0])
    cs.start()
    greet([(lax.rem(r + d, R), t) for d in range(1, R)] + [(r, 1 - t)])
    s = Scatter(grads, out, units, (own, obuf, cv, xv, yv, zv, fv), (load, store, cr, xr, yr, zr, fr, snd))
    s.begin()
    cs.wait()
    for d in range(1, R):
        to = lax.rem(r + d, R)
        remote(sown.at[to], sv.at[R - 1 - d], ssend, srecv, to, t)

    def step(i, carry):
        s.tick(i)
        return carry

    lax.fori_loop(0, s.ticks(), step, 0)
    landed(sown.at[0:R - 1], ssend)
    landed(sv.at[0:R - 1], srecv)
    total = sown[r]
    for d in range(R - 1):
        total = total + sv[d]
    sx[0] = total
    pltpu.make_async_remote_copy(src_ref=sx.at[0], dst_ref=sx.at[1], send_sem=sxsem.at[0], recv_sem=sxsem.at[1], device_id=(r, 1 - t), device_id_type=MESH).start()
    landed(sx.at[0], sxsem.at[0])
    landed(sx.at[1], sxsem.at[1])
    sx[0] = sx[0] + sx[1]
    done = pltpu.make_async_copy(sx.at[0], small_out, sload.at[1])
    done.start()
    s.finish()
    done.wait()


def scatter_call(grads, small, cid):
    R, rows, _ = grads.shape
    units = rows // UNIT
    bf = jnp.bfloat16
    return pl.pallas_call(
        functools.partial(scatter_kernel, units),
        out_shape=(jax.ShapeDtypeStruct((rows, 1024), jnp.float32), jax.ShapeDtypeStruct(small.shape[1:], small.dtype)),
        in_specs=[pl.BlockSpec(memory_space=ANY)] * 2,
        out_specs=(pl.BlockSpec(memory_space=ANY), pl.BlockSpec(memory_space=ANY)),
        scratch_shapes=[pltpu.VMEM((2, 8, UNIT, 1024), bf), pltpu.VMEM((2, UNIT, 1024), jnp.float32),
                        pltpu.VMEM((units, 8, UNIT, 1024), bf), pltpu.VMEM((units, 8, S_EDGE, 1024), bf), pltpu.VMEM((units, 4, S_PLANE, 1024), bf),
                        pltpu.VMEM((units, 5, S_PLANE, 1024), bf), pltpu.VMEM((units, S_PLANE, 1024), bf),
                        pltpu.VMEM(small.shape, small.dtype), pltpu.VMEM((R - 1,) + small.shape[1:], small.dtype), pltpu.VMEM((2,) + small.shape[1:], small.dtype),
                        pltpu.SemaphoreType.DMA((2,)), pltpu.SemaphoreType.DMA((2,)), pltpu.SemaphoreType.DMA((units,)), pltpu.SemaphoreType.DMA((units,)),
                        pltpu.SemaphoreType.DMA((units, 4)), pltpu.SemaphoreType.DMA((units, 5)), pltpu.SemaphoreType.DMA((units,)), pltpu.SemaphoreType.DMA((6,)),
                        pltpu.SemaphoreType.DMA((2,)), pltpu.SemaphoreType.DMA, pltpu.SemaphoreType.DMA, pltpu.SemaphoreType.DMA((2,))],
        compiler_params=pltpu.CompilerParams(collective_id=cid, has_side_effects=True, vmem_limit_bytes=67043328),
        name="scatter_grads",
    )(grads.reshape(R // 2, 2, rows, 1024), small)


HALO = 384
FI1, FO1, QKV, ATT, GLU, CONV, FI2, FO2, UNITS = 0, 4, 8, 11, 12, 14, 15, 19, 23
GAIN, SHIFT, BIAS, TAPS, REL = 0, 6, 20, 28, 33
F32, BF16 = jnp.float32, jnp.bfloat16
TILE = 1024
NN = (((1,), (0,)), ((), ()))
NT = (((1,), (1,)), ((), ()))
TN = (((0,), (0,)), ((), ()))
VMEM_LIMIT = 67043328


def dot(a, b, dims=NN):
    return lax.dot_general(a, b, dims, preferred_element_type=F32)


def by_rows(count, size, fn):
    loop(count // size, lambda i: fn(pl.ds(pl.multiple_of(i * size, size), size)))


def by_cols(count, fn):
    loop(count // TILE, lambda i: fn(pl.ds(pl.multiple_of(i * TILE, TILE), TILE)))


def normalized(v):
    centred = v - jnp.mean(v, axis=-1, keepdims=True)
    rs = lax.rsqrt(jnp.mean(centred * centred, axis=-1, keepdims=True) + EPS)
    return centred * rs, rs


def norm_back(w, gain, vhat, rs):
    wg = w * gain
    return rs * (wg - jnp.mean(wg, axis=-1, keepdims=True) - vhat * jnp.mean(wg * vhat, axis=-1, keepdims=True))


def eight(v):
    return jnp.sum(v.reshape(v.shape[0] // 8, 8, v.shape[1]), axis=0)


def sigmoid(v):
    return 1.0 / (1.0 + jnp.exp(-v))


class Weights:
    def __init__(self, full, buf, sems, blocks):
        self.full, self.buf, self.sems, self.blocks = full, buf, sems, blocks
        self.R = full.shape[0]
        self.n = 1024 // self.R

    def copies(self, k):
        unit, kind, index = self.blocks[k]
        n, R = self.n, self.R
        if kind == "in":
            return [(self.full.at[s, (unit + index) * n:(unit + index + 1) * n], self.buf.at[k, s * n:(s + 1) * n]) for s in range(R)]
        return [(self.full.at[index * (R // 4) + s, unit * n:(unit + 4) * n], self.buf.at[k, s * 4 * n:(s + 1) * 4 * n]) for s in range(R // 4)]

    def start(self, *ks):
        for k in ks or range(len(self.blocks)):
            for src, dst in self.copies(k):
                pltpu.make_async_copy(src, dst, self.sems.at[k]).start()

    def wait(self, *ks):
        for k in ks:
            pltpu.make_async_copy(self.buf.at[k], self.buf.at[k], self.sems.at[k]).wait()


class Grads:
    def __init__(self, out, buf, sems):
        self.out, self.buf, self.sems, self.count = out, buf, sems, 0
        self.R = out.shape[0]
        self.n = 1024 // self.R

    def put(self, unit, kind, index, left, right):
        slot = self.count % 2
        buf, n, R = self.buf.at[slot], self.n, self.R
        if self.count >= 2:
            self.wait(slot)

        def cols(c):
            buf[:, c] = dot(left, right(c), TN).astype(BF16)
        by_cols(1024, cols)
        if kind == "in":
            pairs = [(buf.at[s * n:(s + 1) * n], self.out.at[s, (unit + index) * n:(unit + index + 1) * n]) for s in range(R)]
        else:
            pairs = [(buf.at[s * 4 * n:(s + 1) * 4 * n], self.out.at[index * (R // 4) + s, unit * n:(unit + 4) * n]) for s in range(R // 4)]
        for src, dst in pairs:
            pltpu.make_async_copy(src, dst, self.sems.at[slot]).start()
        self.count += 1

    def wait(self, slot):
        pltpu.make_async_copy(self.buf.at[slot], self.buf.at[slot], self.sems.at[slot]).wait()

    def finish(self):
        for slot in range(min(2, self.count)):
            self.wait(slot)


def flipped(x, size):
    m = size
    return x + m - 2 * m * lax.rem(x // m, 2)


def cube_peers():
    r, t = lax.axis_index("rows"), lax.axis_index("tm")
    peers, m = [], 1
    while m < lax.axis_size("rows"):
        peers.append((flipped(r, m), t))
        m *= 2
    m = 1
    while m < lax.axis_size("tm"):
        peers.append((r, flipped(t, m)))
        m *= 2
    return peers


def add_all(send, recv, ssem, rsem):
    for i, (rows, tm) in enumerate(cube_peers()):
        remote(send.at[i], recv.at[i], ssem.at[i], rsem.at[i], rows, tm)
        landed(send.at[i], ssem.at[i])
        landed(recv.at[i], rsem.at[i])
        send[i + 1] = send[i] + recv[i]
    return len(cube_peers())


def edge_peers():
    r, t, T = lax.axis_index("rows"), lax.axis_index("tm"), lax.axis_size("tm")
    return [(r, lax.rem(t + 1, T)), (r, lax.rem(t + T - 1, T))]


def swap_edges(pad, count, sems):
    r, t, T = lax.axis_index("rows"), lax.axis_index("tm"), lax.axis_size("tm")

    @pl.when(t < T - 1)
    def _():
        remote(pad.at[count:count + 8], pad.at[0:8], sems.at[0], sems.at[1], r, t + 1)

    @pl.when(t > 0)
    def _():
        remote(pad.at[8:16], pad.at[count + 8:count + 16], sems.at[2], sems.at[3], r, t - 1)

    @pl.when(t < T - 1)
    def _():
        landed(pad.at[0:8], sems.at[0])
        landed(pad.at[0:8], sems.at[3])

    @pl.when(t > 0)
    def _():
        landed(pad.at[0:8], sems.at[2])
        landed(pad.at[0:8], sems.at[1])


def whole():
    return pl.BlockSpec(memory_space=pltpu.VMEM)


def anywhere():
    return pl.BlockSpec(memory_space=ANY)


def shape(*dims, dtype=F32):
    return jax.ShapeDtypeStruct(dims, dtype)


BLOCKS_A = tuple([(FI1, "in", j) for j in range(4)] + [(FO1, "out", j) for j in range(4)] + [(QKV, "in", j) for j in range(3)])


def norm_tokens(tokens, params, a):
    def norm(rows):
        vhat, _ = normalized(tokens[rows].astype(F32))
        a[rows] = (vhat * params[GAIN:GAIN + 1] + params[SHIFT:SHIFT + 1]).astype(BF16)
    by_rows(tokens.shape[0], 256, norm)


def norm_resid(x1, params, a):
    def norm(rows):
        vhat, _ = normalized(x1[rows])
        a[rows] = (vhat * params[GAIN + 1:GAIN + 2] + params[SHIFT + 1:SHIFT + 2]).astype(BF16)
    by_rows(x1.shape[0], 256, norm)


class Front:
    def __init__(self, w, params, tokens, x1, z1, a, h, zbuf, zsem):
        self.w, self.params, self.tokens, self.x1, self.z1, self.a, self.h, self.zbuf, self.zsem = w, params, tokens, x1, z1, a, h, zbuf, zsem

    def stored(self, slot):
        pltpu.make_async_copy(self.zbuf.at[slot], self.zbuf.at[slot], self.zsem.at[slot]).wait()

    def hidden(self, j):
        slot = j % 2
        self.w.wait(j)
        if j >= 2:
            self.stored(slot)
        z = dot(self.a[...], self.w.buf[j]) + self.params[BIAS + j:BIAS + j + 1]
        self.zbuf[slot] = z
        self.h[j] = (z * sigmoid(z)).astype(BF16)
        pltpu.make_async_copy(self.zbuf.at[slot], self.z1.at[:, j * 1024:(j + 1) * 1024], self.zsem.at[slot]).start()

    def project(self, j):
        self.w.wait(4 + j)
        part = dot(self.h[j], self.w.buf[4 + j])
        if j > 0:
            part = self.x1[...] + part
        if j == 3:
            part = self.tokens[...].astype(F32) + 0.5 * (part + self.params[SHIFT + 6:SHIFT + 7])
        self.x1[...] = part

    def mix(self, block, source, shift, out, rows):
        value = dot(source[...], self.w.buf[8 + block])
        if shift is not None:
            value = value + self.params[shift:shift + 1]
        out[rows] = value.astype(BF16)


def front_kernel(blocks, *refs):
    small, *refs = refs
    ws, refs = refs[:8], refs[8:]
    (tokens, full, params, x1, z1, q, k, v, beside, own, slab, slabs, wbuf, a, h, zbuf,
     load, keep, ssend, srecv, wsem, zsem, esem, *sems) = refs
    r, t, c, y, z = place()
    units, R, count = len(blocks), lax.axis_size("rows"), tokens.shape[0]
    copies = []
    for unit, (w, row, col) in enumerate(blocks):
        cp = pltpu.make_async_copy(ws[w].at[row:row + UNIT, col:col + 1024], own.at[unit * UNIT:(unit + 1) * UNIT], load.at[unit])
        cp.start()
        copies.append(cp)
    cs = pltpu.make_async_copy(small, slab, keep)
    cs.start()
    greet([(lax.rem(r + d, R), t) for d in range(1, R)] + [(r, 1 - t)])
    cs.wait()
    for d in range(1, R):
        remote(slab, slabs.at[r], ssend, srecv, lax.rem(r + d, R), t)
    stored = []
    for unit, cp in enumerate(copies):
        cp.wait()
        put = pltpu.make_async_copy(own.at[unit * UNIT:(unit + 1) * UNIT], full.at[r, unit * UNIT:(unit + 1) * UNIT], load.at[unit])
        put.start()
        stored.append(put)
    for put in stored:
        put.wait()
    g = Gather(full, 0, units, sems)
    g.begin()
    landed(slabs.at[0:R - 1], ssend)
    landed(slabs.at[0:R - 1], srecv)
    slabs[r] = slab[...]
    for pair in range(R // 2):
        params[:, pair * 128:(pair + 1) * 128] = (slabs[2 * pair].astype(F32) + slabs[2 * pair + 1].astype(F32))[0:40]
    for s in range(R):
        rows = slabs[s].astype(F32)
        for b in range(2):
            for part in range(2):
                at = 40 + 2 * b + part
                params[BIAS + 4 * b + s // 4:BIAS + 4 * b + s // 4 + 1, (s % 4) * 256 + part * 128:(s % 4) * 256 + (part + 1) * 128] = rows[at:at + 1]
    w = Weights(full, wbuf, wsem, BLOCKS_A)
    f = Front(w, params, tokens, x1, z1, a, h, zbuf, zsem)
    norm_tokens(tokens, params, a)
    mine, other = pl.ds(pl.multiple_of(t * HALO, 128), count), pl.ds(pl.multiple_of((1 - t) * count, 128), HALO)

    def exchange():
        norm_resid(x1, params, a)
        first = pl.multiple_of((1 - t) * (count - HALO), 128)
        remote(a.at[pl.ds(first, HALO)], beside, esem.at[0], esem.at[1], r, 1 - t)

    def receive():
        landed(beside, esem.at[0])
        landed(beside, esem.at[1])
        f.mix(1, beside, None, k, other)

    work = {5: lambda: f.hidden(0), 6: lambda: f.hidden(1), 7: lambda: f.hidden(2), 8: lambda: f.hidden(3),
            12: lambda: (f.project(0), f.project(1)), 13: lambda: (f.project(2), f.project(3), exchange()),
            14: lambda: (w.wait(8, 9), f.mix(0, a, SHIFT + 7, q, slice(None)), f.mix(1, a, None, k, mine)),
            15: lambda: (w.wait(10), f.mix(2, a, SHIFT + 8, v, mine)), 16: receive, 17: lambda: f.mix(2, beside, SHIFT + 8, v, other)}
    for step in range(18):
        g.tick(step)
        unit = step - g.LAG
        if 0 <= unit < 11:
            g.arrived(unit)
            if unit == 7:
                w.start(4, 5, 6, 7)
            elif unit < 4 or unit > 7:
                w.start(unit)
        if step in work:
            work[step]()
    g.run(18, units + g.LAG)
    g.finish()
    for slot in range(2):
        f.stored(slot)


def front(small, weights, tokens, cid):
    count, R, blocks = tokens.shape[0], lax.axis_size("rows"), []
    near = count + HALO
    for i, weight in enumerate(weights):
        n, cols = weight.shape
        blocks += [(i, row, col) for col in range(0, cols, 1024) for row in range(0, n, UNIT)]
    units, sem = len(blocks), pltpu.SemaphoreType.DMA
    return pl.pallas_call(
        functools.partial(front_kernel, tuple(blocks)),
        out_shape=[shape(R, units * UNIT, 1024, dtype=BF16), shape(40, 1024), shape(count, 1024), shape(count, 4096), shape(count, 1024, dtype=BF16),
                   shape(near, 1024, dtype=BF16), shape(near, 1024, dtype=BF16), shape(HALO, 1024, dtype=BF16)],
        in_specs=[anywhere()] * 9 + [whole()], out_specs=[anywhere(), whole(), whole(), anywhere()] + [whole()] * 4,
        scratch_shapes=[pltpu.VMEM((units * UNIT, 1024), BF16), pltpu.VMEM(small.shape, BF16), pltpu.VMEM((R,) + small.shape, BF16),
                        pltpu.VMEM((11, 1024, 1024), BF16), pltpu.VMEM((count, 1024), BF16), pltpu.VMEM((4, count, 1024), BF16), pltpu.VMEM((2, count, 1024), F32),
                        sem((units,)), sem, sem, sem, sem((11,)), sem((2,)), sem((2,))] + Gather.scratch(units),
        compiler_params=pltpu.CompilerParams(vmem_limit_bytes=VMEM_LIMIT, collective_id=cid, has_side_effects=True),
        name="front",
    )(small, *weights, tokens)


def plain_front_kernel(tokens, params, full, x1, z1, q, k, v, wbuf, a, h, zbuf, wsem, zsem):
    w = Weights(full, wbuf, wsem, BLOCKS_A)
    w.start()
    f = Front(w, params, tokens, x1, z1, a, h, zbuf, zsem)
    norm_tokens(tokens, params, a)
    for j in range(4):
        f.hidden(j)
    for j in range(4):
        f.project(j)
    norm_resid(x1, params, a)
    w.wait(8, 9, 10)
    f.mix(0, a, SHIFT + 7, q, slice(None))
    f.mix(1, a, None, k, slice(None))
    f.mix(2, a, SHIFT + 8, v, slice(None))
    for slot in range(2):
        f.stored(slot)


def plain_front(tokens, params, full):
    count = tokens.shape[0]
    return pl.pallas_call(
        plain_front_kernel,
        out_shape=[shape(count, 1024), shape(count, 4096)] + [shape(count, 1024, dtype=BF16)] * 3,
        in_specs=[whole(), whole(), anywhere()], out_specs=[whole(), anywhere(), whole(), whole(), whole()],
        scratch_shapes=[pltpu.VMEM((11, 1024, 1024), BF16), pltpu.VMEM((count, 1024), BF16), pltpu.VMEM((4, count, 1024), BF16), pltpu.VMEM((2, count, 1024), F32),
                        pltpu.SemaphoreType.DMA((11,)), pltpu.SemaphoreType.DMA((2,))],
        compiler_params=pltpu.CompilerParams(vmem_limit_bytes=VMEM_LIMIT),
        name="front",
    )(tokens, params, full)


QB = 128


def strip_of(window, length):
    return pltpu.roll(jnp.broadcast_to(window, (QB, length)), 0, 1, stride=1, stride_axis=0)


def score_block(q, k, strip, base, b, near, segq, segk, scale):
    start = pl.multiple_of(base - b * QB, 128)
    s = dot(q, k, NT) * scale + strip[:, pl.ds(start, near)]
    return jnp.where(segq == segk, s, NEG), start


def attend_kernel(scale, off, q, k, v, window, segq, segk, o, lse, strip):
    near = k.shape[0]
    strip[...] = strip_of(window[0], window.shape[-1])
    base = near + QB - off[0]

    def block(b):
        rows = pl.ds(pl.multiple_of(b * QB, QB), QB)
        s, _ = score_block(q[rows], k[...], strip, base, b, near, segq[rows], segk[...], scale)
        top = jnp.max(s, axis=-1, keepdims=True)
        p = jnp.exp(s - top)
        total = jnp.sum(p, axis=-1, keepdims=True)
        o[rows] = dot(p.astype(BF16), v[...]) / total
        lse[0, rows] = jnp.broadcast_to(top + jnp.log(total), (QB, 128))
    loop(q.shape[0] // QB, block)


def head_block(n):
    return pl.BlockSpec((n, 128), lambda h, off: (0, h))


def attend(q, k, v, windows, segq, segk, off):
    count, near, length = q.shape[0], k.shape[0], windows.shape[-1]
    return pl.pallas_call(
        functools.partial(attend_kernel, 1.0 / math.sqrt(128)),
        out_shape=[shape(count, 1024), shape(HEADS, count, 128)],
        grid_spec=pltpu.PrefetchScalarGridSpec(
            num_scalar_prefetch=1, grid=(HEADS,),
            in_specs=[head_block(count), head_block(near), head_block(near), pl.BlockSpec((1, 1, length), lambda h, off: (h, 0, 0)),
                      pl.BlockSpec((count, 1), lambda h, off: (0, 0)), pl.BlockSpec((1, near), lambda h, off: (0, 0))],
            out_specs=[head_block(count), pl.BlockSpec((1, count, 128), lambda h, off: (h, 0, 0))],
            scratch_shapes=[pltpu.VMEM((QB, length), F32)]),
        compiler_params=pltpu.CompilerParams(vmem_limit_bytes=VMEM_LIMIT),
        name="attend",
    )(off, q, k, v, windows, segq, segk)


def attend_back_kernel(scale, off, q, k, v, window, segq, segk, o, lse, do, dq, dk, dv, dtable, strip, ds, pb, acc):
    near = k.shape[0]
    length = window.shape[-1]
    strip[...] = strip_of(window[0], length)
    acc[...] = jnp.zeros_like(acc)
    base = near + QB - off[0]

    def block(b):
        rows = pl.ds(pl.multiple_of(b * QB, QB), QB)
        s, start = score_block(q[rows], k[...], strip, base, b, near, segq[rows], segk[...], scale)
        p = jnp.exp(s - lse[0, rows, 0:1])
        delta = jnp.sum(do[rows].astype(F32) * o[rows], axis=-1, keepdims=True)
        d = (p * (dot(do[rows], v[...], NT) - delta)).astype(BF16)
        pb[rows] = p.astype(BF16)
        ds[rows] = d
        dq[rows] = (dot(d, k[...]) * scale).astype(BF16)
        acc[:, pl.ds(start, near)] += d.astype(F32)
    loop(q.shape[0] // QB, block)
    dims = (((0,), (0,)), ((), ()))
    dk[...] = (dot(ds[...], q[...], dims) * scale).astype(BF16)
    dv[...] = dot(pb[...], do[...], dims).astype(BF16)
    rows, size = acc[...], QB
    while size > 1:
        size //= 2
        rows = rows[:size] + pltpu.roll(rows[size:], length - size, 1)
    dtable[0] = rows


def attend_back(q, k, v, windows, segq, segk, off, o, lse, do):
    count, near, length = q.shape[0], k.shape[0], windows.shape[-1]
    return pl.pallas_call(
        functools.partial(attend_back_kernel, 1.0 / math.sqrt(128)),
        out_shape=[shape(count, 1024, dtype=BF16), shape(near, 1024, dtype=BF16), shape(near, 1024, dtype=BF16), shape(HEADS, 1, length)],
        grid_spec=pltpu.PrefetchScalarGridSpec(
            num_scalar_prefetch=1, grid=(HEADS,),
            in_specs=[head_block(count), head_block(near), head_block(near), pl.BlockSpec((1, 1, length), lambda h, off: (h, 0, 0)),
                      pl.BlockSpec((count, 1), lambda h, off: (0, 0)), pl.BlockSpec((1, near), lambda h, off: (0, 0)),
                      head_block(count), pl.BlockSpec((1, count, 128), lambda h, off: (h, 0, 0)), head_block(count)],
            out_specs=[head_block(count), head_block(near), head_block(near), pl.BlockSpec((1, 1, length), lambda h, off: (h, 0, 0))],
            scratch_shapes=[pltpu.VMEM((QB, length), F32), pltpu.VMEM((count, near), BF16), pltpu.VMEM((count, near), BF16), pltpu.VMEM((QB, length), F32)]),
        compiler_params=pltpu.CompilerParams(vmem_limit_bytes=VMEM_LIMIT),
        name="attend_back",
    )(off, q, k, v, windows, segq, segk, o, lse, do)


ROWS = 128


BLOCKS_C = ((ATT, "in", 0), (GLU, "in", 0), (GLU, "in", 1))


def convolve_kernel(x1, o, params, seg, full, x2, c1, c2, u, y, sums, wbuf, a, half, send, recv, wsem, esem, ssem, rsem):
    w = Weights(full, wbuf, wsem, BLOCKS_C)
    w.start()
    count = x1.shape[0]
    u[0:8] = jnp.zeros((8, 1024), F32)
    u[count + 8:count + 16] = jnp.zeros((8, 1024), F32)
    greet(cube_peers() + edge_peers())

    def cast(rows):
        a[rows] = o[rows].astype(BF16)
    by_rows(count, 256, cast)
    w.wait(0)

    def project(c):
        x2[:, c] = x1[:, c] + dot(a[...], wbuf[0, :, c]) + params[SHIFT + 9:SHIFT + 10, c]
    by_cols(1024, project)

    def norm(rows):
        vhat, _ = normalized(x2[rows])
        a[rows] = (vhat * params[GAIN + 2:GAIN + 3] + params[SHIFT + 2:SHIFT + 3]).astype(BF16)
    by_rows(count, 256, norm)
    w.wait(1, 2)

    def gate(c):
        value = dot(a[...], wbuf[1, :, c]) + params[SHIFT + 10:SHIFT + 11, c]
        other = dot(a[...], wbuf[2, :, c]) + params[SHIFT + 11:SHIFT + 12, c]
        c1[:, c] = value
        c2[:, c] = other
        u[8:count + 8, c] = (value * sigmoid(other)).astype(BF16).astype(F32)
    by_cols(1024, gate)
    swap_edges(u, count, esem)
    half[...] = jnp.zeros_like(half)

    def taps(i):
        first = pl.multiple_of(i * ROWS, ROWS)
        here = seg[pl.ds(first + 8, ROWS)]
        total = jnp.zeros((ROWS, 1024), F32)
        block = u[pl.ds(first, ROWS + 16)]
        segs = seg[pl.ds(first, ROWS + 16)]
        for tap in range(KSIZE):
            k = slice(6 + tap, 6 + tap + ROWS)
            total = total + params[TAPS + tap:TAPS + tap + 1] * jnp.where(segs[k] == here, block[k], 0.0)
        y[pl.ds(first, ROWS)] = total
        half[0:8] += eight(total)
        half[8:16] += eight(total * total)
    loop(count // ROWS, taps)
    fold(half, send)
    steps = add_all(send, recv, ssem, rsem)
    sums[...] = send[steps]


def fold(half, send):
    send[0, 0:1] = jnp.sum(half[0:8], axis=0, keepdims=True)
    send[0, 1:2] = jnp.sum(half[8:16], axis=0, keepdims=True)


def reduce_scratch(rows=2):
    steps = (lax.axis_size("rows").bit_length() - 1) + (lax.axis_size("tm").bit_length() - 1)
    return [pltpu.VMEM((steps + 1, rows, 1024), F32), pltpu.VMEM((steps, rows, 1024), F32)], [pltpu.SemaphoreType.DMA((steps,)), pltpu.SemaphoreType.DMA((steps,))]


def convolve(x1, o, params, seg, full, cid):
    count = x1.shape[0]
    bufs, sems = reduce_scratch()
    return pl.pallas_call(
        convolve_kernel,
        out_shape=[shape(count, 1024), shape(count, 1024), shape(count, 1024), shape(count + 16, 1024), shape(count, 1024), shape(2, 1024)],
        in_specs=[whole()] * 4 + [anywhere()], out_specs=[whole()] * 6,
        scratch_shapes=[pltpu.VMEM((3, 1024, 1024), BF16), pltpu.VMEM((count, 1024), BF16), pltpu.VMEM((16, 1024), F32)] + bufs + [pltpu.SemaphoreType.DMA((3,)), pltpu.SemaphoreType.DMA((4,))] + sems,
        compiler_params=pltpu.CompilerParams(vmem_limit_bytes=VMEM_LIMIT, collective_id=cid, has_side_effects=True),
        name="convolve",
    )(x1, o, params, seg, full)


def batch_stats(sums, frames):
    mean = sums[0:1] / frames
    square = sums[1:2] / frames
    return mean, lax.rsqrt(square - mean * mean + EPS)


BLOCKS_D = tuple([(CONV, "in", 0)] + [(FI2, "in", j) for j in range(4)] + [(FO2, "out", j) for j in range(4)])


def middle_kernel(frames, x2, y, sums, cot, params, full, out, g3, dn, totals, small, grads,
                  wbuf, a, e, d, dz, h, z, stage, half, send, recv, wsem, gsem, ssem, rsem):
    w = Weights(full, wbuf, wsem, BLOCKS_D)
    w.start()
    greet(cube_peers())
    g = Grads(grads, stage, gsem)
    count = x2.shape[0]
    mean, inverse = batch_stats(sums, frames)
    small[...] = jnp.zeros_like(small)
    half[...] = jnp.zeros_like(half)

    def active(rows):
        n = (y[rows] - mean) * inverse * params[GAIN + 5:GAIN + 6] + params[SHIFT + 5:SHIFT + 6]
        e[rows] = (n * sigmoid(n)).astype(BF16)
    by_rows(count, 256, active)
    w.wait(0)
    x3 = g3

    def project(c):
        x3[:, c] = x2[:, c] + dot(e[...], wbuf[0, :, c]) + params[SHIFT + 12:SHIFT + 13, c]
    by_cols(1024, project)

    def norm(rows):
        vhat, _ = normalized(x3[rows])
        a[rows] = (vhat * params[GAIN + 3:GAIN + 4] + params[SHIFT + 3:SHIFT + 4]).astype(BF16)
    by_rows(count, 256, norm)
    for j in range(4):
        w.wait(1 + j)

    def hidden(j):
        def cols(c):
            v = dot(a[...], wbuf[1 + j, :, c]) + params[pl.ds(BIAS + 4 + j, 1), c]
            z[j, :, c] = v
            h[j, :, c] = (v * sigmoid(v)).astype(BF16)
        by_cols(1024, cols)
    loop(4, hidden)
    w.wait(5, 6, 7, 8)

    def outward(c):
        acc = dot(h[0], wbuf[5, :, c])
        for j in range(1, 4):
            acc = acc + dot(h[j], wbuf[5 + j, :, c])
        out[:, c] = x3[:, c] + 0.5 * (acc + params[SHIFT + 13:SHIFT + 14, c])
    by_cols(1024, outward)

    def last(rows):
        vhat, rs = normalized(out[rows])
        gain = params[GAIN + 4:GAIN + 5]
        out[rows] = vhat * gain + params[SHIFT + 4:SHIFT + 5]
        ct = cot[rows]
        small[0:8] += eight(ct * vhat)
        small[8:16] += eight(ct)
        g4 = norm_back(ct, gain, vhat, rs)
        dn[rows] = g4
        half = (0.5 * g4).astype(BF16)
        d[rows] = half
        small[16:24] += eight(half.astype(F32))
    by_rows(count, 256, last)

    def back(j):
        def cols(c):
            v = z[j, :, c]
            s = sigmoid(v)
            dh = dot(d[...], wbuf[5 + j, c, :], NT) * (s * (1.0 + v * (1.0 - s)))
            dh = dh.astype(BF16)
            dz[j, :, c] = dh
            small[pl.ds(pl.multiple_of(24 + 8 * j, 8), 8), c] += eight(dh.astype(F32))
        by_cols(1024, cols)
    loop(4, back)
    for j in range(4):
        g.put(FO2, "out", j, h[j], lambda c: d[:, c])
    for j in range(4):
        g.put(FI2, "in", j, a[...], lambda c, j=j: dz[j, :, c])
    da = z.at[0]

    def inward(c):
        acc = dot(dz[0], wbuf[1, c, :], NT)
        for j in range(1, 4):
            acc = acc + dot(dz[j], wbuf[1 + j, c, :], NT)
        da[:, c] = acc
    by_cols(1024, inward)

    def resid(rows):
        vhat, rs = normalized(x3[rows])
        w3 = da[rows]
        small[56:64] += eight(w3 * vhat)
        small[64:72] += eight(w3)
        total = dn[rows] + norm_back(w3, params[GAIN + 3:GAIN + 4], vhat, rs)
        g3[rows] = total
        de = total.astype(BF16)
        d[rows] = de
        small[72:80] += eight(de.astype(F32))
    by_rows(count, 256, resid)
    g.put(CONV, "in", 0, e[...], lambda c: d[:, c])

    def dnorm(c):
        dn[:, c] = dot(d[...], wbuf[0, c, :], NT)
    by_cols(1024, dnorm)

    def finish(rows):
        yhat = (y[rows] - mean) * inverse
        n = yhat * params[GAIN + 5:GAIN + 6] + params[SHIFT + 5:SHIFT + 6]
        s = sigmoid(n)
        v = dn[rows] * (s * (1.0 + n * (1.0 - s)))
        dn[rows] = v
        half[0:8] += eight(v * yhat)
        half[8:16] += eight(v)
    by_rows(count, 256, finish)
    small[80:96] = half[...]
    fold(half, send)
    steps = add_all(send, recv, ssem, rsem)
    totals[...] = send[steps]
    g.finish()


def middle(x2, y, sums, cot, params, full, frames, cid):
    count = x2.shape[0]
    bufs, sems = reduce_scratch()
    return pl.pallas_call(
        functools.partial(middle_kernel, frames),
        out_shape=[shape(count, 1024), shape(count, 1024), shape(count, 1024), shape(2, 1024), shape(96, 1024), shape(*full.shape, dtype=BF16)],
        in_specs=[whole()] * 5 + [anywhere()], out_specs=[whole()] * 5 + [anywhere()],
        scratch_shapes=[pltpu.VMEM((9, 1024, 1024), BF16), pltpu.VMEM((count, 1024), BF16), pltpu.VMEM((count, 1024), BF16), pltpu.VMEM((count, 1024), BF16),
                        pltpu.VMEM((4, count, 1024), BF16), pltpu.VMEM((4, count, 1024), BF16), pltpu.VMEM((4, count, 1024), F32),
                        pltpu.VMEM((2, 1024, 1024), BF16), pltpu.VMEM((16, 1024), F32)] + bufs + [pltpu.SemaphoreType.DMA((9,)), pltpu.SemaphoreType.DMA((2,))] + sems,
        compiler_params=pltpu.CompilerParams(vmem_limit_bytes=VMEM_LIMIT, collective_id=cid, has_side_effects=True),
        name="middle",
    )(x2, y, sums, cot, params, full)


def convolve_back_kernel(frames, dn, y, sums, totals, c1, c2, u, x2, g3, o, params, seg, full, grads_in, g2, dob, small, grads,
                         wbuf, a, d, dc, pad, stage, wsem, gsem, esem):
    w = Weights(full, wbuf, wsem, BLOCKS_C)
    w.start()
    count = x2.shape[0]
    pad[0:8] = jnp.zeros((8, 1024), F32)
    pad[count + 8:count + 16] = jnp.zeros((8, 1024), F32)
    greet(edge_peers())
    g = Grads(grads, stage, gsem)
    mean, inverse = batch_stats(sums, frames)
    gain = params[GAIN + 5:GAIN + 6]
    product = totals[0:1] * gain / frames
    total = totals[1:2] * gain / frames
    small[...] = jnp.zeros_like(small)

    def dy(i):
        rows = pl.ds(pl.multiple_of(i * ROWS, ROWS), ROWS)
        yhat = (y[rows] - mean) * inverse
        v = inverse * (dn[rows] * gain - total - yhat * product)
        pad[pl.ds(pl.multiple_of(i * ROWS + 8, 8), ROWS)] = v.astype(BF16).astype(F32)
        vhat, _ = normalized(x2[rows])
        a[rows] = (vhat * params[GAIN + 2:GAIN + 3] + params[SHIFT + 2:SHIFT + 3]).astype(BF16)
    loop(count // ROWS, dy)
    swap_edges(pad, count, esem)

    def taps(i):
        first = pl.multiple_of(i * ROWS, ROWS)
        rows = pl.ds(first, ROWS)
        block, grad, segs = u[pl.ds(first, ROWS + 16)], pad[pl.ds(first, ROWS + 16)], seg[pl.ds(first, ROWS + 16)]
        here, own = segs[8:ROWS + 8], grad[8:ROWS + 8]
        du = jnp.zeros((ROWS, 1024), F32)
        for tap in range(KSIZE):
            k = slice(6 + tap, 6 + tap + ROWS)
            small[8 * tap:8 * tap + 8] += eight(own * jnp.where(segs[k] == here, block[k], 0.0))
            b = slice(10 - tap, 10 - tap + ROWS)
            du = du + params[TAPS + tap:TAPS + tap + 1] * jnp.where(segs[b] == here, grad[b], 0.0)
        s = sigmoid(c2[rows])
        left = (du * s).astype(BF16)
        right = (du * c1[rows] * s * (1.0 - s)).astype(BF16)
        dc[0, rows] = left
        dc[1, rows] = right
        small[40:48] += eight(left.astype(F32))
        small[48:56] += eight(right.astype(F32))
    loop(count // ROWS, taps)
    w.wait(0, 1, 2)
    da = pad.at[0:count]

    def inward(c):
        da[:, c] = dot(dc[0], wbuf[1, c, :], NT) + dot(dc[1], wbuf[2, c, :], NT)
    by_cols(1024, inward)

    def resid(rows):
        vhat, rs = normalized(x2[rows])
        v = da[rows]
        small[56:64] += eight(v * vhat)
        small[64:72] += eight(v)
        both = g3[rows] + norm_back(v, params[GAIN + 2:GAIN + 3], vhat, rs)
        g2[rows] = both
        dx = both.astype(BF16)
        d[rows] = dx
        small[72:80] += eight(dx.astype(F32))
    by_rows(count, 256, resid)

    def attended(c):
        dob[:, c] = dot(d[...], wbuf[0, c, :], NT).astype(BF16)
    by_cols(1024, attended)
    for j in range(2):
        g.put(GLU, "in", j, a[...], lambda c, j=j: dc[j, :, c])

    def cast(rows):
        a[rows] = o[rows].astype(BF16)
    by_rows(count, 256, cast)
    g.put(ATT, "in", 0, a[...], lambda c: d[:, c])
    g.finish()


def convolve_back(dn, y, sums, totals, c1, c2, u, x2, g3, o, params, seg, full, grads, frames, cid):
    count = x2.shape[0]
    return pl.pallas_call(
        functools.partial(convolve_back_kernel, frames),
        out_shape=[shape(count, 1024), shape(count, 1024, dtype=BF16), shape(80, 1024), shape(*full.shape, dtype=BF16)],
        in_specs=[whole()] * 12 + [anywhere()] * 2, out_specs=[whole()] * 3 + [anywhere()],
        scratch_shapes=[pltpu.VMEM((3, 1024, 1024), BF16), pltpu.VMEM((count, 1024), BF16), pltpu.VMEM((count, 1024), BF16), pltpu.VMEM((2, count, 1024), BF16),
                        pltpu.VMEM((count + 16, 1024), F32), pltpu.VMEM((2, 1024, 1024), BF16),
                        pltpu.SemaphoreType.DMA((3,)), pltpu.SemaphoreType.DMA((2,)), pltpu.SemaphoreType.DMA((4,))],
        input_output_aliases={13: 3},
        compiler_params=pltpu.CompilerParams(vmem_limit_bytes=VMEM_LIMIT, collective_id=cid, has_side_effects=True),
        name="convolve_back",
    )(dn, y, sums, totals, c1, c2, u, x2, g3, o, params, seg, full, grads)


BLOCKS_E = tuple([(QKV, "in", j) for j in range(3)] + [(FO1, "out", j) for j in range(4)] + [(FI1, "in", j) for j in range(4)])


def rear_kernel(halo, tokens, x1, z1, g2, dq, dk, dv, params, full, *refs):
    if halo:
        beside, grads_in, dtok, small, grads, wbuf, a, d, dz, zbuf, hbuf, stage, da, back, got, wsem, zsem, gsem, esem = refs
    else:
        grads_in, dtok, small, grads, wbuf, a, d, dz, zbuf, hbuf, stage, da, wsem, zsem, gsem = refs
    w = Weights(full, wbuf, wsem, BLOCKS_E)
    w.start()
    g = Grads(grads, stage, gsem)
    count = tokens.shape[0]
    for j in range(2):
        pltpu.make_async_copy(z1.at[:, j * 1024:(j + 1) * 1024], zbuf.at[j], zsem.at[j]).start()
    small[...] = jnp.zeros_like(small)
    own = 0
    if halo:
        r, t = lax.axis_index("rows"), lax.axis_index("tm")
        greet([(r, 1 - t)])
        own, other = pl.multiple_of(t * HALO, 128), pl.multiple_of((1 - t) * count, 128)
        w.wait(1, 2)

        def outside(c):
            back[:, c] = (dot(dk[pl.ds(other, HALO)], wbuf[1, c, :], NT) + dot(dv[pl.ds(other, HALO)], wbuf[2, c, :], NT)).astype(BF16)
        by_cols(1024, outside)
        remote(back, got, esem.at[0], esem.at[1], r, 1 - t)
        w.wait(0)
    else:
        w.wait(0, 1, 2)
    mine = pl.ds(own, count)

    def inside(c):
        da[:, c] = dot(dq[...], wbuf[0, c, :], NT) + dot(dk[mine], wbuf[1, c, :], NT) + dot(dv[mine], wbuf[2, c, :], NT)
    by_cols(1024, inside)

    def norm(rows):
        vhat, _ = normalized(x1[rows])
        a[rows] = (vhat * params[GAIN + 1:GAIN + 2] + params[SHIFT + 1:SHIFT + 2]).astype(BF16)
        small[0:8] += eight(dq[rows].astype(F32))
    by_rows(count, 256, norm)

    def values(rows):
        small[8:16] += eight(dv[rows].astype(F32))
    by_rows(dv.shape[0], 128, values)
    g.put(QKV, "in", 0, a[...], lambda c: dq[:, c])
    if halo:
        for j, grad in ((1, dk), (2, dv)):
            slot = g.count % 2
            buf, n, R = stage.at[slot], g.n, g.R
            if g.count >= 2:
                g.wait(slot)

            def cols(c, grad=grad, buf=buf):
                buf[:, c] = (dot(a[...], grad[mine, c], TN) + dot(beside[...], grad[pl.ds(other, HALO), c], TN)).astype(BF16)
            by_cols(1024, cols)
            for s in range(R):
                pltpu.make_async_copy(buf.at[s * n:(s + 1) * n], grads.at[s, (QKV + j) * n:(QKV + j + 1) * n], gsem.at[slot]).start()
            g.count += 1
        landed(back, esem.at[0])
        landed(got, esem.at[1])
        first = pl.multiple_of((1 - t) * (count - HALO), 128)

        def merge(i):
            rows = pl.ds(pl.multiple_of(first + i * 64, 64), 64)
            da[rows] += got[pl.ds(pl.multiple_of(i * 64, 64), 64)].astype(F32)
        loop(HALO // 64, merge)
    else:
        g.put(QKV, "in", 1, a[...], lambda c: dk[:, c])
        g.put(QKV, "in", 2, a[...], lambda c: dv[:, c])

    def resid(rows):
        vhat, rs = normalized(x1[rows])
        v = da[rows]
        small[16:24] += eight(v * vhat)
        small[24:32] += eight(v)
        both = g2[rows] + norm_back(v, params[GAIN + 1:GAIN + 2], vhat, rs)
        dtok[rows] = both
        half = (0.5 * both).astype(BF16)
        d[rows] = half
        small[32:40] += eight(half.astype(F32))
        vhat, _ = normalized(tokens[rows].astype(F32))
        a[rows] = (vhat * params[GAIN:GAIN + 1] + params[SHIFT:SHIFT + 1]).astype(BF16)
    by_rows(count, 256, resid)
    w.wait(3, 4, 5, 6)
    for j in range(4):
        slot = j % 2
        pltpu.make_async_copy(zbuf.at[slot], zbuf.at[slot], zsem.at[slot]).wait()

        def cols(c, j=j, slot=slot):
            v = zbuf[slot, :, c]
            s = sigmoid(v)
            hbuf[:, c] = (v * s).astype(BF16)
            dh = (dot(d[...], wbuf[3 + j, c, :], NT) * (s * (1.0 + v * (1.0 - s)))).astype(BF16)
            dz[j, :, c] = dh
            small[40 + 8 * j:48 + 8 * j, c] += eight(dh.astype(F32))
        by_cols(1024, cols)
        if j + 2 < 4:
            pltpu.make_async_copy(z1.at[:, (j + 2) * 1024:(j + 3) * 1024], zbuf.at[slot], zsem.at[slot]).start()
        g.put(FO1, "out", j, hbuf[...], lambda c: d[:, c])
    for j in range(4):
        g.put(FI1, "in", j, a[...], lambda c, j=j: dz[j, :, c])
    w.wait(7, 8, 9, 10)

    def inward(c):
        acc = dot(dz[0], wbuf[7, c, :], NT)
        for j in range(1, 4):
            acc = acc + dot(dz[j], wbuf[7 + j, c, :], NT)
        da[:, c] = acc
    by_cols(1024, inward)

    def last(rows):
        vhat, rs = normalized(tokens[rows].astype(F32))
        v = da[rows]
        small[72:80] += eight(v * vhat)
        small[80:88] += eight(v)
        dtok[rows] = dtok[rows] + norm_back(v, params[GAIN:GAIN + 1], vhat, rs)
    by_rows(count, 256, last)
    g.finish()


def rear(tokens, x1, z1, g2, dq, dk, dv, params, full, beside, grads, cid):
    count = tokens.shape[0]
    halo = beside is not None
    scratch = [pltpu.VMEM((11, 1024, 1024), BF16), pltpu.VMEM((count, 1024), BF16), pltpu.VMEM((count, 1024), BF16), pltpu.VMEM((4, count, 1024), BF16),
               pltpu.VMEM((2, count, 1024), F32), pltpu.VMEM((count, 1024), BF16), pltpu.VMEM((2, 1024, 1024), BF16), pltpu.VMEM((count, 1024), F32)]
    if halo:
        scratch += [pltpu.VMEM((HALO, 1024), BF16), pltpu.VMEM((HALO, 1024), BF16)]
    scratch += [pltpu.SemaphoreType.DMA((11,)), pltpu.SemaphoreType.DMA((2,)), pltpu.SemaphoreType.DMA((2,))]
    if halo:
        scratch.append(pltpu.SemaphoreType.DMA((2,)))
    specs = [whole(), whole(), anywhere()] + [whole()] * 5 + [anywhere()] + ([whole()] if halo else []) + [anywhere()]
    return pl.pallas_call(
        functools.partial(rear_kernel, halo),
        out_shape=[shape(count, 1024), shape(88, 1024), shape(*full.shape, dtype=BF16)],
        in_specs=specs, out_specs=[whole(), whole(), anywhere()], scratch_shapes=scratch,
        input_output_aliases={len(specs) - 1: 2},
        compiler_params=pltpu.CompilerParams(vmem_limit_bytes=VMEM_LIMIT, **({"collective_id": cid, "has_side_effects": True} if halo else {})),
        name="rear",
    )(tokens, x1, z1, g2, dq, dk, dv, params, full, *((beside,) if halo else ()), grads)


def pack_rows(gains, shifts, ffn_bias, conv_kernel, rel_table):
    n = rel_table.shape[0]
    rows = jnp.concatenate([gains, shifts, ffn_bias.reshape(2 * 4, n), conv_kernel, rel_table[None]], axis=0).reshape(-1)
    return jnp.pad(rows, (0, 8 * 384 - rows.shape[0])).reshape(8, 384)


def slab_rows(gains, shifts, ffn_bias, conv_kernel, rel_table):
    rows = jnp.concatenate([gains, shifts, jnp.zeros((8, 64), BF16), conv_kernel, rel_table[None], jnp.zeros((6, 64), BF16)], axis=0)
    zero = jnp.zeros_like(rows)
    odd = lax.rem(lax.axis_index("rows"), 2) == 1
    wide = jnp.concatenate([jnp.where(odd, zero, rows), jnp.where(odd, rows, zero)], axis=1)
    return jnp.concatenate([wide, ffn_bias.reshape(4, 128), jnp.zeros((4, 128), BF16)], axis=0)


def wide_rows(smalls):
    R = smalls.shape[0]
    n = 1024 // R
    rows = smalls.reshape(R, -1)[:, : 34 * n].reshape(R, 34, n).astype(F32)
    flat = rows.transpose(1, 0, 2).reshape(34, 1024)
    bias = rows[:, 20:28].reshape(R, 2, 4 * n).transpose(1, 0, 2).reshape(8, 1024)
    return jnp.concatenate([flat[:20], bias, flat[28:], jnp.zeros((6, 1024), F32)], axis=0)


def slot_rows(rows, R):
    n = 1024 // R
    flat = rows.reshape(34, R, n).transpose(1, 0, 2)
    bias = rows[20:28].reshape(2, R, 4, n).transpose(1, 0, 2, 3).reshape(R, 8, n)
    flat = jnp.concatenate([flat[:, :20], bias, flat[:, 28:]], axis=1).reshape(R, 34 * n)
    return jnp.pad(flat, ((0, 0), (0, 8 * 384 - 34 * n))).reshape(R, 8, 384)


def shard_rows(small, R):
    n = 1024 // R
    rows = small.reshape(-1)[: 34 * n].reshape(34, n)
    return (rows[:6], rows[6:20], rows[20:28].reshape(2, 4 * n), rows[28:33], rows[33])


def pack_weights(weights):
    blocks = []
    for w in weights:
        rows, cols = w.shape
        blocks.append(w.reshape(rows, cols // 1024, 1024).transpose(1, 0, 2).reshape(-1, 1024))
    return jnp.concatenate(blocks, axis=0)


def unpack_shard(shard, weights):
    out, row = [], 0
    for w in weights:
        n, cols = w.shape
        count = n * cols // 1024
        out.append(shard[row : row + count].reshape(cols // 1024, n, 1024).transpose(1, 0, 2).reshape(n, cols))
        row += count
    return tuple(out)


def body(tokens, cotangent, segment_ids, rel_bucket, ffn1_in, ffn1_out, qkv_weight, attn_out, glu_in, conv_out, ffn2_in, ffn2_out,
         gains, shifts, ffn_bias, conv_kernel, rel_table):
    packed_rows, count, width = tokens.shape
    R, T = lax.axis_size("rows"), lax.axis_size("tm")
    t = lax.axis_index("tm")
    links = R == 16 and T == 2 and count == 512
    frames = R * T * count * packed_rows
    weights = (ffn1_in, ffn1_out, qkv_weight, attn_out, glu_in, conv_out, ffn2_in, ffn2_out)
    tok = tokens.reshape(count, width)
    if links:
        full, params, x1, z1, q, k, v, beside = front(slab_rows(gains, shifts, ffn_bias, conv_kernel, rel_table), weights, tok, 0)
    else:
        full = lax.all_gather(pack_weights(weights), "rows", axis=0)
        params = wide_rows(lax.all_gather(pack_rows(gains, shifts, ffn_bias, conv_kernel, rel_table), "rows", axis=0))

    seg_all = lax.all_gather(segment_ids, "tm", axis=1, tiled=True)[0]
    seg_far = jnp.pad(seg_all, (HALO, HALO), constant_values=-1)
    segx = lax.dynamic_slice_in_dim(seg_far, HALO + t * count - 8, count + 16)[:, None]
    segq = segment_ids.reshape(count, 1)
    if links:
        near, off = count + HALO, t * HALO
        segk = lax.dynamic_slice_in_dim(seg_all, t * (count - HALO), near)[None]
    else:
        near, off = T * count, t * count
        segk = seg_all[None]
    length = 2 * near + QB
    places = np.clip(np.arange(length) - (near + QB), -MAXD, MAXD) + MAXD
    before, after = int(np.argmax(places > 0)), int(np.argmax(places >= 2 * MAXD))
    buckets = jnp.concatenate([jnp.broadcast_to(rel_bucket[:1], (before,)), rel_bucket[1 : 2 * MAXD], jnp.broadcast_to(rel_bucket[2 * MAXD :], (length - after,))])
    hot = (buckets[None, :] == jnp.arange(NB, dtype=jnp.int32)[:, None]).astype(F32)
    windows = jnp.dot(params[REL].reshape(HEADS, NB), hot, precision=HIGH).reshape(HEADS, 1, length)
    off = off.astype(jnp.int32).reshape(1)

    if not links:
        x1, z1, q, k, v = plain_front(tok, params, full)
        beside = None
        k = lax.all_gather(k, "tm", axis=0, tiled=True)
        v = lax.all_gather(v, "tm", axis=0, tiled=True)
    o, lse = attend(q, k, v, windows, segq, segk, off)
    x2, c1, c2, u, y, sums = convolve(x1, o, params, segx, full, 3)
    output, g3, dn, totals, small_d, grads = middle(x2, y, sums, cotangent.reshape(count, width), params, full, frames, 4)
    g2, dob, small_c, grads = convolve_back(dn, y, sums, totals, c1, c2, u, x2, g3, o, params, segx, full, grads, frames, 5)
    dq, dk, dv, dtable = attend_back(q, k, v, windows, segq, segk, off, o, lse, dob)
    if not links:
        dk = lax.psum_scatter(dk, "tm", scatter_dimension=0, tiled=True)
        dv = lax.psum_scatter(dv, "tm", scatter_dimension=0, tiled=True)
    dtok, small_e, grads = rear(tok, x1, z1, g2, dq, dk, dv, params, full, beside, grads, 6)

    rel = lax.dot_general(dtable.reshape(HEADS, length), hot, (((1,), (1,)), ((), ())), precision=HIGH).reshape(1, 1024)
    d = jnp.sum(small_d.reshape(12, 8, 1024), axis=1)
    c = jnp.sum(small_c.reshape(10, 8, 1024), axis=1)
    e = jnp.sum(small_e.reshape(11, 8, 1024), axis=1)
    rows = jnp.concatenate([
        e[9:10], e[2:3], c[7:8], d[7:8], d[0:1], d[10:11],
        e[10:11], e[3:4], c[8:9], d[8:9], d[1:2], d[11:12], e[4:5], e[0:2], c[9:10], c[5:7], d[9:10], d[2:3],
        e[5:9], d[3:7], c[0:5], rel])
    if links:
        shard, small = scatter_call(grads, slot_rows(rows, R), 1)
    else:
        shard = lax.psum(lax.psum_scatter(grads, "rows", scatter_dimension=0, tiled=False), "tm").astype(F32)
        small = lax.psum(lax.psum_scatter(slot_rows(rows, R), "rows", scatter_dimension=0, tiled=False), "tm")
    return (output.reshape(tokens.shape), dtok.reshape(tokens.shape)) + unpack_shard(shard, weights) + shard_rows(small, R)


def solution(mesh):
    return jax.shard_map(
        body,
        mesh=mesh,
        in_specs=(
            P("rows", "tm", None),
            P("rows", "tm", None),
            P("rows", "tm"),
            P(),
            P("rows", None),
            P("rows", None),
            P("rows", None),
            P("rows", None),
            P("rows", None),
            P("rows", None),
            P("rows", None),
            P("rows", None),
            P(None, "rows"),
            P(None, "rows"),
            P(None, "rows"),
            P(None, "rows"),
            P("rows"),
        ),
        out_specs=(
            P("rows", "tm", None),
            P("rows", "tm", None),
            P("rows", None),
            P("rows", None),
            P("rows", None),
            P("rows", None),
            P("rows", None),
            P("rows", None),
            P("rows", None),
            P("rows", None),
            P(None, "rows"),
            P(None, "rows"),
            P(None, "rows"),
            P(None, "rows"),
            P("rows"),
        ),
        check_vma=False,
    )
```

```python
import functools
import math

import jax
import jax.numpy as jnp
import numpy as np
from jax import lax
from jax.experimental import pallas as pl
from jax.experimental.pallas import tpu as pltpu
from jax.sharding import PartitionSpec as P

HEADS = 8
KSIZE = 5
NB = 128
MAXD = 256


EPS = 1e-05
NEG = -1e30
HIGH = lax.Precision.HIGHEST


MESH = pl.DeviceIdType.MESH
ANY = pl.ANY


def place():
    r = lax.axis_index("rows")
    t = lax.axis_index("tm")
    return r, t, lax.rem(r, 2), lax.rem(r // 2, 2), r // 4


def remote(src, dst, send, recv, rows, tm):
    pltpu.make_async_remote_copy(
        src_ref=src, dst_ref=dst, send_sem=send, recv_sem=recv,
        device_id=(rows, tm), device_id_type=MESH,
    ).start()


def landed(ref, sem):
    pltpu.make_async_copy(ref, ref, sem).wait()


def greet(peers):
    barrier = pltpu.get_barrier_semaphore()
    for rows, tm in peers:
        pl.semaphore_signal(barrier, inc=1, device_id=(rows, tm), device_id_type=MESH)
    pl.semaphore_wait(barrier, len(peers))


def link_peers():
    r, t, c, y, z = place()
    return [(r + 1 - 2 * c, t), (r + 2 - 4 * y, t), (lax.rem(r + 4, 16), t), (lax.rem(r + 12, 16), t), (r, 1 - t)]


def loop(n, fn, first=0):
    def one(i, carry):
        fn(i)
        return carry
    lax.fori_loop(first, n, one, 0)


UNIT = 64
EDGE = 24
MIDDLE = UNIT - 2 * EDGE
PLANE = EDGE + MIDDLE


class Gather:
    LEAD = 3
    EVENTS = (("from_z", 1, 0), ("from_y", 0, 0), ("from_z", 2, 1), ("from_y", 1, 1), ("from_x", 0, 1), ("from_z", 3, 2),
              ("from_y", 2, 2), ("from_x", 1, 2), ("from_y", 3, 3), ("from_x", 2, 3), ("from_x", 3, 4))
    LAG = 4

    def __init__(self, full, first, units, sems):
        self.full, self.first, self.units = full, first, units
        self.zr, self.yr, self.xr, self.cr, self.snd = sems
        self.r, self.t, self.c, self.y, self.z = place()
        self.taken = set()

    @staticmethod
    def scratch(units):
        sem = pltpu.SemaphoreType.DMA
        return [sem((units, 4)), sem((units, 4)), sem((units, 8)), sem((units,)), sem((5,))]

    def slot(self, z, y):
        return z * 4 + y * 2 + self.c

    def rows_of(self, unit, start, size):
        return pl.ds(pl.multiple_of((unit + self.first) * UNIT + start, 8), size)

    def inplane(self, slot, unit):
        return self.full.at[slot, self.rows_of(unit, self.t * EDGE, PLANE)]

    def edge(self, slot, unit, tm):
        return self.full.at[slot, self.rows_of(unit, tm * PLANE, EDGE)]

    def to_core(self, ref, unit):
        remote(ref, ref, self.snd.at[4], self.cr.at[unit], self.r + 1 - 2 * self.c, self.t)

    def send_own(self, unit):
        r, t, z = self.r, self.t, self.z
        plane = self.inplane(r, unit)

        @pl.when(z < 3)
        def _():
            remote(plane, plane, self.snd.at[0], self.zr.at[unit, z], r + 4, t)

        @pl.when(z > 0)
        def _():
            remote(plane, plane, self.snd.at[1], self.zr.at[unit, z], r - 4, t)

        remote(plane, plane, self.snd.at[2], self.yr.at[unit, z], self.slot(z, 1 - self.y), t)
        self.to_core(self.full.at[r, self.rows_of(unit, 0, UNIT)], unit)

    def pass_on(self, unit, z, y):
        s = self.slot(z, y)
        part = self.edge(s, unit, self.t)
        remote(part, part, self.snd.at[3], self.xr.at[unit, z * 2 + y], self.r, 1 - self.t)
        self.to_core(self.inplane(s, unit), unit)

    def from_z(self, unit, distance):
        for sign in (-1, 1):
            z = self.z + sign * distance

            @pl.when((z >= 0) & (z <= 3))
            def _(z=z, sign=sign):
                plane = self.inplane(self.slot(z, self.y), unit)
                landed(plane, self.zr.at[unit, z])
                onward = self.z - sign

                @pl.when((onward >= 0) & (onward <= 3))
                def _():
                    remote(plane, plane, self.snd.at[0 if sign < 0 else 1], self.zr.at[unit, z], self.slot(onward, self.y), self.t)

                remote(plane, plane, self.snd.at[2], self.yr.at[unit, z], self.slot(self.z, 1 - self.y), self.t)
                self.pass_on(unit, z, self.y)

    def from_y(self, unit, distance):
        for sign in (-1, 1) if distance else (1,):
            z = self.z + sign * distance

            @pl.when((z >= 0) & (z <= 3))
            def _(z=z):
                landed(self.inplane(self.slot(z, 1 - self.y), unit), self.yr.at[unit, z])
                self.pass_on(unit, z, 1 - self.y)

    def from_x(self, unit, distance):
        for other in (False, True) if distance else (True,):
            y = 1 - self.y if other else self.y
            for sign in (-1, 1) if distance else (1,):
                z = self.z + sign * distance

                @pl.when((z >= 0) & (z <= 3))
                def _(z=z, y=y):
                    part = self.edge(self.slot(z, y), unit, 1 - self.t)
                    landed(part, self.xr.at[unit, z * 2 + y])
                    self.to_core(part, unit)

    def begin(self):
        for unit in range(min(self.LEAD, self.units)):
            self.send_own(unit)

    def part(self, step, quarter):
        bounds = (0, 3, 6, 9, len(self.EVENTS))
        for name, distance, lag in self.EVENTS[bounds[quarter]:bounds[quarter + 1]]:
            unit = step - lag

            @pl.when((unit >= 0) & (unit < self.units))
            def _(name=name, distance=distance, unit=unit):
                getattr(self, name)(unit, distance)
        if quarter == 3:
            unit = step + self.LEAD

            @pl.when(unit < self.units)
            def _():
                self.send_own(unit)

    def tick(self, step):
        for quarter in range(4):
            self.part(step, quarter)

    def run(self, first, last):
        loop(last, self.tick, first)

    def arrived(self, unit):
        self.taken.add(unit)
        landed(self.full.at[0:8, self.rows_of(unit, 0, UNIT)], self.cr.at[unit])

    def finish(self):
        full, units, z = self.full, self.units, self.z
        for unit in range(units):
            if unit not in self.taken:
                self.arrived(unit)
        plane = units * PLANE
        for k in range(4):
            @pl.when(z == k)
            def _(k=k):
                if k < 3:
                    landed(full.at[0:k + 1, 0:plane], self.snd.at[0])
                if k > 0:
                    landed(full.at[0:4 - k, 0:plane], self.snd.at[1])
        landed(full.at[0:4, 0:plane], self.snd.at[2])
        landed(full.at[0:7, 0:units * EDGE], self.snd.at[3])
        landed(full.at[0:8, 0:units * UNIT], self.snd.at[4])


S_EDGE = 16
S_MIDDLE = UNIT - 2 * S_EDGE
S_PLANE = S_EDGE + S_MIDDLE


class Scatter:
    def __init__(self, grads, out, units, bufs, sems):
        self.grads, self.out, self.units = grads, out, units
        self.own, self.obuf, self.cv, self.xv, self.yv, self.zv, self.fv = bufs
        self.load, self.store, self.cr, self.xr, self.yr, self.zr, self.fr, self.snd = sems
        self.r, self.t, self.c, self.y, self.z = place()

    def mine(self):
        return pl.ds(pl.multiple_of(self.t * S_EDGE, 16), S_PLANE)

    def edge(self, tm):
        return pl.ds(pl.multiple_of(tm * S_PLANE, 16), S_EDGE)

    def own_copy(self, unit):
        rows = pl.ds(pl.multiple_of(unit * UNIT, UNIT), UNIT)
        return pltpu.make_async_copy(self.grads.at[:, self.c, rows], self.own.at[lax.rem(unit, 2)], self.load.at[lax.rem(unit, 2)])

    def send_core(self, unit):
        rows = pl.ds(pl.multiple_of(unit * UNIT, UNIT), UNIT)
        remote(self.grads.at[:, 1 - self.c, rows], self.cv.at[unit], self.snd.at[0], self.cr.at[unit], self.r + 1 - 2 * self.c, self.t)

    def add(self, a, b, n):
        def one(i, carry):
            a[i] = (a[i].astype(jnp.float32) + b[i].astype(jnp.float32)).astype(jnp.bfloat16)
            return carry
        lax.fori_loop(0, n, one, 0)

    def sum_core(self, unit):
        cv = self.cv.at[unit]
        landed(cv, self.cr.at[unit])
        self.own_copy(unit).wait()
        self.add(cv, self.own.at[lax.rem(unit, 2)], 8)

        @pl.when(unit + 2 < self.units)
        def _():
            self.own_copy(unit + 2).start()
        remote(cv.at[:, self.edge(1 - self.t)], self.xv.at[unit], self.snd.at[1], self.xr.at[unit], self.r, 1 - self.t)

    def sum_x(self, unit):
        xv, cv = self.xv.at[unit], self.cv.at[unit]
        landed(xv, self.xr.at[unit])
        self.add(cv.at[:, self.edge(self.t)], xv, 8)
        for k in range(4):
            remote(cv.at[k * 2 + 1 - self.y, self.mine()], self.yv.at[unit, k], self.snd.at[2], self.yr.at[unit, k], self.r + 2 - 4 * self.y, self.t)

    def at_z(self, unit, z):
        return self.cv.at[unit, z * 2 + self.y, self.mine()]

    def send_z(self, unit, target, up):
        at = self.at_z(unit, target)
        remote(at, self.zv.at[unit, target + (1 if up else 0)], self.snd.at[3 if up else 4], self.zr.at[unit, target + (1 if up else 0)],
               self.r + (4 if up else -4), self.t)

    def take_z(self, unit, target, below):
        at = self.at_z(unit, target)
        entry = target + (1 if below else 0)
        zv = self.zv.at[unit, entry]
        landed(zv, self.zr.at[unit, entry])
        at[...] = (at[...].astype(jnp.float32) + zv[...].astype(jnp.float32)).astype(jnp.bfloat16)

    def sum_y(self, unit):
        for k in range(4):
            yv = self.yv.at[unit, k]
            landed(yv, self.yr.at[unit, k])
            at = self.at_z(unit, k)
            at[...] = (at[...].astype(jnp.float32) + yv[...].astype(jnp.float32)).astype(jnp.bfloat16)

        @pl.when(self.z == 0)
        def _():
            for target in (3, 2, 1):
                self.send_z(unit, target, True)

        @pl.when(self.z == 3)
        def _():
            for target in (0, 1, 2):
                self.send_z(unit, target, False)

    def hop(self, unit, number):
        for z in range(4):
            @pl.when(self.z == z)
            def _(z=z):
                if number == z:
                    for target in range(3, z - 1, -1):
                        self.take_z(unit, target, True)
                        if target > z:
                            self.send_z(unit, target, True)
                if number == 3 - z:
                    for target in range(0, z + 1):
                        self.take_z(unit, target, False)
                        if target < z:
                            self.send_z(unit, target, False)

    def exchange(self, unit):
        at = self.at_z(unit, self.z)
        remote(at, self.fv.at[unit], self.snd.at[5], self.fr.at[unit], self.r, 1 - self.t)

    def store_copy(self, unit):
        return pltpu.make_async_copy(self.obuf.at[lax.rem(unit, 2)], self.out.at[pl.ds(pl.multiple_of(unit * UNIT, UNIT), UNIT)], self.store.at[lax.rem(unit, 2)])

    def conclude(self, unit):
        fv = self.fv.at[unit]
        landed(fv, self.fr.at[unit])
        at = self.cv.at[unit, self.z * 2 + self.y]

        @pl.when(unit >= 2)
        def _():
            self.store_copy(unit - 2).wait()
        obuf = self.obuf.at[lax.rem(unit, 2)]
        middle = pl.ds(S_EDGE, S_MIDDLE)
        obuf[middle] = at[middle].astype(jnp.float32) + fv[pl.ds(pl.multiple_of(self.t * S_EDGE, 16), S_MIDDLE)].astype(jnp.float32)
        obuf[self.edge(self.t)] = at[self.edge(self.t)].astype(jnp.float32)
        obuf[self.edge(1 - self.t)] = fv[pl.ds(pl.multiple_of((1 - self.t) * S_MIDDLE, 16), S_EDGE)].astype(jnp.float32)
        self.store_copy(unit).start()

    LEAD = 3
    EVENTS = (("sum_core", 0, ()), ("sum_x", 1, ()), ("sum_y", 2, ()), ("hop", 3, (1,)), ("hop", 4, (2,)), ("hop", 5, (3,)), ("exchange", 5, ()), ("conclude", 6, ()))

    def ticks(self):
        return self.units + max(e[1] for e in self.EVENTS)

    def begin(self):
        for unit in range(min(2, self.units)):
            self.own_copy(unit).start()
        for unit in range(min(self.LEAD, self.units)):
            self.send_core(unit)

    def tick(self, step):
        for name, lag, args in self.EVENTS:
            unit = step - lag

            @pl.when((unit >= 0) & (unit < self.units))
            def _(name=name, unit=unit, args=args):
                getattr(self, name)(unit, *args)
        unit = step + self.LEAD

        @pl.when(unit < self.units)
        def _():
            self.send_core(unit)

    def finish(self):
        units, z, grads = self.units, self.z, self.grads
        for unit in range(max(0, units - 2), units):
            self.store_copy(unit).wait()
        landed(grads.at[:, 0, 0:units * UNIT], self.snd.at[0])
        landed(grads.at[:, 0, 0:units * S_EDGE], self.snd.at[1])
        landed(grads.at[0:4, 0, 0:units * S_PLANE], self.snd.at[2])
        for k in range(4):
            @pl.when(z == k)
            def _(k=k):
                if k < 3:
                    landed(grads.at[0:3 - k, 0, 0:units * S_PLANE], self.snd.at[3])
                if k > 0:
                    landed(grads.at[0:k, 0, 0:units * S_PLANE], self.snd.at[4])
        landed(grads.at[0, 0, 0:units * S_PLANE], self.snd.at[5])


def scatter_kernel(units, grads, small, last, out, small_out, last_out, lv, lout, lsem, own, obuf, cv, xv, yv, zv, fv, sown, sv, sx, load, store, cr, xr, yr, zr, fr, snd, sload, ssend, srecv, sxsem):
    r, t, c, y, z = place()
    R = lax.axis_size("rows")
    cs = pltpu.make_async_copy(small, sown, sload.at[0])
    cs.start()
    greet([(lax.rem(r + d, R), t) for d in range(1, R)] + [(r, 1 - t)])
    s = Scatter(grads, out, units, (own, obuf, cv, xv, yv, zv, fv), (load, store, cr, xr, yr, zr, fr, snd))
    s.begin()
    lc = pltpu.make_async_copy(last, lv.at[0], lsem.at[0])
    lc.start()
    lc.wait()
    cs.wait()
    for d in range(1, R):
        to = lax.rem(r + d, R)
        remote(sown.at[to], sv.at[R - 1 - d], ssend, srecv, to, t)

    pieces = last.shape[0] // 16

    def step(i, carry):
        @pl.when((i >= 2) & (i < pieces + 2))
        def _():
            rows = pl.ds(pl.multiple_of((i - 2) * 16, 16), 16)
            remote(lv.at[0, rows], lv.at[1, rows], lsem.at[1], lsem.at[2], r, 1 - t)
        s.tick(i)
        return carry

    lax.fori_loop(0, s.ticks(), step, 0)
    landed(sown.at[0:R - 1], ssend)
    landed(sv.at[0:R - 1], srecv)
    total = sown[r]
    for d in range(R - 1):
        total = total + sv[d]
    sx[0] = total
    pltpu.make_async_remote_copy(src_ref=sx.at[0], dst_ref=sx.at[1], send_sem=sxsem.at[0], recv_sem=sxsem.at[1], device_id=(r, 1 - t), device_id_type=MESH).start()
    landed(sx.at[0], sxsem.at[0])
    landed(sx.at[1], sxsem.at[1])
    sx[0] = sx[0] + sx[1]
    done = pltpu.make_async_copy(sx.at[0], small_out, sload.at[1])
    done.start()
    landed(lv.at[0], lsem.at[1])
    landed(lv.at[1], lsem.at[2])
    lout[...] = lv[0].astype(jnp.float32) + lv[1].astype(jnp.float32)
    lc = pltpu.make_async_copy(lout, last_out, lsem.at[0])
    lc.start()
    s.finish()
    done.wait()
    lc.wait()


def scatter_call(grads, small, last, cid):
    R, rows, _ = grads.shape
    units = rows // UNIT
    bf = jnp.bfloat16
    return pl.pallas_call(
        functools.partial(scatter_kernel, units),
        out_shape=(jax.ShapeDtypeStruct((rows, 1024), jnp.float32), jax.ShapeDtypeStruct(small.shape[1:], small.dtype), jax.ShapeDtypeStruct(last.shape, jnp.float32)),
        in_specs=[pl.BlockSpec(memory_space=ANY)] * 3,
        out_specs=(pl.BlockSpec(memory_space=ANY),) * 3,
        scratch_shapes=[pltpu.VMEM((2,) + last.shape, bf), pltpu.VMEM(last.shape, jnp.float32), pltpu.SemaphoreType.DMA((3,)),
                        pltpu.VMEM((2, 8, UNIT, 1024), bf), pltpu.VMEM((2, UNIT, 1024), jnp.float32),
                        pltpu.VMEM((units, 8, UNIT, 1024), bf), pltpu.VMEM((units, 8, S_EDGE, 1024), bf), pltpu.VMEM((units, 4, S_PLANE, 1024), bf),
                        pltpu.VMEM((units, 5, S_PLANE, 1024), bf), pltpu.VMEM((units, S_PLANE, 1024), bf),
                        pltpu.VMEM(small.shape, small.dtype), pltpu.VMEM((R - 1,) + small.shape[1:], small.dtype), pltpu.VMEM((2,) + small.shape[1:], small.dtype),
                        pltpu.SemaphoreType.DMA((2,)), pltpu.SemaphoreType.DMA((2,)), pltpu.SemaphoreType.DMA((units,)), pltpu.SemaphoreType.DMA((units,)),
                        pltpu.SemaphoreType.DMA((units, 4)), pltpu.SemaphoreType.DMA((units, 5)), pltpu.SemaphoreType.DMA((units,)), pltpu.SemaphoreType.DMA((6,)),
                        pltpu.SemaphoreType.DMA((2,)), pltpu.SemaphoreType.DMA, pltpu.SemaphoreType.DMA, pltpu.SemaphoreType.DMA((2,))],
        compiler_params=pltpu.CompilerParams(collective_id=cid, has_side_effects=True, vmem_limit_bytes=67043328),
        name="scatter_grads",
    )(grads.reshape(R // 2, 2, rows, 1024), small, last)


HALO = 384
FI1, FO1, QKV, ATT, GLU, CONV, FI2, FO2, UNITS = 0, 4, 8, 11, 12, 14, 15, 19, 23
GAIN, SHIFT, BIAS, TAPS, REL = 0, 6, 20, 28, 33
F32, BF16 = jnp.float32, jnp.bfloat16
TILE = 1024
NN = (((1,), (0,)), ((), ()))
NT = (((1,), (1,)), ((), ()))
TN = (((0,), (0,)), ((), ()))
VMEM_LIMIT = 67043328


def dot(a, b, dims=NN):
    return lax.dot_general(a, b, dims, preferred_element_type=F32)


def by_rows(count, size, fn):
    loop(count // size, lambda i: fn(pl.ds(pl.multiple_of(i * size, size), size)))


def by_cols(count, fn):
    loop(count // TILE, lambda i: fn(pl.ds(pl.multiple_of(i * TILE, TILE), TILE)))


def normalized(v):
    centred = v - jnp.mean(v, axis=-1, keepdims=True)
    rs = lax.rsqrt(jnp.mean(centred * centred, axis=-1, keepdims=True) + EPS)
    return centred * rs, rs


def norm_back(w, gain, vhat, rs):
    wg = w * gain
    return rs * (wg - jnp.mean(wg, axis=-1, keepdims=True) - vhat * jnp.mean(wg * vhat, axis=-1, keepdims=True))


def eight(v):
    return jnp.sum(v.reshape(v.shape[0] // 8, 8, v.shape[1]), axis=0)


def sigmoid(v):
    return 1.0 / (1.0 + jnp.exp(-v))


class Weights:
    def __init__(self, full, buf, sems, blocks):
        self.full, self.buf, self.sems, self.blocks = full, buf, sems, blocks
        self.R = full.shape[0]
        self.n = 1024 // self.R

    def copies(self, k):
        unit, kind, index = self.blocks[k]
        n, R = self.n, self.R
        if kind == "in":
            return [(self.full.at[s, (unit + index) * n:(unit + index + 1) * n], self.buf.at[k, s * n:(s + 1) * n]) for s in range(R)]
        return [(self.full.at[index * (R // 4) + s, unit * n:(unit + 4) * n], self.buf.at[k, s * 4 * n:(s + 1) * 4 * n]) for s in range(R // 4)]

    def start(self, *ks):
        for k in ks or range(len(self.blocks)):
            for src, dst in self.copies(k):
                pltpu.make_async_copy(src, dst, self.sems.at[k]).start()

    def wait(self, *ks):
        for k in ks:
            pltpu.make_async_copy(self.buf.at[k], self.buf.at[k], self.sems.at[k]).wait()


class Grads:
    def __init__(self, out, buf, sems):
        self.out, self.buf, self.sems, self.count = out, buf, sems, 0
        self.R = out.shape[0]
        self.n = 1024 // self.R

    def put(self, unit, kind, index, left, right, out=None):
        out = self.out if out is None else out
        slot = self.count % 2
        buf, n, R = self.buf.at[slot], self.n, self.R
        if self.count >= 2:
            self.wait(slot)

        def cols(c):
            buf[:, c] = dot(left, right(c), TN).astype(BF16)
        by_cols(1024, cols)
        if kind == "in":
            pairs = [(buf.at[s * n:(s + 1) * n], out.at[s, (unit + index) * n:(unit + index + 1) * n]) for s in range(R)]
        else:
            pairs = [(buf.at[s * 4 * n:(s + 1) * 4 * n], out.at[index * (R // 4) + s, unit * n:(unit + 4) * n]) for s in range(R // 4)]
        for src, dst in pairs:
            pltpu.make_async_copy(src, dst, self.sems.at[slot]).start()
        self.count += 1

    def wait(self, slot):
        pltpu.make_async_copy(self.buf.at[slot], self.buf.at[slot], self.sems.at[slot]).wait()

    def finish(self):
        for slot in range(min(2, self.count)):
            self.wait(slot)


def flipped(x, size):
    m = size
    return x + m - 2 * m * lax.rem(x // m, 2)


def cube_peers():
    r, t = lax.axis_index("rows"), lax.axis_index("tm")
    peers, m = [], 1
    while m < lax.axis_size("rows"):
        peers.append((flipped(r, m), t))
        m *= 2
    m = 1
    while m < lax.axis_size("tm"):
        peers.append((r, flipped(t, m)))
        m *= 2
    return peers


def add_all(send, recv, ssem, rsem):
    for i, (rows, tm) in enumerate(cube_peers()):
        remote(send.at[i], recv.at[i], ssem.at[i], rsem.at[i], rows, tm)
        landed(send.at[i], ssem.at[i])
        landed(recv.at[i], rsem.at[i])
        send[i + 1] = send[i] + recv[i]
    return len(cube_peers())


def edge_peers():
    r, t, T = lax.axis_index("rows"), lax.axis_index("tm"), lax.axis_size("tm")
    return [(r, lax.rem(t + 1, T)), (r, lax.rem(t + T - 1, T))]


def swap_edges(pad, count, sems):
    r, t, T = lax.axis_index("rows"), lax.axis_index("tm"), lax.axis_size("tm")

    @pl.when(t < T - 1)
    def _():
        remote(pad.at[count:count + 8], pad.at[0:8], sems.at[0], sems.at[1], r, t + 1)

    @pl.when(t > 0)
    def _():
        remote(pad.at[8:16], pad.at[count + 8:count + 16], sems.at[2], sems.at[3], r, t - 1)

    @pl.when(t < T - 1)
    def _():
        landed(pad.at[0:8], sems.at[0])
        landed(pad.at[0:8], sems.at[3])

    @pl.when(t > 0)
    def _():
        landed(pad.at[0:8], sems.at[2])
        landed(pad.at[0:8], sems.at[1])


def whole():
    return pl.BlockSpec(memory_space=pltpu.VMEM)


def anywhere():
    return pl.BlockSpec(memory_space=ANY)


def shape(*dims, dtype=F32):
    return jax.ShapeDtypeStruct(dims, dtype)


BLOCKS_A = tuple([(FI1, "in", j) for j in range(4)] + [(FO1, "out", j) for j in range(4)] + [(QKV, "in", j) for j in range(3)])


def norm_tokens(tokens, params, a):
    def norm(rows):
        vhat, _ = normalized(tokens[rows].astype(F32))
        a[rows] = (vhat * params[GAIN:GAIN + 1] + params[SHIFT:SHIFT + 1]).astype(BF16)
    by_rows(tokens.shape[0], 256, norm)


def norm_resid(x1, params, a):
    def norm(rows):
        vhat, _ = normalized(x1[rows])
        a[rows] = (vhat * params[GAIN + 1:GAIN + 2] + params[SHIFT + 1:SHIFT + 2]).astype(BF16)
    by_rows(x1.shape[0], 256, norm)


class Front:
    def __init__(self, w, params, tokens, x1, z1, a, h, zbuf, zsem):
        self.w, self.params, self.tokens, self.x1, self.z1, self.a, self.h, self.zbuf, self.zsem = w, params, tokens, x1, z1, a, h, zbuf, zsem

    def stored(self, slot):
        pltpu.make_async_copy(self.zbuf.at[slot], self.zbuf.at[slot], self.zsem.at[slot]).wait()

    def hidden(self, j):
        slot = j % 2
        self.w.wait(j)
        if j >= 2:
            self.stored(slot)
        z = dot(self.a[...], self.w.buf[j]) + self.params[BIAS + j:BIAS + j + 1]
        self.zbuf[slot] = z
        self.h[j] = (z * sigmoid(z)).astype(BF16)
        pltpu.make_async_copy(self.zbuf.at[slot], self.z1.at[:, j * 1024:(j + 1) * 1024], self.zsem.at[slot]).start()

    def project(self, j):
        self.w.wait(4 + j)
        part = dot(self.h[j], self.w.buf[4 + j])
        if j > 0:
            part = self.x1[...] + part
        if j == 3:
            part = self.tokens[...].astype(F32) + 0.5 * (part + self.params[SHIFT + 6:SHIFT + 7])
        self.x1[...] = part

    def mix(self, block, source, shift, out, rows):
        value = dot(source[...], self.w.buf[8 + block])
        if shift is not None:
            value = value + self.params[shift:shift + 1]
        out[rows] = value.astype(BF16)


def front_kernel(blocks, *refs):
    small, *refs = refs
    ws, refs = refs[:8], refs[8:]
    (tokens, hot, segq, segk, full, params, x1, z1, q, k, v, beside, o, lse, windows, own, slab, slabs, table, strip, wbuf, a, h, zbuf,
     load, keep, ssend, srecv, wsem, zsem, esem, *sems) = refs
    r, t, c, y, z = place()
    units, R, count = len(blocks), lax.axis_size("rows"), tokens.shape[0]
    copies = []
    for unit, (w, row, col) in enumerate(blocks):
        cp = pltpu.make_async_copy(ws[w].at[row:row + UNIT, col:col + 1024], own.at[unit * UNIT:(unit + 1) * UNIT], load.at[unit])
        cp.start()
        copies.append(cp)
    cs = pltpu.make_async_copy(small, slab, keep)
    cs.start()
    greet([(lax.rem(r + d, R), t) for d in range(1, R)] + [(r, 1 - t)])
    cs.wait()
    for d in range(1, R):
        remote(slab, slabs.at[r], ssend, srecv, lax.rem(r + d, R), t)
    stored = []
    for unit, cp in enumerate(copies):
        cp.wait()
        put = pltpu.make_async_copy(own.at[unit * UNIT:(unit + 1) * UNIT], full.at[r, unit * UNIT:(unit + 1) * UNIT], load.at[unit])
        put.start()
        stored.append(put)
    for put in stored:
        put.wait()
    g = Gather(full, 0, units, sems)
    g.begin()

    def take_rows():
        landed(slabs.at[0:R - 1], ssend)
        landed(slabs.at[0:R - 1], srecv)
        slabs[r] = slab[...]
        for pair in range(R // 2):
            params[:, pair * 128:(pair + 1) * 128] = (slabs[2 * pair].astype(F32) + slabs[2 * pair + 1].astype(F32))[0:40]
        for s in range(R):
            rows = slabs[s].astype(F32)
            for b in range(2):
                for part in range(2):
                    at = 40 + 2 * b + part
                    params[BIAS + 4 * b + s // 4:BIAS + 4 * b + s // 4 + 1, (s % 4) * 256 + part * 128:(s % 4) * 256 + (part + 1) * 128] = rows[at:at + 1]

    w = Weights(full, wbuf, wsem, BLOCKS_A)
    f = Front(w, params, tokens, x1, z1, a, h, zbuf, zsem)
    mine, other = pl.ds(pl.multiple_of(t * HALO, 128), count), pl.ds(pl.multiple_of((1 - t) * count, 128), HALO)

    def exchange():
        norm_resid(x1, params, a)
        first = pl.multiple_of((1 - t) * (count - HALO), 128)
        remote(a.at[pl.ds(first, HALO)], beside, esem.at[0], esem.at[1], r, 1 - t)

    def receive():
        landed(beside, esem.at[0])
        landed(beside, esem.at[1])
        f.mix(1, beside, None, k, other)

    def bias_rows():
        for head in range(HEADS):
            table[head:head + 1] = params[REL:REL + 1, head * NB:(head + 1) * NB].astype(BF16)
        windows[...] = dot(table[...], hot[...])

    def head_rows(head, b):
        cols, rows = pl.ds(pl.multiple_of(head * 128, 128), 128), pl.ds(b * QB, QB)
        if b == 0:
            strip[...] = strip_of(windows[pl.ds(head, 1)], windows.shape[-1])
        base = k.shape[0] + QB - t * HALO
        attend_rows(q[rows, cols], k[:, cols], v[:, cols], strip, base, b, segq[rows], segk[...], o.at[rows, cols], lse.at[head, rows])

    work = {(2, 1): take_rows, (3, 1): lambda: norm_tokens(tokens, params, a), (4, 1): bias_rows, (5, 1): lambda: f.hidden(0), (6, 1): lambda: f.hidden(1), (7, 1): lambda: f.hidden(2), (8, 1): lambda: f.hidden(3),
            (12, 0): lambda: f.project(0), (12, 2): lambda: f.project(1), (13, 0): lambda: f.project(2), (13, 1): lambda: f.project(3), (13, 2): exchange,
            (14, 1): lambda: (w.wait(8), f.mix(0, a, SHIFT + 7, q, slice(None))), (14, 3): lambda: (w.wait(9), f.mix(1, a, None, k, mine)),
            (15, 1): lambda: (w.wait(10), f.mix(2, a, SHIFT + 8, v, mine)), (16, 1): receive, (17, 1): lambda: f.mix(2, beside, SHIFT + 8, v, other)}
    for step in range(18):
        for quarter in range(4):
            g.part(step, quarter)
            if (step, quarter) in work:
                work[step, quarter]()
        unit = step - g.LAG
        if 0 <= unit < 11:
            g.arrived(unit)
            if unit == 7:
                w.start(4, 5, 6, 7)
            elif unit < 4 or unit > 7:
                w.start(unit)

    def heads(step):
        for quarter in range(4):
            g.part(step, quarter)
            head_rows(step - 18, quarter)
    loop(18 + HEADS, heads, 18)
    g.run(18 + HEADS, units + g.LAG)
    g.finish()
    for slot in range(2):
        f.stored(slot)


def front(small, weights, tokens, hot, segq, segk, cid):
    length = hot.shape[1]
    count, R, blocks = tokens.shape[0], lax.axis_size("rows"), []
    near = count + HALO
    for i, weight in enumerate(weights):
        n, cols = weight.shape
        blocks += [(i, row, col) for col in range(0, cols, 1024) for row in range(0, n, UNIT)]
    units, sem = len(blocks), pltpu.SemaphoreType.DMA
    return pl.pallas_call(
        functools.partial(front_kernel, tuple(blocks)),
        out_shape=[shape(R, units * UNIT, 1024, dtype=BF16), shape(40, 1024), shape(count, 1024), shape(count, 4096), shape(count, 1024, dtype=BF16),
                   shape(near, 1024, dtype=BF16), shape(near, 1024, dtype=BF16), shape(HALO, 1024, dtype=BF16),
                   shape(count, 1024), shape(HEADS, count, 128), shape(HEADS, length)],
        in_specs=[anywhere()] * 9 + [whole()] * 4, out_specs=[anywhere(), whole(), whole(), anywhere()] + [whole()] * 7,
        scratch_shapes=[pltpu.VMEM((units * UNIT, 1024), BF16), pltpu.VMEM(small.shape, BF16), pltpu.VMEM((R,) + small.shape, BF16), pltpu.VMEM((HEADS, NB), BF16), pltpu.VMEM((QB, length), F32),
                        pltpu.VMEM((11, 1024, 1024), BF16), pltpu.VMEM((count, 1024), BF16), pltpu.VMEM((4, count, 1024), BF16), pltpu.VMEM((2, count, 1024), F32),
                        sem((units,)), sem, sem, sem, sem((11,)), sem((2,)), sem((2,))] + Gather.scratch(units),
        compiler_params=pltpu.CompilerParams(vmem_limit_bytes=VMEM_LIMIT, collective_id=cid, has_side_effects=True),
        name="front",
    )(small, *weights, tokens, hot, segq, segk)


def plain_front_kernel(tokens, params, full, x1, z1, q, k, v, wbuf, a, h, zbuf, wsem, zsem):
    w = Weights(full, wbuf, wsem, BLOCKS_A)
    w.start()
    f = Front(w, params, tokens, x1, z1, a, h, zbuf, zsem)
    norm_tokens(tokens, params, a)
    for j in range(4):
        f.hidden(j)
    for j in range(4):
        f.project(j)
    norm_resid(x1, params, a)
    w.wait(8, 9, 10)
    f.mix(0, a, SHIFT + 7, q, slice(None))
    f.mix(1, a, None, k, slice(None))
    f.mix(2, a, SHIFT + 8, v, slice(None))
    for slot in range(2):
        f.stored(slot)


def plain_front(tokens, params, full):
    count = tokens.shape[0]
    return pl.pallas_call(
        plain_front_kernel,
        out_shape=[shape(count, 1024), shape(count, 4096)] + [shape(count, 1024, dtype=BF16)] * 3,
        in_specs=[whole(), whole(), anywhere()], out_specs=[whole(), anywhere(), whole(), whole(), whole()],
        scratch_shapes=[pltpu.VMEM((11, 1024, 1024), BF16), pltpu.VMEM((count, 1024), BF16), pltpu.VMEM((4, count, 1024), BF16), pltpu.VMEM((2, count, 1024), F32),
                        pltpu.SemaphoreType.DMA((11,)), pltpu.SemaphoreType.DMA((2,))],
        compiler_params=pltpu.CompilerParams(vmem_limit_bytes=VMEM_LIMIT),
        name="front",
    )(tokens, params, full)


QB = 128


def strip_of(window, length):
    return pltpu.roll(jnp.broadcast_to(window, (QB, length)), 0, 1, stride=1, stride_axis=0)


def score_block(q, k, strip, base, b, near, segq, segk, scale):
    start = pl.multiple_of(base - b * QB, 128)
    s = dot(q, k, NT) * scale + strip[:, pl.ds(start, near)]
    return jnp.where(segq == segk, s, NEG), start


SCALE = 1.0 / math.sqrt(128)


def attend_rows(q, k, v, strip, base, b, segq, segk, o, lse):
    s, _ = score_block(q, k, strip, base, b, k.shape[0], segq, segk, SCALE)
    top = jnp.max(s, axis=-1, keepdims=True)
    p = jnp.exp(s - top)
    total = jnp.sum(p, axis=-1, keepdims=True)
    o[...] = dot(p.astype(BF16), v) / total
    lse[...] = jnp.broadcast_to(top + jnp.log(total), (QB, 128))


def attend_kernel(off, q, k, v, window, segq, segk, o, lse, strip):
    near = k.shape[0]
    strip[...] = strip_of(window[0], window.shape[-1])
    base = near + QB - off[0]

    def block(b):
        rows = pl.ds(pl.multiple_of(b * QB, QB), QB)
        attend_rows(q[rows], k[...], v[...], strip, base, b, segq[rows], segk[...], o.at[rows], lse.at[0, rows])
    loop(q.shape[0] // QB, block)


def head_block(n):
    return pl.BlockSpec((n, 128), lambda h, off: (0, h))


def attend(q, k, v, windows, segq, segk, off):
    count, near, length = q.shape[0], k.shape[0], windows.shape[-1]
    return pl.pallas_call(
        attend_kernel,
        out_shape=[shape(count, 1024), shape(HEADS, count, 128)],
        grid_spec=pltpu.PrefetchScalarGridSpec(
            num_scalar_prefetch=1, grid=(HEADS,),
            in_specs=[head_block(count), head_block(near), head_block(near), pl.BlockSpec((1, 1, length), lambda h, off: (h, 0, 0)),
                      pl.BlockSpec((count, 1), lambda h, off: (0, 0)), pl.BlockSpec((1, near), lambda h, off: (0, 0))],
            out_specs=[head_block(count), pl.BlockSpec((1, count, 128), lambda h, off: (h, 0, 0))],
            scratch_shapes=[pltpu.VMEM((QB, length), F32)]),
        compiler_params=pltpu.CompilerParams(vmem_limit_bytes=VMEM_LIMIT),
        name="attend",
    )(off, q, k, v, windows, segq, segk)


def attend_back_kernel(scale, off, q, k, v, window, segq, segk, o, lse, do, dq, dk, dv, dtable, strip, ds, pb, acc):
    near = k.shape[0]
    length = window.shape[-1]
    strip[...] = strip_of(window[0], length)
    acc[...] = jnp.zeros_like(acc)
    base = near + QB - off[0]

    def block(b):
        rows = pl.ds(pl.multiple_of(b * QB, QB), QB)
        s, start = score_block(q[rows], k[...], strip, base, b, near, segq[rows], segk[...], scale)
        p = jnp.exp(s - lse[0, rows, 0:1])
        delta = jnp.sum(do[rows].astype(F32) * o[rows], axis=-1, keepdims=True)
        d = (p * (dot(do[rows], v[...], NT) - delta)).astype(BF16)
        pb[rows] = p.astype(BF16)
        ds[rows] = d
        dq[rows] = (dot(d, k[...]) * scale).astype(BF16)
        acc[:, pl.ds(start, near)] += d.astype(F32)
    loop(q.shape[0] // QB, block)
    dims = (((0,), (0,)), ((), ()))
    dk[...] = (dot(ds[...], q[...], dims) * scale).astype(BF16)
    dv[...] = dot(pb[...], do[...], dims).astype(BF16)
    rows, size = acc[...], QB
    while size > 1:
        size //= 2
        rows = rows[:size] + pltpu.roll(rows[size:], length - size, 1)
    dtable[0] = rows


def attend_back(q, k, v, windows, segq, segk, off, o, lse, do):
    count, near, length = q.shape[0], k.shape[0], windows.shape[-1]
    return pl.pallas_call(
        functools.partial(attend_back_kernel, 1.0 / math.sqrt(128)),
        out_shape=[shape(count, 1024, dtype=BF16), shape(near, 1024, dtype=BF16), shape(near, 1024, dtype=BF16), shape(HEADS, 1, length)],
        grid_spec=pltpu.PrefetchScalarGridSpec(
            num_scalar_prefetch=1, grid=(HEADS,),
            in_specs=[head_block(count), head_block(near), head_block(near), pl.BlockSpec((1, 1, length), lambda h, off: (h, 0, 0)),
                      pl.BlockSpec((count, 1), lambda h, off: (0, 0)), pl.BlockSpec((1, near), lambda h, off: (0, 0)),
                      head_block(count), pl.BlockSpec((1, count, 128), lambda h, off: (h, 0, 0)), head_block(count)],
            out_specs=[head_block(count), head_block(near), head_block(near), pl.BlockSpec((1, 1, length), lambda h, off: (h, 0, 0))],
            scratch_shapes=[pltpu.VMEM((QB, length), F32), pltpu.VMEM((count, near), BF16), pltpu.VMEM((count, near), BF16), pltpu.VMEM((QB, length), F32)]),
        compiler_params=pltpu.CompilerParams(vmem_limit_bytes=VMEM_LIMIT),
        name="attend_back",
    )(off, q, k, v, windows, segq, segk, o, lse, do)


ROWS = 128


BLOCKS_C = ((ATT, "in", 0), (GLU, "in", 0), (GLU, "in", 1))


def convolve_kernel(x1, o, params, seg, full, x2, c1, c2, u, y, sums, wbuf, a, half, send, recv, wsem, esem, ssem, rsem):
    w = Weights(full, wbuf, wsem, BLOCKS_C)
    w.start()
    count = x1.shape[0]
    u[0:8] = jnp.zeros((8, 1024), F32)
    u[count + 8:count + 16] = jnp.zeros((8, 1024), F32)
    greet(cube_peers() + edge_peers())

    def cast(rows):
        a[rows] = o[rows].astype(BF16)
    by_rows(count, 256, cast)
    w.wait(0)

    def project(c):
        x2[:, c] = x1[:, c] + dot(a[...], wbuf[0, :, c]) + params[SHIFT + 9:SHIFT + 10, c]
    by_cols(1024, project)

    def norm(rows):
        vhat, _ = normalized(x2[rows])
        a[rows] = (vhat * params[GAIN + 2:GAIN + 3] + params[SHIFT + 2:SHIFT + 3]).astype(BF16)
    by_rows(count, 256, norm)
    w.wait(1, 2)

    def gate(c):
        value = dot(a[...], wbuf[1, :, c]) + params[SHIFT + 10:SHIFT + 11, c]
        other = dot(a[...], wbuf[2, :, c]) + params[SHIFT + 11:SHIFT + 12, c]
        c1[:, c] = value
        c2[:, c] = other
        u[8:count + 8, c] = (value * sigmoid(other)).astype(BF16).astype(F32)
    by_cols(1024, gate)
    swap_edges(u, count, esem)
    half[...] = jnp.zeros_like(half)

    def taps(i):
        first = pl.multiple_of(i * ROWS, ROWS)
        here = seg[pl.ds(first + 8, ROWS)]
        total = jnp.zeros((ROWS, 1024), F32)
        block = u[pl.ds(first, ROWS + 16)]
        segs = seg[pl.ds(first, ROWS + 16)]
        for tap in range(KSIZE):
            k = slice(6 + tap, 6 + tap + ROWS)
            total = total + params[TAPS + tap:TAPS + tap + 1] * jnp.where(segs[k] == here, block[k], 0.0)
        y[pl.ds(first, ROWS)] = total
        half[0:8] += eight(total)
        half[8:16] += eight(total * total)
    loop(count // ROWS, taps)
    fold(half, send)
    steps = add_all(send, recv, ssem, rsem)
    sums[...] = send[steps]


def fold(half, send):
    send[0, 0:1] = jnp.sum(half[0:8], axis=0, keepdims=True)
    send[0, 1:2] = jnp.sum(half[8:16], axis=0, keepdims=True)


def reduce_scratch(rows=2):
    steps = (lax.axis_size("rows").bit_length() - 1) + (lax.axis_size("tm").bit_length() - 1)
    return [pltpu.VMEM((steps + 1, rows, 1024), F32), pltpu.VMEM((steps, rows, 1024), F32)], [pltpu.SemaphoreType.DMA((steps,)), pltpu.SemaphoreType.DMA((steps,))]


def convolve(x1, o, params, seg, full, cid):
    count = x1.shape[0]
    bufs, sems = reduce_scratch()
    return pl.pallas_call(
        convolve_kernel,
        out_shape=[shape(count, 1024), shape(count, 1024), shape(count, 1024), shape(count + 16, 1024), shape(count, 1024), shape(2, 1024)],
        in_specs=[whole()] * 4 + [anywhere()], out_specs=[whole()] * 6,
        scratch_shapes=[pltpu.VMEM((3, 1024, 1024), BF16), pltpu.VMEM((count, 1024), BF16), pltpu.VMEM((16, 1024), F32)] + bufs + [pltpu.SemaphoreType.DMA((3,)), pltpu.SemaphoreType.DMA((4,))] + sems,
        compiler_params=pltpu.CompilerParams(vmem_limit_bytes=VMEM_LIMIT, collective_id=cid, has_side_effects=True),
        name="convolve",
    )(x1, o, params, seg, full)


def batch_stats(sums, frames):
    mean = sums[0:1] / frames
    square = sums[1:2] / frames
    return mean, lax.rsqrt(square - mean * mean + EPS)


BLOCKS_D = tuple([(CONV, "in", 0)] + [(FI2, "in", j) for j in range(4)] + [(FO2, "out", j) for j in range(4)])


def middle_kernel(frames, x2, y, sums, cot, params, full, out, g3, dn, totals, small, grads, grads_b,
                  wbuf, a, e, d, dz, h, z, stage, half, send, recv, wsem, gsem, ssem, rsem):
    w = Weights(full, wbuf, wsem, BLOCKS_D)
    w.start()
    greet(cube_peers())
    g = Grads(grads, stage, gsem)
    count = x2.shape[0]
    mean, inverse = batch_stats(sums, frames)
    small[...] = jnp.zeros_like(small)
    half[...] = jnp.zeros_like(half)

    def active(rows):
        n = (y[rows] - mean) * inverse * params[GAIN + 5:GAIN + 6] + params[SHIFT + 5:SHIFT + 6]
        e[rows] = (n * sigmoid(n)).astype(BF16)
    by_rows(count, 256, active)
    w.wait(0)
    x3 = g3

    def project(c):
        x3[:, c] = x2[:, c] + dot(e[...], wbuf[0, :, c]) + params[SHIFT + 12:SHIFT + 13, c]
    by_cols(1024, project)

    def norm(rows):
        vhat, _ = normalized(x3[rows])
        a[rows] = (vhat * params[GAIN + 3:GAIN + 4] + params[SHIFT + 3:SHIFT + 4]).astype(BF16)
    by_rows(count, 256, norm)
    for j in range(4):
        w.wait(1 + j)

    def hidden(j):
        def cols(c):
            v = dot(a[...], wbuf[1 + j, :, c]) + params[pl.ds(BIAS + 4 + j, 1), c]
            z[j, :, c] = v
            h[j, :, c] = (v * sigmoid(v)).astype(BF16)
        by_cols(1024, cols)
    loop(4, hidden)
    w.wait(5, 6, 7, 8)

    def outward(c):
        acc = dot(h[0], wbuf[5, :, c])
        for j in range(1, 4):
            acc = acc + dot(h[j], wbuf[5 + j, :, c])
        out[:, c] = x3[:, c] + 0.5 * (acc + params[SHIFT + 13:SHIFT + 14, c])
    by_cols(1024, outward)

    def last(rows):
        vhat, rs = normalized(out[rows])
        gain = params[GAIN + 4:GAIN + 5]
        out[rows] = vhat * gain + params[SHIFT + 4:SHIFT + 5]
        ct = cot[rows]
        small[0:8] += eight(ct * vhat)
        small[8:16] += eight(ct)
        g4 = norm_back(ct, gain, vhat, rs)
        dn[rows] = g4
        half = (0.5 * g4).astype(BF16)
        d[rows] = half
        small[16:24] += eight(half.astype(F32))
    by_rows(count, 256, last)

    def back(j):
        def cols(c):
            v = z[j, :, c]
            s = sigmoid(v)
            dh = dot(d[...], wbuf[5 + j, c, :], NT) * (s * (1.0 + v * (1.0 - s)))
            dh = dh.astype(BF16)
            dz[j, :, c] = dh
            small[pl.ds(pl.multiple_of(24 + 8 * j, 8), 8), c] += eight(dh.astype(F32))
        by_cols(1024, cols)
    loop(4, back)
    for j in range(4):
        g.put(0, "out", j, h[j], lambda c: d[:, c], grads_b)
    for j in range(4):
        g.put(FI2, "in", j, a[...], lambda c, j=j: dz[j, :, c])
    da = z.at[0]

    def inward(c):
        acc = dot(dz[0], wbuf[1, c, :], NT)
        for j in range(1, 4):
            acc = acc + dot(dz[j], wbuf[1 + j, c, :], NT)
        da[:, c] = acc
    by_cols(1024, inward)

    def resid(rows):
        vhat, rs = normalized(x3[rows])
        w3 = da[rows]
        small[56:64] += eight(w3 * vhat)
        small[64:72] += eight(w3)
        total = dn[rows] + norm_back(w3, params[GAIN + 3:GAIN + 4], vhat, rs)
        g3[rows] = total
        de = total.astype(BF16)
        d[rows] = de
        small[72:80] += eight(de.astype(F32))
    by_rows(count, 256, resid)
    g.put(CONV, "in", 0, e[...], lambda c: d[:, c])

    def dnorm(c):
        dn[:, c] = dot(d[...], wbuf[0, c, :], NT)
    by_cols(1024, dnorm)

    def finish(rows):
        yhat = (y[rows] - mean) * inverse
        n = yhat * params[GAIN + 5:GAIN + 6] + params[SHIFT + 5:SHIFT + 6]
        s = sigmoid(n)
        v = dn[rows] * (s * (1.0 + n * (1.0 - s)))
        dn[rows] = v
        half[0:8] += eight(v * yhat)
        half[8:16] += eight(v)
    by_rows(count, 256, finish)
    small[80:96] = half[...]
    fold(half, send)
    steps = add_all(send, recv, ssem, rsem)
    totals[...] = send[steps]
    g.finish()


def middle(x2, y, sums, cot, params, full, frames, cid):
    count = x2.shape[0]
    bufs, sems = reduce_scratch()
    return pl.pallas_call(
        functools.partial(middle_kernel, frames),
        out_shape=[shape(count, 1024), shape(count, 1024), shape(count, 1024), shape(2, 1024), shape(96, 1024), shape(full.shape[0], FO2 * 1024 // full.shape[0], 1024, dtype=BF16), shape(full.shape[0], 4096 // full.shape[0], 1024, dtype=BF16)],
        in_specs=[whole()] * 5 + [anywhere()], out_specs=[whole()] * 5 + [anywhere()] * 2,
        scratch_shapes=[pltpu.VMEM((9, 1024, 1024), BF16), pltpu.VMEM((count, 1024), BF16), pltpu.VMEM((count, 1024), BF16), pltpu.VMEM((count, 1024), BF16),
                        pltpu.VMEM((4, count, 1024), BF16), pltpu.VMEM((4, count, 1024), BF16), pltpu.VMEM((4, count, 1024), F32),
                        pltpu.VMEM((2, 1024, 1024), BF16), pltpu.VMEM((16, 1024), F32)] + bufs + [pltpu.SemaphoreType.DMA((9,)), pltpu.SemaphoreType.DMA((2,))] + sems,
        compiler_params=pltpu.CompilerParams(vmem_limit_bytes=VMEM_LIMIT, collective_id=cid, has_side_effects=True),
        name="middle",
    )(x2, y, sums, cot, params, full)


def convolve_back_kernel(frames, dn, y, sums, totals, c1, c2, u, x2, g3, o, params, seg, full, grads_in, g2, dob, small, grads,
                         wbuf, a, d, dc, pad, stage, wsem, gsem, esem):
    w = Weights(full, wbuf, wsem, BLOCKS_C)
    w.start()
    count = x2.shape[0]
    pad[0:8] = jnp.zeros((8, 1024), F32)
    pad[count + 8:count + 16] = jnp.zeros((8, 1024), F32)
    greet(edge_peers())
    g = Grads(grads, stage, gsem)
    mean, inverse = batch_stats(sums, frames)
    gain = params[GAIN + 5:GAIN + 6]
    product = totals[0:1] * gain / frames
    total = totals[1:2] * gain / frames
    small[...] = jnp.zeros_like(small)

    def dy(i):
        rows = pl.ds(pl.multiple_of(i * ROWS, ROWS), ROWS)
        yhat = (y[rows] - mean) * inverse
        v = inverse * (dn[rows] * gain - total - yhat * product)
        pad[pl.ds(pl.multiple_of(i * ROWS + 8, 8), ROWS)] = v.astype(BF16).astype(F32)
        vhat, _ = normalized(x2[rows])
        a[rows] = (vhat * params[GAIN + 2:GAIN + 3] + params[SHIFT + 2:SHIFT + 3]).astype(BF16)
    loop(count // ROWS, dy)
    swap_edges(pad, count, esem)

    def taps(i):
        first = pl.multiple_of(i * ROWS, ROWS)
        rows = pl.ds(first, ROWS)
        block, grad, segs = u[pl.ds(first, ROWS + 16)], pad[pl.ds(first, ROWS + 16)], seg[pl.ds(first, ROWS + 16)]
        here, own = segs[8:ROWS + 8], grad[8:ROWS + 8]
        du = jnp.zeros((ROWS, 1024), F32)
        for tap in range(KSIZE):
            k = slice(6 + tap, 6 + tap + ROWS)
            small[8 * tap:8 * tap + 8] += eight(own * jnp.where(segs[k] == here, block[k], 0.0))
            b = slice(10 - tap, 10 - tap + ROWS)
            du = du + params[TAPS + tap:TAPS + tap + 1] * jnp.where(segs[b] == here, grad[b], 0.0)
        s = sigmoid(c2[rows])
        left = (du * s).astype(BF16)
        right = (du * c1[rows] * s * (1.0 - s)).astype(BF16)
        dc[0, rows] = left
        dc[1, rows] = right
        small[40:48] += eight(left.astype(F32))
        small[48:56] += eight(right.astype(F32))
    loop(count // ROWS, taps)
    w.wait(0, 1, 2)
    da = pad.at[0:count]

    def inward(c):
        da[:, c] = dot(dc[0], wbuf[1, c, :], NT) + dot(dc[1], wbuf[2, c, :], NT)
    by_cols(1024, inward)

    def resid(rows):
        vhat, rs = normalized(x2[rows])
        v = da[rows]
        small[56:64] += eight(v * vhat)
        small[64:72] += eight(v)
        both = g3[rows] + norm_back(v, params[GAIN + 2:GAIN + 3], vhat, rs)
        g2[rows] = both
        dx = both.astype(BF16)
        d[rows] = dx
        small[72:80] += eight(dx.astype(F32))
    by_rows(count, 256, resid)

    def attended(c):
        dob[:, c] = dot(d[...], wbuf[0, c, :], NT).astype(BF16)
    by_cols(1024, attended)
    for j in range(2):
        g.put(GLU, "in", j, a[...], lambda c, j=j: dc[j, :, c])

    def cast(rows):
        a[rows] = o[rows].astype(BF16)
    by_rows(count, 256, cast)
    g.put(ATT, "in", 0, a[...], lambda c: d[:, c])
    g.finish()


def convolve_back(dn, y, sums, totals, c1, c2, u, x2, g3, o, params, seg, full, grads, frames, cid):
    count = x2.shape[0]
    return pl.pallas_call(
        functools.partial(convolve_back_kernel, frames),
        out_shape=[shape(count, 1024), shape(count, 1024, dtype=BF16), shape(80, 1024), shape(*grads.shape, dtype=BF16)],
        in_specs=[whole()] * 12 + [anywhere()] * 2, out_specs=[whole()] * 3 + [anywhere()],
        scratch_shapes=[pltpu.VMEM((3, 1024, 1024), BF16), pltpu.VMEM((count, 1024), BF16), pltpu.VMEM((count, 1024), BF16), pltpu.VMEM((2, count, 1024), BF16),
                        pltpu.VMEM((count + 16, 1024), F32), pltpu.VMEM((2, 1024, 1024), BF16),
                        pltpu.SemaphoreType.DMA((3,)), pltpu.SemaphoreType.DMA((2,)), pltpu.SemaphoreType.DMA((4,))],
        input_output_aliases={13: 3},
        compiler_params=pltpu.CompilerParams(vmem_limit_bytes=VMEM_LIMIT, collective_id=cid, has_side_effects=True),
        name="convolve_back",
    )(dn, y, sums, totals, c1, c2, u, x2, g3, o, params, seg, full, grads)


BLOCKS_E = tuple([(QKV, "in", j) for j in range(3)] + [(FO1, "out", j) for j in range(4)] + [(FI1, "in", j) for j in range(4)])


def rear_kernel(halo, tokens, x1, z1, g2, dq, dk, dv, params, full, *refs):
    if halo:
        beside, grads_in, dtok, small, grads, wbuf, a, d, dz, zbuf, hbuf, stage, da, back, got, wsem, zsem, gsem, esem = refs
    else:
        grads_in, dtok, small, grads, wbuf, a, d, dz, zbuf, hbuf, stage, da, wsem, zsem, gsem = refs
    w = Weights(full, wbuf, wsem, BLOCKS_E)
    w.start()
    g = Grads(grads, stage, gsem)
    count = tokens.shape[0]
    for j in range(2):
        pltpu.make_async_copy(z1.at[:, j * 1024:(j + 1) * 1024], zbuf.at[j], zsem.at[j]).start()
    small[...] = jnp.zeros_like(small)
    own = 0
    if halo:
        r, t = lax.axis_index("rows"), lax.axis_index("tm")
        greet([(r, 1 - t)])
        own, other = pl.multiple_of(t * HALO, 128), pl.multiple_of((1 - t) * count, 128)
        w.wait(1, 2)

        def outside(c):
            back[:, c] = (dot(dk[pl.ds(other, HALO)], wbuf[1, c, :], NT) + dot(dv[pl.ds(other, HALO)], wbuf[2, c, :], NT)).astype(BF16)
        by_cols(1024, outside)
        remote(back, got, esem.at[0], esem.at[1], r, 1 - t)
        w.wait(0)
    else:
        w.wait(0, 1, 2)
    mine = pl.ds(own, count)

    def inside(c):
        da[:, c] = dot(dq[...], wbuf[0, c, :], NT) + dot(dk[mine], wbuf[1, c, :], NT) + dot(dv[mine], wbuf[2, c, :], NT)
    by_cols(1024, inside)

    def norm(rows):
        vhat, _ = normalized(x1[rows])
        a[rows] = (vhat * params[GAIN + 1:GAIN + 2] + params[SHIFT + 1:SHIFT + 2]).astype(BF16)
        small[0:8] += eight(dq[rows].astype(F32))
    by_rows(count, 256, norm)

    def values(rows):
        small[8:16] += eight(dv[rows].astype(F32))
    by_rows(dv.shape[0], 128, values)
    g.put(QKV, "in", 0, a[...], lambda c: dq[:, c])
    if halo:
        for j, grad in ((1, dk), (2, dv)):
            slot = g.count % 2
            buf, n, R = stage.at[slot], g.n, g.R
            if g.count >= 2:
                g.wait(slot)

            def cols(c, grad=grad, buf=buf):
                buf[:, c] = (dot(a[...], grad[mine, c], TN) + dot(beside[...], grad[pl.ds(other, HALO), c], TN)).astype(BF16)
            by_cols(1024, cols)
            for s in range(R):
                pltpu.make_async_copy(buf.at[s * n:(s + 1) * n], grads.at[s, (QKV + j) * n:(QKV + j + 1) * n], gsem.at[slot]).start()
            g.count += 1
        landed(back, esem.at[0])
        landed(got, esem.at[1])
        first = pl.multiple_of((1 - t) * (count - HALO), 128)

        def merge(i):
            rows = pl.ds(pl.multiple_of(first + i * 64, 64), 64)
            da[rows] += got[pl.ds(pl.multiple_of(i * 64, 64), 64)].astype(F32)
        loop(HALO // 64, merge)
    else:
        g.put(QKV, "in", 1, a[...], lambda c: dk[:, c])
        g.put(QKV, "in", 2, a[...], lambda c: dv[:, c])

    def resid(rows):
        vhat, rs = normalized(x1[rows])
        v = da[rows]
        small[16:24] += eight(v * vhat)
        small[24:32] += eight(v)
        both = g2[rows] + norm_back(v, params[GAIN + 1:GAIN + 2], vhat, rs)
        dtok[rows] = both
        half = (0.5 * both).astype(BF16)
        d[rows] = half
        small[32:40] += eight(half.astype(F32))
        vhat, _ = normalized(tokens[rows].astype(F32))
        a[rows] = (vhat * params[GAIN:GAIN + 1] + params[SHIFT:SHIFT + 1]).astype(BF16)
    by_rows(count, 256, resid)
    w.wait(3, 4, 5, 6)
    for j in range(4):
        slot = j % 2
        pltpu.make_async_copy(zbuf.at[slot], zbuf.at[slot], zsem.at[slot]).wait()

        def cols(c, j=j, slot=slot):
            v = zbuf[slot, :, c]
            s = sigmoid(v)
            hbuf[:, c] = (v * s).astype(BF16)
            dh = (dot(d[...], wbuf[3 + j, c, :], NT) * (s * (1.0 + v * (1.0 - s)))).astype(BF16)
            dz[j, :, c] = dh
            small[40 + 8 * j:48 + 8 * j, c] += eight(dh.astype(F32))
        by_cols(1024, cols)
        if j + 2 < 4:
            pltpu.make_async_copy(z1.at[:, (j + 2) * 1024:(j + 3) * 1024], zbuf.at[slot], zsem.at[slot]).start()
        g.put(FO1, "out", j, hbuf[...], lambda c: d[:, c])
    for j in range(4):
        g.put(FI1, "in", j, a[...], lambda c, j=j: dz[j, :, c])
    w.wait(7, 8, 9, 10)

    def inward(c):
        acc = dot(dz[0], wbuf[7, c, :], NT)
        for j in range(1, 4):
            acc = acc + dot(dz[j], wbuf[7 + j, c, :], NT)
        da[:, c] = acc
    by_cols(1024, inward)

    def last(rows):
        vhat, rs = normalized(tokens[rows].astype(F32))
        v = da[rows]
        small[72:80] += eight(v * vhat)
        small[80:88] += eight(v)
        dtok[rows] = dtok[rows] + norm_back(v, params[GAIN:GAIN + 1], vhat, rs)
    by_rows(count, 256, last)
    g.finish()


def rear(tokens, x1, z1, g2, dq, dk, dv, params, full, beside, grads, cid):
    count = tokens.shape[0]
    halo = beside is not None
    scratch = [pltpu.VMEM((11, 1024, 1024), BF16), pltpu.VMEM((count, 1024), BF16), pltpu.VMEM((count, 1024), BF16), pltpu.VMEM((4, count, 1024), BF16),
               pltpu.VMEM((2, count, 1024), F32), pltpu.VMEM((count, 1024), BF16), pltpu.VMEM((2, 1024, 1024), BF16), pltpu.VMEM((count, 1024), F32)]
    if halo:
        scratch += [pltpu.VMEM((HALO, 1024), BF16), pltpu.VMEM((HALO, 1024), BF16)]
    scratch += [pltpu.SemaphoreType.DMA((11,)), pltpu.SemaphoreType.DMA((2,)), pltpu.SemaphoreType.DMA((2,))]
    if halo:
        scratch.append(pltpu.SemaphoreType.DMA((2,)))
    specs = [whole(), whole(), anywhere()] + [whole()] * 5 + [anywhere()] + ([whole()] if halo else []) + [anywhere()]
    return pl.pallas_call(
        functools.partial(rear_kernel, halo),
        out_shape=[shape(count, 1024), shape(88, 1024), shape(*grads.shape, dtype=BF16)],
        in_specs=specs, out_specs=[whole(), whole(), anywhere()], scratch_shapes=scratch,
        input_output_aliases={len(specs) - 1: 2},
        compiler_params=pltpu.CompilerParams(vmem_limit_bytes=VMEM_LIMIT, **({"collective_id": cid, "has_side_effects": True} if halo else {})),
        name="rear",
    )(tokens, x1, z1, g2, dq, dk, dv, params, full, *((beside,) if halo else ()), grads)


def pack_rows(gains, shifts, ffn_bias, conv_kernel, rel_table):
    n = rel_table.shape[0]
    rows = jnp.concatenate([gains, shifts, ffn_bias.reshape(2 * 4, n), conv_kernel, rel_table[None]], axis=0).reshape(-1)
    return jnp.pad(rows, (0, 8 * 384 - rows.shape[0])).reshape(8, 384)


def slab_rows(gains, shifts, ffn_bias, conv_kernel, rel_table):
    rows = jnp.concatenate([gains, shifts, jnp.zeros((8, 64), BF16), conv_kernel, rel_table[None], jnp.zeros((6, 64), BF16)], axis=0)
    zero = jnp.zeros_like(rows)
    odd = lax.rem(lax.axis_index("rows"), 2) == 1
    wide = jnp.concatenate([jnp.where(odd, zero, rows), jnp.where(odd, rows, zero)], axis=1)
    return jnp.concatenate([wide, ffn_bias.reshape(4, 128), jnp.zeros((4, 128), BF16)], axis=0)


def wide_rows(smalls):
    R = smalls.shape[0]
    n = 1024 // R
    rows = smalls.reshape(R, -1)[:, : 34 * n].reshape(R, 34, n).astype(F32)
    flat = rows.transpose(1, 0, 2).reshape(34, 1024)
    bias = rows[:, 20:28].reshape(R, 2, 4 * n).transpose(1, 0, 2).reshape(8, 1024)
    return jnp.concatenate([flat[:20], bias, flat[28:], jnp.zeros((6, 1024), F32)], axis=0)


def slot_rows(rows, R):
    n = 1024 // R
    flat = rows.reshape(34, R, n).transpose(1, 0, 2)
    bias = rows[20:28].reshape(2, R, 4, n).transpose(1, 0, 2, 3).reshape(R, 8, n)
    flat = jnp.concatenate([flat[:, :20], bias, flat[:, 28:]], axis=1).reshape(R, 34 * n)
    return jnp.pad(flat, ((0, 0), (0, 8 * 384 - 34 * n))).reshape(R, 8, 384)


def shard_rows(small, R):
    n = 1024 // R
    rows = small.reshape(-1)[: 34 * n].reshape(34, n)
    return (rows[:6], rows[6:20], rows[20:28].reshape(2, 4 * n), rows[28:33], rows[33])


def pack_weights(weights):
    blocks = []
    for w in weights:
        rows, cols = w.shape
        blocks.append(w.reshape(rows, cols // 1024, 1024).transpose(1, 0, 2).reshape(-1, 1024))
    return jnp.concatenate(blocks, axis=0)


def unpack_shard(shard, weights):
    out, row = [], 0
    for w in weights:
        n, cols = w.shape
        count = n * cols // 1024
        out.append(shard[row : row + count].reshape(cols // 1024, n, 1024).transpose(1, 0, 2).reshape(n, cols))
        row += count
    return tuple(out)


def body(tokens, cotangent, segment_ids, rel_bucket, ffn1_in, ffn1_out, qkv_weight, attn_out, glu_in, conv_out, ffn2_in, ffn2_out,
         gains, shifts, ffn_bias, conv_kernel, rel_table):
    packed_rows, count, width = tokens.shape
    R, T = lax.axis_size("rows"), lax.axis_size("tm")
    t = lax.axis_index("tm")
    links = R == 16 and T == 2 and count == 512
    frames = R * T * count * packed_rows
    weights = (ffn1_in, ffn1_out, qkv_weight, attn_out, glu_in, conv_out, ffn2_in, ffn2_out)
    seg_all = lax.all_gather(segment_ids, "tm", axis=1, tiled=True)[0]
    seg_far = jnp.pad(seg_all, (HALO, HALO), constant_values=-1)
    segx = lax.dynamic_slice_in_dim(seg_far, HALO + t * count - 8, count + 16)[:, None]
    segq = segment_ids.reshape(count, 1)
    if links:
        near, off = count + HALO, t * HALO
        segk = lax.dynamic_slice_in_dim(seg_all, t * (count - HALO), near)[None]
    else:
        near, off = T * count, t * count
        segk = seg_all[None]
    length = 2 * near + QB
    places = np.clip(np.arange(length) - (near + QB), -MAXD, MAXD) + MAXD
    before, after = int(np.argmax(places > 0)), int(np.argmax(places >= 2 * MAXD))
    buckets = jnp.concatenate([jnp.broadcast_to(rel_bucket[:1], (before,)), rel_bucket[1 : 2 * MAXD], jnp.broadcast_to(rel_bucket[2 * MAXD :], (length - after,))])
    hot = (buckets[None, :] == jnp.arange(NB, dtype=jnp.int32)[:, None]).astype(F32)
    off = off.astype(jnp.int32).reshape(1)
    tok = tokens.reshape(count, width)
    if links:
        full, params, x1, z1, q, k, v, beside, o, lse, windows = front(slab_rows(gains, shifts, ffn_bias, conv_kernel, rel_table), weights, tok, hot.astype(BF16), segq, segk, 0)
        windows = windows.reshape(HEADS, 1, length)
    else:
        full = lax.all_gather(pack_weights(weights), "rows", axis=0)
        params = wide_rows(lax.all_gather(pack_rows(gains, shifts, ffn_bias, conv_kernel, rel_table), "rows", axis=0))

        windows = jnp.dot(params[REL].reshape(HEADS, NB), hot, precision=HIGH).reshape(HEADS, 1, length)

    if not links:
        x1, z1, q, k, v = plain_front(tok, params, full)
        beside = None
        k = lax.all_gather(k, "tm", axis=0, tiled=True)
        v = lax.all_gather(v, "tm", axis=0, tiled=True)
        o, lse = attend(q, k, v, windows, segq, segk, off)
    x2, c1, c2, u, y, sums = convolve(x1, o, params, segx, full, 3)
    output, g3, dn, totals, small_d, grads, grads_b = middle(x2, y, sums, cotangent.reshape(count, width), params, full, frames, 4)
    last = lax.psum_scatter(grads_b, "rows", scatter_dimension=0, tiled=False)
    g2, dob, small_c, grads = convolve_back(dn, y, sums, totals, c1, c2, u, x2, g3, o, params, segx, full, grads, frames, 5)
    dq, dk, dv, dtable = attend_back(q, k, v, windows, segq, segk, off, o, lse, dob)
    if not links:
        dk = lax.psum_scatter(dk, "tm", scatter_dimension=0, tiled=True)
        dv = lax.psum_scatter(dv, "tm", scatter_dimension=0, tiled=True)
    dtok, small_e, grads = rear(tok, x1, z1, g2, dq, dk, dv, params, full, beside, grads, 6)

    rel = lax.dot_general(dtable.reshape(HEADS, length), hot, (((1,), (1,)), ((), ())), precision=HIGH).reshape(1, 1024)
    d = jnp.sum(small_d.reshape(12, 8, 1024), axis=1)
    c = jnp.sum(small_c.reshape(10, 8, 1024), axis=1)
    e = jnp.sum(small_e.reshape(11, 8, 1024), axis=1)
    rows = jnp.concatenate([
        e[9:10], e[2:3], c[7:8], d[7:8], d[0:1], d[10:11],
        e[10:11], e[3:4], c[8:9], d[8:9], d[1:2], d[11:12], e[4:5], e[0:2], c[9:10], c[5:7], d[9:10], d[2:3],
        e[5:9], d[3:7], c[0:5], rel])
    if links:
        shard, small, last = scatter_call(grads, slot_rows(rows, R), last, 1)
    else:
        shard = lax.psum(lax.psum_scatter(grads, "rows", scatter_dimension=0, tiled=False), "tm").astype(F32)
        small = lax.psum(lax.psum_scatter(slot_rows(rows, R), "rows", scatter_dimension=0, tiled=False), "tm")
        last = lax.psum(last, "tm").astype(F32)
    return (output.reshape(tokens.shape), dtok.reshape(tokens.shape)) + unpack_shard(shard, weights[:7]) + (last,) + shard_rows(small, R)


def solution(mesh):
    return jax.shard_map(
        body,
        mesh=mesh,
        in_specs=(
            P("rows", "tm", None),
            P("rows", "tm", None),
            P("rows", "tm"),
            P(),
            P("rows", None),
            P("rows", None),
            P("rows", None),
            P("rows", None),
            P("rows", None),
            P("rows", None),
            P("rows", None),
            P("rows", None),
            P(None, "rows"),
            P(None, "rows"),
            P(None, "rows"),
            P(None, "rows"),
            P("rows"),
        ),
        out_specs=(
            P("rows", "tm", None),
            P("rows", "tm", None),
            P("rows", None),
            P("rows", None),
            P("rows", None),
            P("rows", None),
            P("rows", None),
            P("rows", None),
            P("rows", None),
            P("rows", None),
            P(None, "rows"),
            P(None, "rows"),
            P(None, "rows"),
            P(None, "rows"),
            P("rows"),
        ),
        check_vma=False,
    )
```

```python
import functools
import math

import jax
import jax.numpy as jnp
import numpy as np
from jax import lax
from jax.experimental import pallas as pl
from jax.experimental.pallas import tpu as pltpu
from jax.sharding import PartitionSpec as P

HEADS = 8
KSIZE = 5
NB = 128
MAXD = 256


EPS = 1e-05
NEG = -1e30
HIGH = lax.Precision.HIGHEST


MESH = pl.DeviceIdType.MESH
ANY = pl.ANY


def place():
    r = lax.axis_index("rows")
    t = lax.axis_index("tm")
    return r, t, lax.rem(r, 2), lax.rem(r // 2, 2), r // 4


def remote(src, dst, send, recv, rows, tm):
    pltpu.make_async_remote_copy(
        src_ref=src, dst_ref=dst, send_sem=send, recv_sem=recv,
        device_id=(rows, tm), device_id_type=MESH,
    ).start()


def landed(ref, sem):
    pltpu.make_async_copy(ref, ref, sem).wait()


def greet(peers):
    barrier = pltpu.get_barrier_semaphore()
    for rows, tm in peers:
        pl.semaphore_signal(barrier, inc=1, device_id=(rows, tm), device_id_type=MESH)
    pl.semaphore_wait(barrier, len(peers))


def link_peers():
    r, t, c, y, z = place()
    return [(r + 1 - 2 * c, t), (r + 2 - 4 * y, t), (lax.rem(r + 4, 16), t), (lax.rem(r + 12, 16), t), (r, 1 - t)]


def loop(n, fn, first=0):
    def one(i, carry):
        fn(i)
        return carry
    lax.fori_loop(first, n, one, 0)


UNIT = 64
EDGE = 24
MIDDLE = UNIT - 2 * EDGE
PLANE = EDGE + MIDDLE


class Gather:
    LEAD = 3
    EVENTS = (("from_z", 1, 0), ("from_y", 0, 0), ("from_z", 2, 1), ("from_y", 1, 1), ("from_x", 0, 1), ("from_z", 3, 2),
              ("from_y", 2, 2), ("from_x", 1, 2), ("from_y", 3, 3), ("from_x", 2, 3), ("from_x", 3, 4))
    LAG = 4

    def __init__(self, full, first, units, sems):
        self.full, self.first, self.units = full, first, units
        self.zr, self.yr, self.xr, self.cr, self.snd = sems
        self.r, self.t, self.c, self.y, self.z = place()
        self.taken = set()

    @staticmethod
    def scratch(units):
        sem = pltpu.SemaphoreType.DMA
        return [sem((units, 4)), sem((units, 4)), sem((units, 8)), sem((units,)), sem((5,))]

    def slot(self, z, y):
        return z * 4 + y * 2 + self.c

    def rows_of(self, unit, start, size):
        return pl.ds(pl.multiple_of((unit + self.first) * UNIT + start, 8), size)

    def inplane(self, slot, unit):
        return self.full.at[slot, self.rows_of(unit, self.t * EDGE, PLANE)]

    def edge(self, slot, unit, tm):
        return self.full.at[slot, self.rows_of(unit, tm * PLANE, EDGE)]

    def to_core(self, ref, unit):
        remote(ref, ref, self.snd.at[4], self.cr.at[unit], self.r + 1 - 2 * self.c, self.t)

    def send_own(self, unit):
        r, t, z = self.r, self.t, self.z
        plane = self.inplane(r, unit)

        @pl.when(z < 3)
        def _():
            remote(plane, plane, self.snd.at[0], self.zr.at[unit, z], r + 4, t)

        @pl.when(z > 0)
        def _():
            remote(plane, plane, self.snd.at[1], self.zr.at[unit, z], r - 4, t)

        remote(plane, plane, self.snd.at[2], self.yr.at[unit, z], self.slot(z, 1 - self.y), t)
        self.to_core(self.full.at[r, self.rows_of(unit, 0, UNIT)], unit)

    def pass_on(self, unit, z, y):
        s = self.slot(z, y)
        part = self.edge(s, unit, self.t)
        remote(part, part, self.snd.at[3], self.xr.at[unit, z * 2 + y], self.r, 1 - self.t)
        self.to_core(self.inplane(s, unit), unit)

    def from_z(self, unit, distance):
        for sign in (-1, 1):
            z = self.z + sign * distance

            @pl.when((z >= 0) & (z <= 3))
            def _(z=z, sign=sign):
                plane = self.inplane(self.slot(z, self.y), unit)
                landed(plane, self.zr.at[unit, z])
                onward = self.z - sign

                @pl.when((onward >= 0) & (onward <= 3))
                def _():
                    remote(plane, plane, self.snd.at[0 if sign < 0 else 1], self.zr.at[unit, z], self.slot(onward, self.y), self.t)

                remote(plane, plane, self.snd.at[2], self.yr.at[unit, z], self.slot(self.z, 1 - self.y), self.t)
                self.pass_on(unit, z, self.y)

    def from_y(self, unit, distance):
        for sign in (-1, 1) if distance else (1,):
            z = self.z + sign * distance

            @pl.when((z >= 0) & (z <= 3))
            def _(z=z):
                landed(self.inplane(self.slot(z, 1 - self.y), unit), self.yr.at[unit, z])
                self.pass_on(unit, z, 1 - self.y)

    def from_x(self, unit, distance):
        for other in (False, True) if distance else (True,):
            y = 1 - self.y if other else self.y
            for sign in (-1, 1) if distance else (1,):
                z = self.z + sign * distance

                @pl.when((z >= 0) & (z <= 3))
                def _(z=z, y=y):
                    part = self.edge(self.slot(z, y), unit, 1 - self.t)
                    landed(part, self.xr.at[unit, z * 2 + y])
                    self.to_core(part, unit)

    def begin(self):
        for unit in range(min(self.LEAD, self.units)):
            self.send_own(unit)

    def part(self, step, quarter):
        bounds = (0, 3, 6, 9, len(self.EVENTS))
        for name, distance, lag in self.EVENTS[bounds[quarter]:bounds[quarter + 1]]:
            unit = step - lag

            @pl.when((unit >= 0) & (unit < self.units))
            def _(name=name, distance=distance, unit=unit):
                getattr(self, name)(unit, distance)
        if quarter == 3:
            unit = step + self.LEAD

            @pl.when(unit < self.units)
            def _():
                self.send_own(unit)

    def tick(self, step):
        for quarter in range(4):
            self.part(step, quarter)

    def run(self, first, last):
        loop(last, self.tick, first)

    def arrived(self, unit):
        self.taken.add(unit)
        landed(self.full.at[0:8, self.rows_of(unit, 0, UNIT)], self.cr.at[unit])

    def finish(self):
        full, units, z = self.full, self.units, self.z
        for unit in range(units):
            if unit not in self.taken:
                self.arrived(unit)
        plane = units * PLANE
        for k in range(4):
            @pl.when(z == k)
            def _(k=k):
                if k < 3:
                    landed(full.at[0:k + 1, 0:plane], self.snd.at[0])
                if k > 0:
                    landed(full.at[0:4 - k, 0:plane], self.snd.at[1])
        landed(full.at[0:4, 0:plane], self.snd.at[2])
        landed(full.at[0:7, 0:units * EDGE], self.snd.at[3])
        landed(full.at[0:8, 0:units * UNIT], self.snd.at[4])


S_EDGE = 16
S_MIDDLE = UNIT - 2 * S_EDGE
S_PLANE = S_EDGE + S_MIDDLE


class Scatter:
    LEAD = 3
    RING = 10
    EVENTS = (("sum_core", 0, ()), ("sum_x", 1, ()), ("sum_y", 2, ()), ("hop", 3, (1,)), ("hop", 4, (2,)), ("hop", 5, (3,)), ("exchange", 5, ()), ("conclude", 6, ()))
    LAG = 6

    def __init__(self, grads, out, units, ready, first, scratch):
        self.grads, self.out, self.units, self.ready, self.first = grads, out, units, ready, first
        (self.own, self.obuf, self.cv, self.xv, self.yv, self.zv, self.fv,
         self.load, self.store, self.cr, self.xr, self.yr, self.zr, self.fr, self.core, self.snd, self.free) = scratch
        self.r, self.t, self.c, self.y, self.z = place()

    @classmethod
    def scratch(cls, units):
        sem, vmem, n, bf = pltpu.SemaphoreType.DMA, pltpu.VMEM, cls.RING, jnp.bfloat16
        return [vmem((2, 8, UNIT, 1024), bf), vmem((2, UNIT, 1024), jnp.float32), vmem((n, 8, UNIT, 1024), bf), vmem((n, 8, S_EDGE, 1024), bf),
                vmem((n, 4, S_PLANE, 1024), bf), vmem((n, 5, S_PLANE, 1024), bf), vmem((n, S_PLANE, 1024), bf),
                sem((2,)), sem((2,)), sem((units,)), sem((units,)), sem((units, 4)), sem((units, 5)), sem((units,)), sem, sem((cls.RING, 5)), pltpu.SemaphoreType.REGULAR((5,))]

    def ring(self, unit):
        return lax.rem(unit, self.RING)

    def rows_of(self, unit):
        late = self.units - self.ready
        after = unit - self.ready
        late_unit = after + late // 2 - jnp.where(after >= late // 2, late, 0)
        number = jnp.where(unit < self.ready, unit + self.first, late_unit)
        return pl.ds(pl.multiple_of(number * UNIT, UNIT), UNIT)

    def mine(self):
        return pl.ds(pl.multiple_of(self.t * S_EDGE, 16), S_PLANE)

    def edge(self, tm):
        return pl.ds(pl.multiple_of(tm * S_PLANE, 16), S_EDGE)

    def granted(self, unit, kind):
        @pl.when(unit >= self.RING)
        def _():
            pl.semaphore_wait(self.free.at[kind], 1)

    def own_copy(self, unit):
        return pltpu.make_async_copy(self.grads.at[:, self.c, self.rows_of(unit)], self.own.at[lax.rem(unit, 2)], self.load.at[lax.rem(unit, 2)])

    def send_core(self, unit):
        self.granted(unit, 0)
        remote(self.grads.at[:, 1 - self.c, self.rows_of(unit)], self.cv.at[self.ring(unit)], self.core, self.cr.at[unit], self.r + 1 - 2 * self.c, self.t)

    def add(self, a, b, n):
        def one(i):
            a[i] = (a[i].astype(jnp.float32) + b[i].astype(jnp.float32)).astype(jnp.bfloat16)
        loop(n, one)

    def sum_core(self, unit):
        at = self.ring(unit)
        cv = self.cv.at[at]
        landed(cv, self.cr.at[unit])
        self.own_copy(unit).wait()
        self.add(cv, self.own.at[lax.rem(unit, 2)], 8)

        @pl.when(unit + 2 < self.units)
        def _():
            self.own_copy(unit + 2).start()
        self.granted(unit, 1)
        remote(cv.at[:, self.edge(1 - self.t)], self.xv.at[at], self.snd.at[at, 0], self.xr.at[unit], self.r, 1 - self.t)

    def sum_x(self, unit):
        at = self.ring(unit)
        xv, cv = self.xv.at[at], self.cv.at[at]
        landed(xv, self.xr.at[unit])
        self.add(cv.at[:, self.edge(self.t)], xv, 8)
        self.granted(unit, 2)
        for k in range(4):
            remote(cv.at[k * 2 + 1 - self.y, self.mine()], self.yv.at[at, k], self.snd.at[at, 1], self.yr.at[unit, k], self.r + 2 - 4 * self.y, self.t)

    def at_z(self, unit, z):
        return self.cv.at[self.ring(unit), z * 2 + self.y, self.mine()]

    def send_z(self, unit, target, up):
        at, entry = self.at_z(unit, target), target + (1 if up else 0)
        remote(at, self.zv.at[self.ring(unit), entry], self.snd.at[self.ring(unit), 2 if up else 3], self.zr.at[unit, entry], self.r + (4 if up else -4), self.t)

    def take_z(self, unit, target, below):
        at, entry = self.at_z(unit, target), target + (1 if below else 0)
        zv = self.zv.at[self.ring(unit), entry]
        landed(zv, self.zr.at[unit, entry])
        at[...] = (at[...].astype(jnp.float32) + zv[...].astype(jnp.float32)).astype(jnp.bfloat16)

    def sum_y(self, unit):
        for k in range(4):
            yv = self.yv.at[self.ring(unit), k]
            landed(yv, self.yr.at[unit, k])
            at = self.at_z(unit, k)
            at[...] = (at[...].astype(jnp.float32) + yv[...].astype(jnp.float32)).astype(jnp.bfloat16)

        @pl.when(self.z == 0)
        def _():
            self.granted(unit, 3)
            for target in (3, 2, 1):
                self.send_z(unit, target, True)

        @pl.when(self.z == 3)
        def _():
            self.granted(unit, 4)
            for target in (0, 1, 2):
                self.send_z(unit, target, False)

    def hop(self, unit, number):
        for z in range(4):
            @pl.when(self.z == z)
            def _(z=z):
                if number == z:
                    if z < 3:
                        self.granted(unit, 3)
                    for target in range(3, z - 1, -1):
                        self.take_z(unit, target, True)
                        if target > z:
                            self.send_z(unit, target, True)
                if number == 3 - z:
                    if z > 0:
                        self.granted(unit, 4)
                    for target in range(0, z + 1):
                        self.take_z(unit, target, False)
                        if target < z:
                            self.send_z(unit, target, False)

    def exchange(self, unit):
        at = self.ring(unit)
        remote(self.at_z(unit, self.z), self.fv.at[at], self.snd.at[at, 4], self.fr.at[unit], self.r, 1 - self.t)

    def store_copy(self, unit):
        return pltpu.make_async_copy(self.obuf.at[lax.rem(unit, 2)], self.out.at[self.rows_of(unit)], self.store.at[lax.rem(unit, 2)])

    def conclude(self, unit):
        at = self.ring(unit)
        fv, cv = self.fv.at[at], self.cv.at[at, self.z * 2 + self.y]
        landed(fv, self.fr.at[unit])

        @pl.when(unit >= 2)
        def _():
            self.store_copy(unit - 2).wait()
        obuf = self.obuf.at[lax.rem(unit, 2)]
        middle = pl.ds(S_EDGE, S_MIDDLE)
        obuf[middle] = cv[middle].astype(jnp.float32) + fv[pl.ds(pl.multiple_of(self.t * S_EDGE, 16), S_MIDDLE)].astype(jnp.float32)
        obuf[self.edge(self.t)] = cv[self.edge(self.t)].astype(jnp.float32)
        obuf[self.edge(1 - self.t)] = fv[pl.ds(pl.multiple_of((1 - self.t) * S_MIDDLE, 16), S_EDGE)].astype(jnp.float32)
        self.store_copy(unit).start()
        landed(self.xv.at[at], self.snd.at[at, 0])
        landed(self.yv.at[at], self.snd.at[at, 1])
        for z in range(4):
            @pl.when(self.z == z)
            def _(z=z):
                if z < 3:
                    landed(self.zv.at[at, 0:3 - z], self.snd.at[at, 2])
                if z > 0:
                    landed(self.zv.at[at, 0:z], self.snd.at[at, 3])
        landed(fv, self.snd.at[at, 4])
        more = unit + self.RING < self.units

        def free(kind, rows, tm):
            pl.semaphore_signal(self.free.at[kind], inc=1, device_id=(rows, tm), device_id_type=MESH)

        @pl.when(more)
        def _():
            free(0, self.r + 1 - 2 * self.c, self.t)
            free(1, self.r, 1 - self.t)
            free(2, self.r + 2 - 4 * self.y, self.t)

        @pl.when(more & (self.z > 0))
        def _():
            free(3, self.r - 4, self.t)

        @pl.when(more & (self.z < 3))
        def _():
            free(4, self.r + 4, self.t)

    def begin(self):
        for unit in range(min(2, self.units)):
            self.own_copy(unit).start()
        for unit in range(min(self.LEAD, self.units)):
            self.send_core(unit)

    def part(self, step, quarter):
        for name, lag, args in self.EVENTS[2 * quarter:2 * quarter + 2]:
            unit = step - lag

            @pl.when((unit >= 0) & (unit < self.units))
            def _(name=name, unit=unit, args=args):
                getattr(self, name)(unit, *args)
        if quarter == 3:
            unit = step + self.LEAD

            @pl.when(unit < self.units)
            def _():
                self.send_core(unit)

    def tick(self, step):
        for quarter in range(4):
            self.part(step, quarter)

    def run(self, first, last):
        loop(last, self.tick, first)

    def finish(self):
        for unit in range(max(0, self.units - 2), self.units):
            self.store_copy(unit).wait()
        landed(self.grads.at[:, 0, 0:self.units * UNIT], self.core)


def spread(slots, landing, send, recv):
    r, t, R = lax.axis_index("rows"), lax.axis_index("tm"), lax.axis_size("rows")
    for d in range(1, R):
        to = lax.rem(r + d, R)
        remote(slots.at[to], landing.at[R - 1 - d], send, recv, to, t)


def gathered(slots, landing, pair, sems, send, recv):
    r, t, R = lax.axis_index("rows"), lax.axis_index("tm"), lax.axis_size("rows")
    landed(slots.at[0:R - 1], send)
    landed(landing.at[0:R - 1], recv)
    total = slots[r]
    for d in range(R - 1):
        total = total + landing[d]
    pair[0] = total
    remote(pair.at[0], pair.at[1], sems.at[0], sems.at[1], r, 1 - t)
    landed(pair.at[0], sems.at[0])
    landed(pair.at[1], sems.at[1])
    pair[0] = pair[0] + pair[1]


HALO = 384
FI1, FO1, QKV, ATT, GLU, CONV, FI2, FO2, UNITS = 0, 4, 8, 11, 12, 14, 15, 19, 23
GAIN, SHIFT, BIAS, TAPS, REL = 0, 6, 20, 28, 33
F32, BF16 = jnp.float32, jnp.bfloat16
TILE = 1024
NN = (((1,), (0,)), ((), ()))
NT = (((1,), (1,)), ((), ()))
TN = (((0,), (0,)), ((), ()))
VMEM_LIMIT = 67043328


def dot(a, b, dims=NN):
    return lax.dot_general(a, b, dims, preferred_element_type=F32)


def by_rows(count, size, fn):
    loop(count // size, lambda i: fn(pl.ds(pl.multiple_of(i * size, size), size)))


def by_cols(count, fn):
    loop(count // TILE, lambda i: fn(pl.ds(pl.multiple_of(i * TILE, TILE), TILE)))


def normalized(v):
    centred = v - jnp.mean(v, axis=-1, keepdims=True)
    rs = lax.rsqrt(jnp.mean(centred * centred, axis=-1, keepdims=True) + EPS)
    return centred * rs, rs


def norm_back(w, gain, vhat, rs):
    wg = w * gain
    return rs * (wg - jnp.mean(wg, axis=-1, keepdims=True) - vhat * jnp.mean(wg * vhat, axis=-1, keepdims=True))


def eight(v):
    return jnp.sum(v.reshape(v.shape[0] // 8, 8, v.shape[1]), axis=0)


def sigmoid(v):
    return 1.0 / (1.0 + jnp.exp(-v))


class Weights:
    def __init__(self, full, buf, sems, blocks):
        self.full, self.buf, self.sems, self.blocks = full, buf, sems, blocks
        self.R = full.shape[0]
        self.n = 1024 // self.R

    def copies(self, k):
        unit, kind, index = self.blocks[k]
        n, R = self.n, self.R
        if kind == "in":
            return [(self.full.at[s, (unit + index) * n:(unit + index + 1) * n], self.buf.at[k, s * n:(s + 1) * n]) for s in range(R)]
        return [(self.full.at[index * (R // 4) + s, unit * n:(unit + 4) * n], self.buf.at[k, s * 4 * n:(s + 1) * 4 * n]) for s in range(R // 4)]

    def start(self, *ks):
        for k in ks or range(len(self.blocks)):
            for src, dst in self.copies(k):
                pltpu.make_async_copy(src, dst, self.sems.at[k]).start()

    def wait(self, *ks):
        for k in ks:
            pltpu.make_async_copy(self.buf.at[k], self.buf.at[k], self.sems.at[k]).wait()


class Grads:
    def __init__(self, out, buf, sems):
        self.out, self.buf, self.sems, self.count = out, buf, sems, 0
        self.R = 2 * out.shape[0]
        self.n = 1024 // self.R

    def put(self, unit, kind, index, left, right, out=None):
        out = self.out if out is None else out
        slot = self.count % 2
        buf, n, R = self.buf.at[slot], self.n, self.R
        if self.count >= 2:
            self.wait(slot)

        def cols(c):
            buf[:, c] = dot(left, right(c), TN).astype(BF16)
        by_cols(1024, cols)
        if kind == "in":
            pairs = [(buf.at[s * n:(s + 1) * n], out.at[s // 2, s % 2, (unit + index) * n:(unit + index + 1) * n]) for s in range(R)]
        else:
            pairs = [(buf.at[s * 4 * n:(s + 1) * 4 * n], out.at[(index * (R // 4) + s) // 2, (index * (R // 4) + s) % 2, unit * n:(unit + 4) * n]) for s in range(R // 4)]
        for src, dst in pairs:
            pltpu.make_async_copy(src, dst, self.sems.at[slot]).start()
        self.count += 1

    def wait(self, slot):
        pltpu.make_async_copy(self.buf.at[slot], self.buf.at[slot], self.sems.at[slot]).wait()

    def finish(self):
        for slot in range(min(2, self.count)):
            self.wait(slot)


def flipped(x, size):
    m = size
    return x + m - 2 * m * lax.rem(x // m, 2)


def cube_peers():
    r, t = lax.axis_index("rows"), lax.axis_index("tm")
    peers, m = [], 1
    while m < lax.axis_size("rows"):
        peers.append((flipped(r, m), t))
        m *= 2
    m = 1
    while m < lax.axis_size("tm"):
        peers.append((r, flipped(t, m)))
        m *= 2
    return peers


def add_all(send, recv, ssem, rsem):
    for i, (rows, tm) in enumerate(cube_peers()):
        remote(send.at[i], recv.at[i], ssem.at[i], rsem.at[i], rows, tm)
        landed(send.at[i], ssem.at[i])
        landed(recv.at[i], rsem.at[i])
        send[i + 1] = send[i] + recv[i]
    return len(cube_peers())


def edge_peers():
    r, t, T = lax.axis_index("rows"), lax.axis_index("tm"), lax.axis_size("tm")
    return [(r, lax.rem(t + 1, T)), (r, lax.rem(t + T - 1, T))]


def swap_edges(pad, count, sems):
    r, t, T = lax.axis_index("rows"), lax.axis_index("tm"), lax.axis_size("tm")

    @pl.when(t < T - 1)
    def _():
        remote(pad.at[count:count + 8], pad.at[0:8], sems.at[0], sems.at[1], r, t + 1)

    @pl.when(t > 0)
    def _():
        remote(pad.at[8:16], pad.at[count + 8:count + 16], sems.at[2], sems.at[3], r, t - 1)

    @pl.when(t < T - 1)
    def _():
        landed(pad.at[0:8], sems.at[0])
        landed(pad.at[0:8], sems.at[3])

    @pl.when(t > 0)
    def _():
        landed(pad.at[0:8], sems.at[2])
        landed(pad.at[0:8], sems.at[1])


def whole():
    return pl.BlockSpec(memory_space=pltpu.VMEM)


def anywhere():
    return pl.BlockSpec(memory_space=ANY)


def shape(*dims, dtype=F32):
    return jax.ShapeDtypeStruct(dims, dtype)


BLOCKS_A = tuple([(FI1, "in", j) for j in range(4)] + [(FO1, "out", j) for j in range(4)] + [(QKV, "in", j) for j in range(3)])


def norm_tokens(tokens, params, a):
    def norm(rows):
        vhat, _ = normalized(tokens[rows].astype(F32))
        a[rows] = (vhat * params[GAIN:GAIN + 1] + params[SHIFT:SHIFT + 1]).astype(BF16)
    by_rows(tokens.shape[0], 256, norm)


def norm_resid(x1, params, a):
    def norm(rows):
        vhat, _ = normalized(x1[rows])
        a[rows] = (vhat * params[GAIN + 1:GAIN + 2] + params[SHIFT + 1:SHIFT + 2]).astype(BF16)
    by_rows(x1.shape[0], 256, norm)


class Front:
    def __init__(self, w, params, tokens, x1, z1, a, h, zbuf, zsem):
        self.w, self.params, self.tokens, self.x1, self.z1, self.a, self.h, self.zbuf, self.zsem = w, params, tokens, x1, z1, a, h, zbuf, zsem

    def stored(self, slot):
        pltpu.make_async_copy(self.zbuf.at[slot], self.zbuf.at[slot], self.zsem.at[slot]).wait()

    def hidden(self, j):
        slot = j % 2
        self.w.wait(j)
        if j >= 2:
            self.stored(slot)
        z = dot(self.a[...], self.w.buf[j]) + self.params[BIAS + j:BIAS + j + 1]
        self.zbuf[slot] = z
        self.h[j] = (z * sigmoid(z)).astype(BF16)
        pltpu.make_async_copy(self.zbuf.at[slot], self.z1.at[:, j * 1024:(j + 1) * 1024], self.zsem.at[slot]).start()

    def project(self, j):
        self.w.wait(4 + j)
        part = dot(self.h[j], self.w.buf[4 + j])
        if j > 0:
            part = self.x1[...] + part
        if j == 3:
            part = self.tokens[...].astype(F32) + 0.5 * (part + self.params[SHIFT + 6:SHIFT + 7])
        self.x1[...] = part

    def mix(self, block, source, shift, out, rows):
        value = dot(source[...], self.w.buf[8 + block])
        if shift is not None:
            value = value + self.params[shift:shift + 1]
        out[rows] = value.astype(BF16)


def front_kernel(blocks, *refs):
    small, *refs = refs
    ws, refs = refs[:8], refs[8:]
    (tokens, hot, segq, segk, full, params, x1, z1, q, k, v, beside, o, lse, windows, own, slab, slabs, table, strip, wbuf, a, h, zbuf,
     load, keep, ssend, srecv, wsem, zsem, esem, *sems) = refs
    r, t, c, y, z = place()
    units, R, count = len(blocks), lax.axis_size("rows"), tokens.shape[0]
    copies = []
    for unit, (w, row, col) in enumerate(blocks):
        cp = pltpu.make_async_copy(ws[w].at[row:row + UNIT, col:col + 1024], own.at[unit * UNIT:(unit + 1) * UNIT], load.at[unit])
        cp.start()
        copies.append(cp)
    cs = pltpu.make_async_copy(small, slab, keep)
    cs.start()
    greet([(lax.rem(r + d, R), t) for d in range(1, R)] + [(r, 1 - t)])
    cs.wait()
    for d in range(1, R):
        remote(slab, slabs.at[r], ssend, srecv, lax.rem(r + d, R), t)
    stored = []
    for unit, cp in enumerate(copies):
        cp.wait()
        put = pltpu.make_async_copy(own.at[unit * UNIT:(unit + 1) * UNIT], full.at[r, unit * UNIT:(unit + 1) * UNIT], load.at[unit])
        put.start()
        stored.append(put)
    for put in stored:
        put.wait()
    g = Gather(full, 0, units, sems)
    g.begin()

    def take_rows():
        landed(slabs.at[0:R - 1], ssend)
        landed(slabs.at[0:R - 1], srecv)
        slabs[r] = slab[...]
        for pair in range(R // 2):
            params[:, pair * 128:(pair + 1) * 128] = (slabs[2 * pair].astype(F32) + slabs[2 * pair + 1].astype(F32))[0:40]
        for s in range(R):
            rows = slabs[s].astype(F32)
            for b in range(2):
                for part in range(2):
                    at = 40 + 2 * b + part
                    params[BIAS + 4 * b + s // 4:BIAS + 4 * b + s // 4 + 1, (s % 4) * 256 + part * 128:(s % 4) * 256 + (part + 1) * 128] = rows[at:at + 1]

    w = Weights(full, wbuf, wsem, BLOCKS_A)
    f = Front(w, params, tokens, x1, z1, a, h, zbuf, zsem)
    mine, other = pl.ds(pl.multiple_of(t * HALO, 128), count), pl.ds(pl.multiple_of((1 - t) * count, 128), HALO)

    def exchange():
        norm_resid(x1, params, a)
        first = pl.multiple_of((1 - t) * (count - HALO), 128)
        remote(a.at[pl.ds(first, HALO)], beside, esem.at[0], esem.at[1], r, 1 - t)

    def receive():
        landed(beside, esem.at[0])
        landed(beside, esem.at[1])
        f.mix(1, beside, None, k, other)

    def bias_rows():
        for head in range(HEADS):
            table[head:head + 1] = params[REL:REL + 1, head * NB:(head + 1) * NB].astype(BF16)
        windows[...] = dot(table[...], hot[...])

    def head_rows(head, b):
        cols, rows = pl.ds(pl.multiple_of(head * 128, 128), 128), pl.ds(b * QB, QB)
        if b == 0:
            strip[...] = strip_of(windows[pl.ds(head, 1)], windows.shape[-1])
        base = k.shape[0] + QB - t * HALO
        attend_rows(q[rows, cols], k[:, cols], v[:, cols], strip, base, b, segq[rows], segk[...], o.at[rows, cols], lse.at[head, rows])

    work = {(2, 1): take_rows, (3, 1): lambda: norm_tokens(tokens, params, a), (4, 1): bias_rows, (5, 1): lambda: f.hidden(0), (6, 1): lambda: f.hidden(1), (7, 1): lambda: f.hidden(2), (8, 1): lambda: f.hidden(3),
            (12, 0): lambda: f.project(0), (12, 2): lambda: f.project(1), (13, 0): lambda: f.project(2), (13, 1): lambda: f.project(3), (13, 2): exchange,
            (14, 1): lambda: (w.wait(8), f.mix(0, a, SHIFT + 7, q, slice(None))), (14, 3): lambda: (w.wait(9), f.mix(1, a, None, k, mine)),
            (15, 1): lambda: (w.wait(10), f.mix(2, a, SHIFT + 8, v, mine)), (16, 1): receive, (17, 1): lambda: f.mix(2, beside, SHIFT + 8, v, other)}
    for step in range(18):
        for quarter in range(4):
            g.part(step, quarter)
            if (step, quarter) in work:
                work[step, quarter]()
        unit = step - g.LAG
        if 0 <= unit < 11:
            g.arrived(unit)
            if unit == 7:
                w.start(4, 5, 6, 7)
            elif unit < 4 or unit > 7:
                w.start(unit)

    def heads(step):
        for quarter in range(4):
            g.part(step, quarter)
            head_rows(step - 18, quarter)
    loop(18 + HEADS, heads, 18)
    g.run(18 + HEADS, units + g.LAG)
    g.finish()
    for slot in range(2):
        f.stored(slot)


def front(small, weights, tokens, hot, segq, segk, cid):
    length = hot.shape[1]
    count, R, blocks = tokens.shape[0], lax.axis_size("rows"), []
    near = count + HALO
    for i, weight in enumerate(weights):
        n, cols = weight.shape
        blocks += [(i, row, col) for col in range(0, cols, 1024) for row in range(0, n, UNIT)]
    units, sem = len(blocks), pltpu.SemaphoreType.DMA
    return pl.pallas_call(
        functools.partial(front_kernel, tuple(blocks)),
        out_shape=[shape(R, units * UNIT, 1024, dtype=BF16), shape(40, 1024), shape(count, 1024), shape(count, 4096), shape(count, 1024, dtype=BF16),
                   shape(near, 1024, dtype=BF16), shape(near, 1024, dtype=BF16), shape(HALO, 1024, dtype=BF16),
                   shape(count, 1024), shape(HEADS, count, 128), shape(HEADS, length)],
        in_specs=[anywhere()] * 9 + [whole()] * 4, out_specs=[anywhere(), whole(), whole(), anywhere()] + [whole()] * 7,
        scratch_shapes=[pltpu.VMEM((units * UNIT, 1024), BF16), pltpu.VMEM(small.shape, BF16), pltpu.VMEM((R,) + small.shape, BF16), pltpu.VMEM((HEADS, NB), BF16), pltpu.VMEM((QB, length), F32),
                        pltpu.VMEM((11, 1024, 1024), BF16), pltpu.VMEM((count, 1024), BF16), pltpu.VMEM((4, count, 1024), BF16), pltpu.VMEM((2, count, 1024), F32),
                        sem((units,)), sem, sem, sem, sem((11,)), sem((2,)), sem((2,))] + Gather.scratch(units),
        compiler_params=pltpu.CompilerParams(vmem_limit_bytes=VMEM_LIMIT, collective_id=cid, has_side_effects=True),
        name="front",
    )(small, *weights, tokens, hot, segq, segk)


def plain_front_kernel(tokens, params, full, x1, z1, q, k, v, wbuf, a, h, zbuf, wsem, zsem):
    w = Weights(full, wbuf, wsem, BLOCKS_A)
    w.start()
    f = Front(w, params, tokens, x1, z1, a, h, zbuf, zsem)
    norm_tokens(tokens, params, a)
    for j in range(4):
        f.hidden(j)
    for j in range(4):
        f.project(j)
    norm_resid(x1, params, a)
    w.wait(8, 9, 10)
    f.mix(0, a, SHIFT + 7, q, slice(None))
    f.mix(1, a, None, k, slice(None))
    f.mix(2, a, SHIFT + 8, v, slice(None))
    for slot in range(2):
        f.stored(slot)


def plain_front(tokens, params, full):
    count = tokens.shape[0]
    return pl.pallas_call(
        plain_front_kernel,
        out_shape=[shape(count, 1024), shape(count, 4096)] + [shape(count, 1024, dtype=BF16)] * 3,
        in_specs=[whole(), whole(), anywhere()], out_specs=[whole(), anywhere(), whole(), whole(), whole()],
        scratch_shapes=[pltpu.VMEM((11, 1024, 1024), BF16), pltpu.VMEM((count, 1024), BF16), pltpu.VMEM((4, count, 1024), BF16), pltpu.VMEM((2, count, 1024), F32),
                        pltpu.SemaphoreType.DMA((11,)), pltpu.SemaphoreType.DMA((2,))],
        compiler_params=pltpu.CompilerParams(vmem_limit_bytes=VMEM_LIMIT),
        name="front",
    )(tokens, params, full)


QB = 128


def strip_of(window, length):
    return pltpu.roll(jnp.broadcast_to(window, (QB, length)), 0, 1, stride=1, stride_axis=0)


def score_block(q, k, strip, base, b, near, segq, segk, scale):
    start = pl.multiple_of(base - b * QB, 128)
    s = dot(q, k, NT) * scale + strip[:, pl.ds(start, near)]
    return jnp.where(segq == segk, s, NEG), start


SCALE = 1.0 / math.sqrt(128)


def attend_rows(q, k, v, strip, base, b, segq, segk, o, lse):
    s, _ = score_block(q, k, strip, base, b, k.shape[0], segq, segk, SCALE)
    top = jnp.max(s, axis=-1, keepdims=True)
    p = jnp.exp(s - top)
    total = jnp.sum(p, axis=-1, keepdims=True)
    o[...] = dot(p.astype(BF16), v) / total
    lse[...] = jnp.broadcast_to(top + jnp.log(total), (QB, 128))


def attend_kernel(off, q, k, v, window, segq, segk, o, lse, strip):
    near = k.shape[0]
    strip[...] = strip_of(window[0], window.shape[-1])
    base = near + QB - off[0]

    def block(b):
        rows = pl.ds(pl.multiple_of(b * QB, QB), QB)
        attend_rows(q[rows], k[...], v[...], strip, base, b, segq[rows], segk[...], o.at[rows], lse.at[0, rows])
    loop(q.shape[0] // QB, block)


def head_block(n):
    return pl.BlockSpec((n, 128), lambda h, off: (0, h))


def attend(q, k, v, windows, segq, segk, off):
    count, near, length = q.shape[0], k.shape[0], windows.shape[-1]
    return pl.pallas_call(
        attend_kernel,
        out_shape=[shape(count, 1024), shape(HEADS, count, 128)],
        grid_spec=pltpu.PrefetchScalarGridSpec(
            num_scalar_prefetch=1, grid=(HEADS,),
            in_specs=[head_block(count), head_block(near), head_block(near), pl.BlockSpec((1, 1, length), lambda h, off: (h, 0, 0)),
                      pl.BlockSpec((count, 1), lambda h, off: (0, 0)), pl.BlockSpec((1, near), lambda h, off: (0, 0))],
            out_specs=[head_block(count), pl.BlockSpec((1, count, 128), lambda h, off: (h, 0, 0))],
            scratch_shapes=[pltpu.VMEM((QB, length), F32)]),
        compiler_params=pltpu.CompilerParams(vmem_limit_bytes=VMEM_LIMIT),
        name="attend",
    )(off, q, k, v, windows, segq, segk)


def attend_back_kernel(scale, off, q, k, v, window, segq, segk, o, lse, do, dq, dk, dv, dtable, strip, ds, pb, acc):
    near = k.shape[0]
    length = window.shape[-1]
    strip[...] = strip_of(window[0], length)
    acc[...] = jnp.zeros_like(acc)
    base = near + QB - off[0]

    def block(b):
        rows = pl.ds(pl.multiple_of(b * QB, QB), QB)
        s, start = score_block(q[rows], k[...], strip, base, b, near, segq[rows], segk[...], scale)
        p = jnp.exp(s - lse[0, rows, 0:1])
        delta = jnp.sum(do[rows].astype(F32) * o[rows], axis=-1, keepdims=True)
        d = (p * (dot(do[rows], v[...], NT) - delta)).astype(BF16)
        pb[rows] = p.astype(BF16)
        ds[rows] = d
        dq[rows] = (dot(d, k[...]) * scale).astype(BF16)
        acc[:, pl.ds(start, near)] += d.astype(F32)
    loop(q.shape[0] // QB, block)
    dims = (((0,), (0,)), ((), ()))
    dk[...] = (dot(ds[...], q[...], dims) * scale).astype(BF16)
    dv[...] = dot(pb[...], do[...], dims).astype(BF16)
    rows, size = acc[...], QB
    while size > 1:
        size //= 2
        rows = rows[:size] + pltpu.roll(rows[size:], length - size, 1)
    dtable[0] = rows


def attend_back(q, k, v, windows, segq, segk, off, o, lse, do):
    count, near, length = q.shape[0], k.shape[0], windows.shape[-1]
    return pl.pallas_call(
        functools.partial(attend_back_kernel, 1.0 / math.sqrt(128)),
        out_shape=[shape(count, 1024, dtype=BF16), shape(near, 1024, dtype=BF16), shape(near, 1024, dtype=BF16), shape(HEADS, 1, length)],
        grid_spec=pltpu.PrefetchScalarGridSpec(
            num_scalar_prefetch=1, grid=(HEADS,),
            in_specs=[head_block(count), head_block(near), head_block(near), pl.BlockSpec((1, 1, length), lambda h, off: (h, 0, 0)),
                      pl.BlockSpec((count, 1), lambda h, off: (0, 0)), pl.BlockSpec((1, near), lambda h, off: (0, 0)),
                      head_block(count), pl.BlockSpec((1, count, 128), lambda h, off: (h, 0, 0)), head_block(count)],
            out_specs=[head_block(count), head_block(near), head_block(near), pl.BlockSpec((1, 1, length), lambda h, off: (h, 0, 0))],
            scratch_shapes=[pltpu.VMEM((QB, length), F32), pltpu.VMEM((count, near), BF16), pltpu.VMEM((count, near), BF16), pltpu.VMEM((QB, length), F32)]),
        compiler_params=pltpu.CompilerParams(vmem_limit_bytes=VMEM_LIMIT),
        name="attend_back",
    )(off, q, k, v, windows, segq, segk, o, lse, do)


ROWS = 128


BLOCKS_C = ((ATT, "in", 0), (GLU, "in", 0), (GLU, "in", 1))


def convolve_kernel(x1, o, params, seg, full, x2, c1, c2, u, y, sums, wbuf, a, half, send, recv, wsem, esem, ssem, rsem):
    w = Weights(full, wbuf, wsem, BLOCKS_C)
    w.start()
    count = x1.shape[0]
    u[0:8] = jnp.zeros((8, 1024), F32)
    u[count + 8:count + 16] = jnp.zeros((8, 1024), F32)
    greet(cube_peers() + edge_peers())

    def cast(rows):
        a[rows] = o[rows].astype(BF16)
    by_rows(count, 256, cast)
    w.wait(0)

    def project(c):
        x2[:, c] = x1[:, c] + dot(a[...], wbuf[0, :, c]) + params[SHIFT + 9:SHIFT + 10, c]
    by_cols(1024, project)

    def norm(rows):
        vhat, _ = normalized(x2[rows])
        a[rows] = (vhat * params[GAIN + 2:GAIN + 3] + params[SHIFT + 2:SHIFT + 3]).astype(BF16)
    by_rows(count, 256, norm)
    w.wait(1, 2)

    def gate(c):
        value = dot(a[...], wbuf[1, :, c]) + params[SHIFT + 10:SHIFT + 11, c]
        other = dot(a[...], wbuf[2, :, c]) + params[SHIFT + 11:SHIFT + 12, c]
        c1[:, c] = value
        c2[:, c] = other
        u[8:count + 8, c] = (value * sigmoid(other)).astype(BF16).astype(F32)
    by_cols(1024, gate)
    swap_edges(u, count, esem)
    half[...] = jnp.zeros_like(half)

    def taps(i):
        first = pl.multiple_of(i * ROWS, ROWS)
        here = seg[pl.ds(first + 8, ROWS)]
        total = jnp.zeros((ROWS, 1024), F32)
        block = u[pl.ds(first, ROWS + 16)]
        segs = seg[pl.ds(first, ROWS + 16)]
        for tap in range(KSIZE):
            k = slice(6 + tap, 6 + tap + ROWS)
            total = total + params[TAPS + tap:TAPS + tap + 1] * jnp.where(segs[k] == here, block[k], 0.0)
        y[pl.ds(first, ROWS)] = total
        half[0:8] += eight(total)
        half[8:16] += eight(total * total)
    loop(count // ROWS, taps)
    fold(half, send)
    steps = add_all(send, recv, ssem, rsem)
    sums[...] = send[steps]


def fold(half, send):
    send[0, 0:1] = jnp.sum(half[0:8], axis=0, keepdims=True)
    send[0, 1:2] = jnp.sum(half[8:16], axis=0, keepdims=True)


def reduce_scratch(rows=2):
    steps = (lax.axis_size("rows").bit_length() - 1) + (lax.axis_size("tm").bit_length() - 1)
    return [pltpu.VMEM((steps + 1, rows, 1024), F32), pltpu.VMEM((steps, rows, 1024), F32)], [pltpu.SemaphoreType.DMA((steps,)), pltpu.SemaphoreType.DMA((steps,))]


def convolve(x1, o, params, seg, full, cid):
    count = x1.shape[0]
    bufs, sems = reduce_scratch()
    return pl.pallas_call(
        convolve_kernel,
        out_shape=[shape(count, 1024), shape(count, 1024), shape(count, 1024), shape(count + 16, 1024), shape(count, 1024), shape(2, 1024)],
        in_specs=[whole()] * 4 + [anywhere()], out_specs=[whole()] * 6,
        scratch_shapes=[pltpu.VMEM((3, 1024, 1024), BF16), pltpu.VMEM((count, 1024), BF16), pltpu.VMEM((16, 1024), F32)] + bufs + [pltpu.SemaphoreType.DMA((3,)), pltpu.SemaphoreType.DMA((4,))] + sems,
        compiler_params=pltpu.CompilerParams(vmem_limit_bytes=VMEM_LIMIT, collective_id=cid, has_side_effects=True),
        name="convolve",
    )(x1, o, params, seg, full)


def batch_stats(sums, frames):
    mean = sums[0:1] / frames
    square = sums[1:2] / frames
    return mean, lax.rsqrt(square - mean * mean + EPS)


BLOCKS_D = tuple([(CONV, "in", 0)] + [(FI2, "in", j) for j in range(4)] + [(FO2, "out", j) for j in range(4)])


def middle_kernel(frames, x2, y, sums, cot, params, full, out, g3, dn, totals, small, grads, grads_b,
                  wbuf, a, e, d, dz, h, z, stage, half, send, recv, wsem, gsem, ssem, rsem):
    w = Weights(full, wbuf, wsem, BLOCKS_D)
    w.start()
    greet(cube_peers())
    g = Grads(grads, stage, gsem)
    count = x2.shape[0]
    mean, inverse = batch_stats(sums, frames)
    small[...] = jnp.zeros_like(small)
    half[...] = jnp.zeros_like(half)

    def active(rows):
        n = (y[rows] - mean) * inverse * params[GAIN + 5:GAIN + 6] + params[SHIFT + 5:SHIFT + 6]
        e[rows] = (n * sigmoid(n)).astype(BF16)
    by_rows(count, 256, active)
    w.wait(0)
    x3 = g3

    def project(c):
        x3[:, c] = x2[:, c] + dot(e[...], wbuf[0, :, c]) + params[SHIFT + 12:SHIFT + 13, c]
    by_cols(1024, project)

    def norm(rows):
        vhat, _ = normalized(x3[rows])
        a[rows] = (vhat * params[GAIN + 3:GAIN + 4] + params[SHIFT + 3:SHIFT + 4]).astype(BF16)
    by_rows(count, 256, norm)
    for j in range(4):
        w.wait(1 + j)

    def hidden(j):
        def cols(c):
            v = dot(a[...], wbuf[1 + j, :, c]) + params[pl.ds(BIAS + 4 + j, 1), c]
            z[j, :, c] = v
            h[j, :, c] = (v * sigmoid(v)).astype(BF16)
        by_cols(1024, cols)
    loop(4, hidden)
    w.wait(5, 6, 7, 8)

    def outward(c):
        acc = dot(h[0], wbuf[5, :, c])
        for j in range(1, 4):
            acc = acc + dot(h[j], wbuf[5 + j, :, c])
        out[:, c] = x3[:, c] + 0.5 * (acc + params[SHIFT + 13:SHIFT + 14, c])
    by_cols(1024, outward)

    def last(rows):
        vhat, rs = normalized(out[rows])
        gain = params[GAIN + 4:GAIN + 5]
        out[rows] = vhat * gain + params[SHIFT + 4:SHIFT + 5]
        ct = cot[rows]
        small[0:8] += eight(ct * vhat)
        small[8:16] += eight(ct)
        g4 = norm_back(ct, gain, vhat, rs)
        dn[rows] = g4
        half = (0.5 * g4).astype(BF16)
        d[rows] = half
        small[16:24] += eight(half.astype(F32))
    by_rows(count, 256, last)

    def back(j):
        def cols(c):
            v = z[j, :, c]
            s = sigmoid(v)
            dh = dot(d[...], wbuf[5 + j, c, :], NT) * (s * (1.0 + v * (1.0 - s)))
            dh = dh.astype(BF16)
            dz[j, :, c] = dh
            small[pl.ds(pl.multiple_of(24 + 8 * j, 8), 8), c] += eight(dh.astype(F32))
        by_cols(1024, cols)
    loop(4, back)
    for j in range(4):
        g.put(0, "out", j, h[j], lambda c: d[:, c], grads_b)
    for j in range(4):
        g.put(FI2, "in", j, a[...], lambda c, j=j: dz[j, :, c])
    da = z.at[0]

    def inward(c):
        acc = dot(dz[0], wbuf[1, c, :], NT)
        for j in range(1, 4):
            acc = acc + dot(dz[j], wbuf[1 + j, c, :], NT)
        da[:, c] = acc
    by_cols(1024, inward)

    def resid(rows):
        vhat, rs = normalized(x3[rows])
        w3 = da[rows]
        small[56:64] += eight(w3 * vhat)
        small[64:72] += eight(w3)
        total = dn[rows] + norm_back(w3, params[GAIN + 3:GAIN + 4], vhat, rs)
        g3[rows] = total
        de = total.astype(BF16)
        d[rows] = de
        small[72:80] += eight(de.astype(F32))
    by_rows(count, 256, resid)
    g.put(CONV, "in", 0, e[...], lambda c: d[:, c])

    def dnorm(c):
        dn[:, c] = dot(d[...], wbuf[0, c, :], NT)
    by_cols(1024, dnorm)

    def finish(rows):
        yhat = (y[rows] - mean) * inverse
        n = yhat * params[GAIN + 5:GAIN + 6] + params[SHIFT + 5:SHIFT + 6]
        s = sigmoid(n)
        v = dn[rows] * (s * (1.0 + n * (1.0 - s)))
        dn[rows] = v
        half[0:8] += eight(v * yhat)
        half[8:16] += eight(v)
    by_rows(count, 256, finish)
    small[80:96] = half[...]
    fold(half, send)
    steps = add_all(send, recv, ssem, rsem)
    totals[...] = send[steps]
    g.finish()


def middle(x2, y, sums, cot, params, full, frames, cid):
    count = x2.shape[0]
    bufs, sems = reduce_scratch()
    return pl.pallas_call(
        functools.partial(middle_kernel, frames),
        out_shape=[shape(count, 1024), shape(count, 1024), shape(count, 1024), shape(2, 1024), shape(96, 1024), shape(full.shape[0] // 2, 2, FO2 * 1024 // full.shape[0], 1024, dtype=BF16), shape(full.shape[0] // 2, 2, 4096 // full.shape[0], 1024, dtype=BF16)],
        in_specs=[whole()] * 5 + [anywhere()], out_specs=[whole()] * 5 + [anywhere()] * 2,
        scratch_shapes=[pltpu.VMEM((9, 1024, 1024), BF16), pltpu.VMEM((count, 1024), BF16), pltpu.VMEM((count, 1024), BF16), pltpu.VMEM((count, 1024), BF16),
                        pltpu.VMEM((4, count, 1024), BF16), pltpu.VMEM((4, count, 1024), BF16), pltpu.VMEM((4, count, 1024), F32),
                        pltpu.VMEM((2, 1024, 1024), BF16), pltpu.VMEM((16, 1024), F32)] + bufs + [pltpu.SemaphoreType.DMA((9,)), pltpu.SemaphoreType.DMA((2,))] + sems,
        compiler_params=pltpu.CompilerParams(vmem_limit_bytes=VMEM_LIMIT, collective_id=cid, has_side_effects=True),
        name="middle",
    )(x2, y, sums, cot, params, full)


def convolve_back_kernel(frames, dn, y, sums, totals, c1, c2, u, x2, g3, o, params, seg, full, grads_in, g2, dob, small, grads,
                         wbuf, a, d, dc, pad, stage, wsem, gsem, esem):
    w = Weights(full, wbuf, wsem, BLOCKS_C)
    w.start()
    count = x2.shape[0]
    pad[0:8] = jnp.zeros((8, 1024), F32)
    pad[count + 8:count + 16] = jnp.zeros((8, 1024), F32)
    greet(edge_peers())
    g = Grads(grads, stage, gsem)
    mean, inverse = batch_stats(sums, frames)
    gain = params[GAIN + 5:GAIN + 6]
    product = totals[0:1] * gain / frames
    total = totals[1:2] * gain / frames
    small[...] = jnp.zeros_like(small)

    def dy(i):
        rows = pl.ds(pl.multiple_of(i * ROWS, ROWS), ROWS)
        yhat = (y[rows] - mean) * inverse
        v = inverse * (dn[rows] * gain - total - yhat * product)
        pad[pl.ds(pl.multiple_of(i * ROWS + 8, 8), ROWS)] = v.astype(BF16).astype(F32)
        vhat, _ = normalized(x2[rows])
        a[rows] = (vhat * params[GAIN + 2:GAIN + 3] + params[SHIFT + 2:SHIFT + 3]).astype(BF16)
    loop(count // ROWS, dy)
    swap_edges(pad, count, esem)

    def taps(i):
        first = pl.multiple_of(i * ROWS, ROWS)
        rows = pl.ds(first, ROWS)
        block, grad, segs = u[pl.ds(first, ROWS + 16)], pad[pl.ds(first, ROWS + 16)], seg[pl.ds(first, ROWS + 16)]
        here, own = segs[8:ROWS + 8], grad[8:ROWS + 8]
        du = jnp.zeros((ROWS, 1024), F32)
        for tap in range(KSIZE):
            k = slice(6 + tap, 6 + tap + ROWS)
            small[8 * tap:8 * tap + 8] += eight(own * jnp.where(segs[k] == here, block[k], 0.0))
            b = slice(10 - tap, 10 - tap + ROWS)
            du = du + params[TAPS + tap:TAPS + tap + 1] * jnp.where(segs[b] == here, grad[b], 0.0)
        s = sigmoid(c2[rows])
        left = (du * s).astype(BF16)
        right = (du * c1[rows] * s * (1.0 - s)).astype(BF16)
        dc[0, rows] = left
        dc[1, rows] = right
        small[40:48] += eight(left.astype(F32))
        small[48:56] += eight(right.astype(F32))
    loop(count // ROWS, taps)
    w.wait(0, 1, 2)
    da = pad.at[0:count]

    def inward(c):
        da[:, c] = dot(dc[0], wbuf[1, c, :], NT) + dot(dc[1], wbuf[2, c, :], NT)
    by_cols(1024, inward)

    def resid(rows):
        vhat, rs = normalized(x2[rows])
        v = da[rows]
        small[56:64] += eight(v * vhat)
        small[64:72] += eight(v)
        both = g3[rows] + norm_back(v, params[GAIN + 2:GAIN + 3], vhat, rs)
        g2[rows] = both
        dx = both.astype(BF16)
        d[rows] = dx
        small[72:80] += eight(dx.astype(F32))
    by_rows(count, 256, resid)

    def attended(c):
        dob[:, c] = dot(d[...], wbuf[0, c, :], NT).astype(BF16)
    by_cols(1024, attended)
    for j in range(2):
        g.put(GLU, "in", j, a[...], lambda c, j=j: dc[j, :, c])

    def cast(rows):
        a[rows] = o[rows].astype(BF16)
    by_rows(count, 256, cast)
    g.put(ATT, "in", 0, a[...], lambda c: d[:, c])
    g.finish()


def convolve_back(dn, y, sums, totals, c1, c2, u, x2, g3, o, params, seg, full, grads, frames, cid):
    count = x2.shape[0]
    return pl.pallas_call(
        functools.partial(convolve_back_kernel, frames),
        out_shape=[shape(count, 1024), shape(count, 1024, dtype=BF16), shape(80, 1024), shape(*grads.shape, dtype=BF16)],
        in_specs=[whole()] * 12 + [anywhere()] * 2, out_specs=[whole()] * 3 + [anywhere()],
        scratch_shapes=[pltpu.VMEM((3, 1024, 1024), BF16), pltpu.VMEM((count, 1024), BF16), pltpu.VMEM((count, 1024), BF16), pltpu.VMEM((2, count, 1024), BF16),
                        pltpu.VMEM((count + 16, 1024), F32), pltpu.VMEM((2, 1024, 1024), BF16),
                        pltpu.SemaphoreType.DMA((3,)), pltpu.SemaphoreType.DMA((2,)), pltpu.SemaphoreType.DMA((4,))],
        input_output_aliases={13: 3},
        compiler_params=pltpu.CompilerParams(vmem_limit_bytes=VMEM_LIMIT, collective_id=cid, has_side_effects=True),
        name="convolve_back",
    )(dn, y, sums, totals, c1, c2, u, x2, g3, o, params, seg, full, grads)


BLOCKS_E = tuple([(QKV, "in", j) for j in range(3)])
BLOCKS_F = tuple([(FO1, "out", j) for j in range(4)] + [(FI1, "in", j) for j in range(4)])


def rear_kernel(halo, x1, g2, dq, dk, dv, params, full, *refs):
    if halo:
        beside, grads_in, g1, small, grads, wbuf, a, stage, da, back, got, wsem, gsem, esem = refs
    else:
        grads_in, g1, small, grads, wbuf, a, stage, da, wsem, gsem = refs
    w = Weights(full, wbuf, wsem, BLOCKS_E)
    w.start()
    g = Grads(grads, stage, gsem)
    count = x1.shape[0]
    small[...] = jnp.zeros_like(small)
    own = 0
    if halo:
        r, t = lax.axis_index("rows"), lax.axis_index("tm")
        greet([(r, 1 - t)])
        own, other = pl.multiple_of(t * HALO, 128), pl.multiple_of((1 - t) * count, 128)
        w.wait(1, 2)

        def outside(c):
            back[:, c] = (dot(dk[pl.ds(other, HALO)], wbuf[1, c, :], NT) + dot(dv[pl.ds(other, HALO)], wbuf[2, c, :], NT)).astype(BF16)
        by_cols(1024, outside)
        remote(back, got, esem.at[0], esem.at[1], r, 1 - t)
        w.wait(0)
    else:
        w.wait(0, 1, 2)
    mine = pl.ds(own, count)

    def inside(c):
        da[:, c] = dot(dq[...], wbuf[0, c, :], NT) + dot(dk[mine], wbuf[1, c, :], NT) + dot(dv[mine], wbuf[2, c, :], NT)
    by_cols(1024, inside)

    def norm(rows):
        vhat, _ = normalized(x1[rows])
        a[rows] = (vhat * params[GAIN + 1:GAIN + 2] + params[SHIFT + 1:SHIFT + 2]).astype(BF16)
        small[0:8] += eight(dq[rows].astype(F32))
    by_rows(count, 256, norm)

    def values(rows):
        small[8:16] += eight(dv[rows].astype(F32))
    by_rows(dv.shape[0], 128, values)
    g.put(QKV, "in", 0, a[...], lambda c: dq[:, c])
    if halo:
        for j, grad in ((1, dk), (2, dv)):
            slot = g.count % 2
            buf, n, R = stage.at[slot], g.n, g.R
            if g.count >= 2:
                g.wait(slot)

            def cols(c, grad=grad, buf=buf):
                buf[:, c] = (dot(a[...], grad[mine, c], TN) + dot(beside[...], grad[pl.ds(other, HALO), c], TN)).astype(BF16)
            by_cols(1024, cols)
            for s in range(R):
                pltpu.make_async_copy(buf.at[s * n:(s + 1) * n], grads.at[s // 2, s % 2, (QKV + j) * n:(QKV + j + 1) * n], gsem.at[slot]).start()
            g.count += 1
        landed(back, esem.at[0])
        landed(got, esem.at[1])
        first = pl.multiple_of((1 - t) * (count - HALO), 128)

        def merge(i):
            rows = pl.ds(pl.multiple_of(first + i * 64, 64), 64)
            da[rows] += got[pl.ds(pl.multiple_of(i * 64, 64), 64)].astype(F32)
        loop(HALO // 64, merge)
    else:
        g.put(QKV, "in", 1, a[...], lambda c: dk[:, c])
        g.put(QKV, "in", 2, a[...], lambda c: dv[:, c])

    def resid(rows):
        vhat, rs = normalized(x1[rows])
        v = da[rows]
        small[16:24] += eight(v * vhat)
        small[24:32] += eight(v)
        g1[rows] = g2[rows] + norm_back(v, params[GAIN + 1:GAIN + 2], vhat, rs)
    by_rows(count, 256, resid)
    g.finish()


def rear(x1, g2, dq, dk, dv, params, full, beside, grads, cid):
    count = x1.shape[0]
    halo = beside is not None
    scratch = [pltpu.VMEM((3, 1024, 1024), BF16), pltpu.VMEM((count, 1024), BF16), pltpu.VMEM((2, 1024, 1024), BF16), pltpu.VMEM((count, 1024), F32)]
    if halo:
        scratch += [pltpu.VMEM((HALO, 1024), BF16), pltpu.VMEM((HALO, 1024), BF16)]
    scratch += [pltpu.SemaphoreType.DMA((3,)), pltpu.SemaphoreType.DMA((2,))]
    if halo:
        scratch.append(pltpu.SemaphoreType.DMA((2,)))
    specs = [whole()] * 6 + [anywhere()] + ([whole()] if halo else []) + [anywhere()]
    return pl.pallas_call(
        functools.partial(rear_kernel, halo),
        out_shape=[shape(count, 1024), shape(32, 1024), shape(*grads.shape, dtype=BF16)],
        in_specs=specs, out_specs=[whole(), whole(), anywhere()], scratch_shapes=scratch,
        input_output_aliases={len(specs) - 1: 2},
        compiler_params=pltpu.CompilerParams(vmem_limit_bytes=VMEM_LIMIT, **({"collective_id": cid, "has_side_effects": True} if halo else {})),
        name="rear",
    )(x1, g2, dq, dk, dv, params, full, *((beside,) if halo else ()), grads)


class Last:
    def __init__(self, full, params, tokens, g1, z1, dtok, small, grads, scratch):
        wbuf, self.a, self.d, self.dz, self.zbuf, self.hbuf, stage, self.da, wsem, self.zsem, gsem = scratch
        self.w = Weights(full, wbuf, wsem, BLOCKS_F[:4])
        self.w2 = Weights(full, wbuf, wsem, BLOCKS_F[4:])
        self.g = Grads(grads, stage, gsem)
        self.params, self.tokens, self.g1, self.z1, self.dtok, self.small = params, tokens, g1, z1, dtok, small

    @staticmethod
    def scratch(count):
        sem, vmem = pltpu.SemaphoreType.DMA, pltpu.VMEM
        return [vmem((4, 1024, 1024), BF16), vmem((count, 1024), BF16), vmem((count, 1024), BF16), vmem((4, count, 1024), BF16), vmem((2, count, 1024), F32),
                vmem((count, 1024), BF16), vmem((2, 1024, 1024), BF16), vmem((count, 1024), F32), sem((4,)), sem((2,)), sem((2,))]

    def z_copy(self, j):
        return pltpu.make_async_copy(self.z1.at[:, j * 1024:(j + 1) * 1024], self.zbuf.at[j % 2], self.zsem.at[j % 2])

    def start(self):
        self.w.start()
        self.z_copy(0).start()
        self.z_copy(1).start()

    def prepare(self):
        self.small[...] = jnp.zeros_like(self.small)

        def rows(rows):
            half = (0.5 * self.g1[rows]).astype(BF16)
            self.d[rows] = half
            self.small[0:8] += eight(half.astype(F32))
        by_rows(self.d.shape[0], 256, rows)
        norm_tokens(self.tokens, self.params, self.a)

    def hidden(self, j):
        self.w.wait(j)
        self.z_copy(j).wait()
        v = self.zbuf[j % 2]
        s = sigmoid(v)
        self.hbuf[...] = (v * s).astype(BF16)
        dh = (dot(self.d[...], self.w.buf[j], NT) * (s * (1.0 + v * (1.0 - s)))).astype(BF16)
        self.dz[j] = dh
        self.small[8 + 8 * j:16 + 8 * j] += eight(dh.astype(F32))
        self.w2.start(j)
        if j + 2 < 4:
            self.z_copy(j + 2).start()

    def outward(self, j):
        self.g.put(FO1, "out", j, self.hbuf[...], lambda c: self.d[:, c])

    def inward(self, j):
        self.g.put(FI1, "in", j, self.a[...], lambda c: self.dz[j, :, c])

    def through(self, j):
        self.w2.wait(j)
        part = dot(self.dz[j], self.w2.buf[j], NT)
        self.da[...] = part if j == 0 else self.da[...] + part

    def end(self):
        def rows(rows):
            vhat, rs = normalized(self.tokens[rows].astype(F32))
            v = self.da[rows]
            self.small[40:48] += eight(v * vhat)
            self.small[48:56] += eight(v)
            self.dtok[rows] = self.g1[rows] + norm_back(v, self.params[GAIN:GAIN + 1], vhat, rs)
        by_rows(self.d.shape[0], 256, rows)


def plain_last_kernel(tokens, g1, z1, params, full, grads_in, dtok, small, grads, *scratch):
    f = Last(full, params, tokens, g1, z1, dtok, small, grads, scratch)
    f.start()
    f.prepare()
    for j in range(4):
        f.hidden(j)
        f.outward(j)
    for j in range(4):
        f.inward(j)
    for j in range(4):
        f.through(j)
    f.end()
    f.g.finish()


def plain_last(tokens, g1, z1, params, full, grads):
    count = tokens.shape[0]
    return pl.pallas_call(
        plain_last_kernel,
        out_shape=[shape(count, 1024), shape(56, 1024), shape(*grads.shape, dtype=BF16)],
        in_specs=[whole(), whole(), anywhere(), whole(), anywhere(), anywhere()], out_specs=[whole(), whole(), anywhere()],
        scratch_shapes=Last.scratch(count), input_output_aliases={5: 2},
        compiler_params=pltpu.CompilerParams(vmem_limit_bytes=VMEM_LIMIT),
        name="last",
    )(tokens, g1, z1, params, full, grads)


def last_kernel(units, ready, first, tokens, g1, z1, params, full, rows_in, share, grads_in, dtok, out, rows_out, late_out, share_out, grads,
                small, lv, lout, sown, sv, sx, town, tv, tx, lsem, sload, ssend, srecv, sxsem, tsend, trecv, txsem, *scratch):
    r, t, c, y, z = place()
    R = lax.axis_size("rows")
    n = len(Last.scratch(tokens.shape[0]))
    f = Last(full, params, tokens, g1, z1, dtok, small, grads, scratch[:n])
    f.start()
    cs = pltpu.make_async_copy(rows_in, sown, sload.at[0])
    cs.start()
    lc = pltpu.make_async_copy(share, lv.at[0], lsem.at[0])
    lc.start()
    greet([(lax.rem(r + d, R), t) for d in range(1, R)] + [(r, 1 - t)])
    s = Scatter(grads, out, units, ready, first, scratch[n:])
    s.begin()
    cs.wait()
    spread(sown, sv, ssend, srecv)
    lc.wait()
    pieces = share.shape[0] // 16

    def piece(i):
        @pl.when((i >= 2) & (i < pieces + 2))
        def _():
            rows = pl.ds(pl.multiple_of((i - 2) * 16, 16), 16)
            remote(lv.at[0, rows], lv.at[1, rows], lsem.at[1], lsem.at[2], r, 1 - t)

    def late_rows():
        town[...] = jnp.zeros_like(town)
        sums = [jnp.sum(small[8 * i:8 * i + 8], axis=0, keepdims=True) for i in range(7)]
        for to in range(R):
            pair = slice(to // 2 * 128, to // 2 * 128 + 128)
            for row, which in ((0, 0), (1, 5), (2, 6)):
                town[to, row:row + 1] = sums[which][:, pair]
            for half in range(2):
                at = (to % 4) * 256 + half * 128
                town[to, 3 + half:4 + half] = sums[1 + to // 4][:, at:at + 128]
        spread(town, tv, tsend, trecv)

    work = {(0, 2): f.prepare, (5, 0): lambda: f.inward(0), (5, 2): lambda: f.inward(1), (6, 0): lambda: f.inward(2), (6, 2): lambda: f.inward(3), (7, 0): f.g.finish,
            (7, 1): lambda: f.through(0), (7, 3): lambda: f.through(1), (8, 1): lambda: f.through(2), (8, 3): lambda: f.through(3), (9, 1): f.end, (10, 1): late_rows}
    for j in range(4):
        work[1 + j, 0] = lambda j=j: f.hidden(j)
        work[1 + j, 2] = lambda j=j: f.outward(j)
    for step in range(11):
        piece(step)
        for quarter in range(4):
            s.part(step, quarter)
            if (step, quarter) in work:
                work[step, quarter]()

    def rest(step):
        piece(step)
        s.tick(step)
    loop(units + s.LAG, rest, 11)
    gathered(sown, sv, sx, sxsem, ssend, srecv)
    gathered(town, tv, tx, txsem, tsend, trecv)
    done = [pltpu.make_async_copy(sx.at[0], rows_out, sload.at[0]), pltpu.make_async_copy(tx.at[0], late_out, sload.at[1])]
    landed(lv.at[0], lsem.at[1])
    landed(lv.at[1], lsem.at[2])
    lout[...] = lv[0].astype(F32) + lv[1].astype(F32)
    done.append(pltpu.make_async_copy(lout, share_out, lsem.at[0]))
    for copy in done:
        copy.start()
    s.finish()
    for copy in done:
        copy.wait()


def last(tokens, g1, z1, params, full, rows, share, grads, cid):
    count, R = tokens.shape[0], full.shape[0]
    units, ready = FO2, FO2 - QKV
    sem, vmem = pltpu.SemaphoreType.DMA, pltpu.VMEM
    late = (8, 128)
    return pl.pallas_call(
        functools.partial(last_kernel, units, ready, QKV),
        out_shape=[shape(count, 1024), shape(units * UNIT, 1024), shape(*rows.shape[1:]), shape(*late), shape(*share.shape), shape(*grads.shape, dtype=BF16)],
        in_specs=[whole(), whole(), anywhere(), whole()] + [anywhere()] * 4, out_specs=[whole()] + [anywhere()] * 5,
        scratch_shapes=[vmem((56, 1024), F32), vmem((2,) + share.shape, BF16), vmem(share.shape, F32),
                        vmem(rows.shape, F32), vmem((R - 1,) + rows.shape[1:], F32), vmem((2,) + rows.shape[1:], F32),
                        vmem((R,) + late, F32), vmem((R - 1,) + late, F32), vmem((2,) + late, F32),
                        sem((3,)), sem((2,)), sem, sem, sem((2,)), sem, sem, sem((2,))] + Last.scratch(count) + Scatter.scratch(units),
        input_output_aliases={7: 5},
        compiler_params=pltpu.CompilerParams(vmem_limit_bytes=VMEM_LIMIT, collective_id=cid, has_side_effects=True),
        name="last",
    )(tokens, g1, z1, params, full, rows, share, grads)


def pack_rows(gains, shifts, ffn_bias, conv_kernel, rel_table):
    n = rel_table.shape[0]
    rows = jnp.concatenate([gains, shifts, ffn_bias.reshape(2 * 4, n), conv_kernel, rel_table[None]], axis=0).reshape(-1)
    return jnp.pad(rows, (0, 8 * 384 - rows.shape[0])).reshape(8, 384)


def slab_rows(gains, shifts, ffn_bias, conv_kernel, rel_table):
    rows = jnp.concatenate([gains, shifts, jnp.zeros((8, 64), BF16), conv_kernel, rel_table[None], jnp.zeros((6, 64), BF16)], axis=0)
    zero = jnp.zeros_like(rows)
    odd = lax.rem(lax.axis_index("rows"), 2) == 1
    wide = jnp.concatenate([jnp.where(odd, zero, rows), jnp.where(odd, rows, zero)], axis=1)
    return jnp.concatenate([wide, ffn_bias.reshape(4, 128), jnp.zeros((4, 128), BF16)], axis=0)


def wide_rows(smalls):
    R = smalls.shape[0]
    n = 1024 // R
    rows = smalls.reshape(R, -1)[:, : 34 * n].reshape(R, 34, n).astype(F32)
    flat = rows.transpose(1, 0, 2).reshape(34, 1024)
    bias = rows[:, 20:28].reshape(R, 2, 4 * n).transpose(1, 0, 2).reshape(8, 1024)
    return jnp.concatenate([flat[:20], bias, flat[28:], jnp.zeros((6, 1024), F32)], axis=0)


def slot_rows(rows, R):
    n = 1024 // R
    flat = rows.reshape(34, R, n).transpose(1, 0, 2)
    bias = rows[20:28].reshape(2, R, 4, n).transpose(1, 0, 2, 3).reshape(R, 8, n)
    flat = jnp.concatenate([flat[:, :20], bias, flat[:, 28:]], axis=1).reshape(R, 34 * n)
    return jnp.pad(flat, ((0, 0), (0, 8 * 384 - 34 * n))).reshape(R, 8, 384)


def split_rows(rows):
    return (rows[:6], rows[6:20], rows[20:28].reshape(2, -1), rows[28:33], rows[33])


def pack_weights(weights):
    blocks = []
    for w in weights:
        rows, cols = w.shape
        blocks.append(w.reshape(rows, cols // 1024, 1024).transpose(1, 0, 2).reshape(-1, 1024))
    return jnp.concatenate(blocks, axis=0)


def unpack_shard(shard, weights):
    out, row = [], 0
    for w in weights:
        n, cols = w.shape
        count = n * cols // 1024
        out.append(shard[row : row + count].reshape(cols // 1024, n, 1024).transpose(1, 0, 2).reshape(n, cols))
        row += count
    return tuple(out)


def body(tokens, cotangent, segment_ids, rel_bucket, ffn1_in, ffn1_out, qkv_weight, attn_out, glu_in, conv_out, ffn2_in, ffn2_out,
         gains, shifts, ffn_bias, conv_kernel, rel_table):
    packed_rows, count, width = tokens.shape
    R, T = lax.axis_size("rows"), lax.axis_size("tm")
    t = lax.axis_index("tm")
    links = R == 16 and T == 2 and count == 512
    frames = R * T * count * packed_rows
    weights = (ffn1_in, ffn1_out, qkv_weight, attn_out, glu_in, conv_out, ffn2_in, ffn2_out)
    seg_all = lax.all_gather(segment_ids, "tm", axis=1, tiled=True)[0]
    seg_far = jnp.pad(seg_all, (HALO, HALO), constant_values=-1)
    segx = lax.dynamic_slice_in_dim(seg_far, HALO + t * count - 8, count + 16)[:, None]
    segq = segment_ids.reshape(count, 1)
    if links:
        near, off = count + HALO, t * HALO
        segk = lax.dynamic_slice_in_dim(seg_all, t * (count - HALO), near)[None]
    else:
        near, off = T * count, t * count
        segk = seg_all[None]
    length = 2 * near + QB
    places = np.clip(np.arange(length) - (near + QB), -MAXD, MAXD) + MAXD
    before, after = int(np.argmax(places > 0)), int(np.argmax(places >= 2 * MAXD))
    buckets = jnp.concatenate([jnp.broadcast_to(rel_bucket[:1], (before,)), rel_bucket[1 : 2 * MAXD], jnp.broadcast_to(rel_bucket[2 * MAXD :], (length - after,))])
    hot = (buckets[None, :] == jnp.arange(NB, dtype=jnp.int32)[:, None]).astype(F32)
    off = off.astype(jnp.int32).reshape(1)
    tok = tokens.reshape(count, width)
    if links:
        full, params, x1, z1, q, k, v, beside, o, lse, windows = front(slab_rows(gains, shifts, ffn_bias, conv_kernel, rel_table), weights, tok, hot.astype(BF16), segq, segk, 0)
        windows = windows.reshape(HEADS, 1, length)
    else:
        full = lax.all_gather(pack_weights(weights), "rows", axis=0)
        params = wide_rows(lax.all_gather(pack_rows(gains, shifts, ffn_bias, conv_kernel, rel_table), "rows", axis=0))

        windows = jnp.dot(params[REL].reshape(HEADS, NB), hot, precision=HIGH).reshape(HEADS, 1, length)

    if not links:
        x1, z1, q, k, v = plain_front(tok, params, full)
        beside = None
        k = lax.all_gather(k, "tm", axis=0, tiled=True)
        v = lax.all_gather(v, "tm", axis=0, tiled=True)
        o, lse = attend(q, k, v, windows, segq, segk, off)
    x2, c1, c2, u, y, sums = convolve(x1, o, params, segx, full, 3)
    output, g3, dn, totals, small_d, grads, grads_b = middle(x2, y, sums, cotangent.reshape(count, width), params, full, frames, 4)
    share = lax.psum_scatter(grads_b.reshape(R, -1, 1024), "rows", scatter_dimension=0, tiled=False)
    g2, dob, small_c, grads = convolve_back(dn, y, sums, totals, c1, c2, u, x2, g3, o, params, segx, full, grads, frames, 5)
    dq, dk, dv, dtable = attend_back(q, k, v, windows, segq, segk, off, o, lse, dob)
    if not links:
        dk = lax.psum_scatter(dk, "tm", scatter_dimension=0, tiled=True)
        dv = lax.psum_scatter(dv, "tm", scatter_dimension=0, tiled=True)
    g1, small_e, grads = rear(x1, g2, dq, dk, dv, params, full, beside, grads, 6)

    rel = lax.dot_general(dtable.reshape(HEADS, length), hot, (((1,), (1,)), ((), ())), precision=HIGH).reshape(1, 1024)
    d = jnp.sum(small_d.reshape(12, 8, 1024), axis=1)
    c = jnp.sum(small_c.reshape(10, 8, 1024), axis=1)
    e = jnp.sum(small_e.reshape(4, 8, 1024), axis=1)
    if links:
        l = jnp.zeros((7, 1024), F32)
    else:
        dtok, small_l, grads = plain_last(tok, g1, z1, params, full, grads)
        l = jnp.sum(small_l.reshape(7, 8, 1024), axis=1)
    rows = jnp.concatenate([
        l[5:6], e[2:3], c[7:8], d[7:8], d[0:1], d[10:11],
        l[6:7], e[3:4], c[8:9], d[8:9], d[1:2], d[11:12], l[0:1], e[0:2], c[9:10], c[5:7], d[9:10], d[2:3],
        l[1:5], d[3:7], c[0:5], rel])
    slots = slot_rows(rows, R)
    if links:
        dtok, shard, small, late, share, _ = last(tok, g1, z1, params, full, slots, share, grads, 1)
    else:
        shard = lax.psum(lax.psum_scatter(grads.reshape(R, -1, 1024), "rows", scatter_dimension=0, tiled=False), "tm").astype(F32)
        small = lax.psum(lax.psum_scatter(slots, "rows", scatter_dimension=0, tiled=False), "tm")
        share = lax.psum(share, "tm").astype(F32)
    rows = small.reshape(-1)[: 34 * (1024 // R)].reshape(34, 1024 // R)
    if links:
        odd = lax.rem(lax.axis_index("rows"), 2) == 1
        mine = jnp.where(odd, late[0:3, 64:], late[0:3, :64])
        rows = jnp.concatenate([mine[1:2], rows[1:6], mine[2:3], rows[7:12], mine[0:1], rows[13:20], late[3:5].reshape(4, 64), rows[24:]])
    return (output.reshape(tokens.shape), dtok.reshape(tokens.shape)) + unpack_shard(shard, weights[:7]) + (share,) + split_rows(rows)


def solution(mesh):
    return jax.shard_map(
        body,
        mesh=mesh,
        in_specs=(
            P("rows", "tm", None),
            P("rows", "tm", None),
            P("rows", "tm"),
            P(),
            P("rows", None),
            P("rows", None),
            P("rows", None),
            P("rows", None),
            P("rows", None),
            P("rows", None),
            P("rows", None),
            P("rows", None),
            P(None, "rows"),
            P(None, "rows"),
            P(None, "rows"),
            P(None, "rows"),
            P("rows"),
        ),
        out_specs=(
            P("rows", "tm", None),
            P("rows", "tm", None),
            P("rows", None),
            P("rows", None),
            P("rows", None),
            P("rows", None),
            P("rows", None),
            P("rows", None),
            P("rows", None),
            P("rows", None),
            P(None, "rows"),
            P(None, "rows"),
            P(None, "rows"),
            P(None, "rows"),
            P("rows"),
        ),
        check_vma=False,
    )
```

```python
import functools
import math

import jax
import jax.numpy as jnp
import numpy as np
from jax import lax
from jax.experimental import pallas as pl
from jax.experimental.pallas import tpu as pltpu
from jax.sharding import PartitionSpec as P

HEADS = 8
KSIZE = 5
NB = 128
MAXD = 256


EPS = 1e-05
NEG = -1e30
HIGH = lax.Precision.HIGHEST


MESH = pl.DeviceIdType.MESH
ANY = pl.ANY


def place():
    r = lax.axis_index("rows")
    t = lax.axis_index("tm")
    return r, t, lax.rem(r, 2), lax.rem(r // 2, 2), r // 4


def remote(src, dst, send, recv, rows, tm):
    pltpu.make_async_remote_copy(
        src_ref=src, dst_ref=dst, send_sem=send, recv_sem=recv,
        device_id=(rows, tm), device_id_type=MESH,
    ).start()


def landed(ref, sem):
    pltpu.make_async_copy(ref, ref, sem).wait()


def greet(peers):
    barrier = pltpu.get_barrier_semaphore()
    for rows, tm in peers:
        pl.semaphore_signal(barrier, inc=1, device_id=(rows, tm), device_id_type=MESH)
    pl.semaphore_wait(barrier, len(peers))


def link_peers():
    r, t, c, y, z = place()
    return [(r + 1 - 2 * c, t), (r + 2 - 4 * y, t), (lax.rem(r + 4, 16), t), (lax.rem(r + 12, 16), t), (r, 1 - t)]


def loop(n, fn, first=0):
    def one(i, carry):
        fn(i)
        return carry
    lax.fori_loop(first, n, one, 0)


UNIT = 64
EDGE = 24
MIDDLE = UNIT - 2 * EDGE
PLANE = EDGE + MIDDLE


class Gather:
    LEAD = 3
    EVENTS = (("from_z", 1, 0), ("from_y", 0, 0), ("from_z", 2, 1), ("from_y", 1, 1), ("from_x", 0, 1), ("from_z", 3, 2),
              ("from_y", 2, 2), ("from_x", 1, 2), ("from_y", 3, 3), ("from_x", 2, 3), ("from_x", 3, 4))
    LAG = 4

    def __init__(self, full, first, units, sems):
        self.full, self.first, self.units = full, first, units
        self.zr, self.yr, self.xr, self.cr, self.snd = sems
        self.r, self.t, self.c, self.y, self.z = place()
        self.taken = set()

    @staticmethod
    def scratch(units):
        sem = pltpu.SemaphoreType.DMA
        return [sem((units, 4)), sem((units, 4)), sem((units, 8)), sem((units,)), sem((5,))]

    def slot(self, z, y):
        return z * 4 + y * 2 + self.c

    def rows_of(self, unit, start, size):
        return pl.ds(pl.multiple_of((unit + self.first) * UNIT + start, 8), size)

    def inplane(self, slot, unit):
        return self.full.at[slot, self.rows_of(unit, self.t * EDGE, PLANE)]

    def edge(self, slot, unit, tm):
        return self.full.at[slot, self.rows_of(unit, tm * PLANE, EDGE)]

    def to_core(self, ref, unit):
        remote(ref, ref, self.snd.at[4], self.cr.at[unit], self.r + 1 - 2 * self.c, self.t)

    def send_own(self, unit):
        r, t, z = self.r, self.t, self.z
        plane = self.inplane(r, unit)

        @pl.when(z < 3)
        def _():
            remote(plane, plane, self.snd.at[0], self.zr.at[unit, z], r + 4, t)

        @pl.when(z > 0)
        def _():
            remote(plane, plane, self.snd.at[1], self.zr.at[unit, z], r - 4, t)

        remote(plane, plane, self.snd.at[2], self.yr.at[unit, z], self.slot(z, 1 - self.y), t)
        self.to_core(self.full.at[r, self.rows_of(unit, 0, UNIT)], unit)

    def pass_on(self, unit, z, y):
        s = self.slot(z, y)
        part = self.edge(s, unit, self.t)
        remote(part, part, self.snd.at[3], self.xr.at[unit, z * 2 + y], self.r, 1 - self.t)
        self.to_core(self.inplane(s, unit), unit)

    def from_z(self, unit, distance):
        for sign in (-1, 1):
            z = self.z + sign * distance

            @pl.when((z >= 0) & (z <= 3))
            def _(z=z, sign=sign):
                plane = self.inplane(self.slot(z, self.y), unit)
                landed(plane, self.zr.at[unit, z])
                onward = self.z - sign

                @pl.when((onward >= 0) & (onward <= 3))
                def _():
                    remote(plane, plane, self.snd.at[0 if sign < 0 else 1], self.zr.at[unit, z], self.slot(onward, self.y), self.t)

                remote(plane, plane, self.snd.at[2], self.yr.at[unit, z], self.slot(self.z, 1 - self.y), self.t)
                self.pass_on(unit, z, self.y)

    def from_y(self, unit, distance):
        for sign in (-1, 1) if distance else (1,):
            z = self.z + sign * distance

            @pl.when((z >= 0) & (z <= 3))
            def _(z=z):
                landed(self.inplane(self.slot(z, 1 - self.y), unit), self.yr.at[unit, z])
                self.pass_on(unit, z, 1 - self.y)

    def from_x(self, unit, distance):
        for other in (False, True) if distance else (True,):
            y = 1 - self.y if other else self.y
            for sign in (-1, 1) if distance else (1,):
                z = self.z + sign * distance

                @pl.when((z >= 0) & (z <= 3))
                def _(z=z, y=y):
                    part = self.edge(self.slot(z, y), unit, 1 - self.t)
                    landed(part, self.xr.at[unit, z * 2 + y])
                    self.to_core(part, unit)

    def begin(self):
        for unit in range(min(self.LEAD, self.units)):
            self.send_own(unit)

    def part(self, step, quarter):
        bounds = (0, 3, 6, 9, len(self.EVENTS))
        for name, distance, lag in self.EVENTS[bounds[quarter]:bounds[quarter + 1]]:
            unit = step - lag

            @pl.when((unit >= 0) & (unit < self.units))
            def _(name=name, distance=distance, unit=unit):
                getattr(self, name)(unit, distance)
        if quarter == 3:
            unit = step + self.LEAD

            @pl.when(unit < self.units)
            def _():
                self.send_own(unit)

    def tick(self, step):
        for quarter in range(4):
            self.part(step, quarter)

    def run(self, first, last):
        loop(last, self.tick, first)

    def arrived(self, unit):
        self.taken.add(unit)
        landed(self.full.at[0:8, self.rows_of(unit, 0, UNIT)], self.cr.at[unit])

    def finish(self):
        full, units, z = self.full, self.units, self.z
        for unit in range(units):
            if unit not in self.taken:
                self.arrived(unit)
        plane = units * PLANE
        for k in range(4):
            @pl.when(z == k)
            def _(k=k):
                if k < 3:
                    landed(full.at[0:k + 1, 0:plane], self.snd.at[0])
                if k > 0:
                    landed(full.at[0:4 - k, 0:plane], self.snd.at[1])
        landed(full.at[0:4, 0:plane], self.snd.at[2])
        landed(full.at[0:7, 0:units * EDGE], self.snd.at[3])
        landed(full.at[0:8, 0:units * UNIT], self.snd.at[4])


S_EDGE = 16
S_MIDDLE = UNIT - 2 * S_EDGE
S_PLANE = S_EDGE + S_MIDDLE


class Scatter:
    LEAD = 3
    RING = 10
    EVENTS = (("sum_core", 0, ()), ("sum_x", 1, ()), ("sum_y", 2, ()), ("hop", 3, (1,)), ("hop", 4, (2,)), ("hop", 5, (3,)), ("exchange", 5, ()), ("conclude", 6, ()))
    LAG = 6

    def __init__(self, grads, out, units, ready, first, scratch):
        self.grads, self.out, self.units, self.ready, self.first = grads, out, units, ready, first
        (self.own, self.obuf, self.cv, self.xv, self.yv, self.zv, self.fv,
         self.load, self.storing, self.cr, self.xr, self.yr, self.zr, self.fr, self.core, self.snd, self.free) = scratch
        self.r, self.t, self.c, self.y, self.z = place()

    @classmethod
    def scratch(cls, units):
        sem, vmem, n, bf = pltpu.SemaphoreType.DMA, pltpu.VMEM, cls.RING, jnp.bfloat16
        return [vmem((2, 8, UNIT, 1024), bf), vmem((2, UNIT, 1024), jnp.float32), vmem((n, 8, UNIT, 1024), bf), vmem((n, 8, S_EDGE, 1024), bf),
                vmem((n, 4, S_PLANE, 1024), bf), vmem((n, 5, S_PLANE, 1024), bf), vmem((n, S_PLANE, 1024), bf),
                sem((2,)), sem((2,)), sem((units,)), sem((units,)), sem((units, 4)), sem((units, 5)), sem((units,)), sem, sem((cls.RING, 5)), pltpu.SemaphoreType.REGULAR((5,))]

    def ring(self, unit):
        return lax.rem(unit, self.RING)

    def number(self, unit):
        late = self.units - self.ready
        after = unit - self.ready
        late_unit = after + late // 2 - jnp.where(after >= late // 2, late, 0)
        return jnp.where(unit < self.ready, unit + self.first, late_unit)

    def rows_of(self, unit):
        return pl.ds(pl.multiple_of(self.number(unit) * UNIT, UNIT), UNIT)

    def mine(self):
        return pl.ds(pl.multiple_of(self.t * S_EDGE, 16), S_PLANE)

    def edge(self, tm):
        return pl.ds(pl.multiple_of(tm * S_PLANE, 16), S_EDGE)

    def granted(self, unit, kind):
        @pl.when(unit >= self.RING)
        def _():
            pl.semaphore_wait(self.free.at[kind], 1)

    def own_copy(self, unit):
        return pltpu.make_async_copy(self.grads.at[:, self.c, self.rows_of(unit)], self.own.at[lax.rem(unit, 2)], self.load.at[lax.rem(unit, 2)])

    def send_core(self, unit):
        self.granted(unit, 0)
        remote(self.grads.at[:, 1 - self.c, self.rows_of(unit)], self.cv.at[self.ring(unit)], self.core, self.cr.at[unit], self.r + 1 - 2 * self.c, self.t)

    def add(self, a, b, n):
        def one(i):
            a[i] = (a[i].astype(jnp.float32) + b[i].astype(jnp.float32)).astype(jnp.bfloat16)
        loop(n, one)

    def sum_core(self, unit):
        at = self.ring(unit)
        cv = self.cv.at[at]
        landed(cv, self.cr.at[unit])
        self.own_copy(unit).wait()
        self.add(cv, self.own.at[lax.rem(unit, 2)], 8)

        @pl.when(unit + 2 < self.units)
        def _():
            self.own_copy(unit + 2).start()
        self.granted(unit, 1)
        remote(cv.at[:, self.edge(1 - self.t)], self.xv.at[at], self.snd.at[at, 0], self.xr.at[unit], self.r, 1 - self.t)

    def sum_x(self, unit):
        at = self.ring(unit)
        xv, cv = self.xv.at[at], self.cv.at[at]
        landed(xv, self.xr.at[unit])
        self.add(cv.at[:, self.edge(self.t)], xv, 8)
        self.granted(unit, 2)
        for k in range(4):
            remote(cv.at[k * 2 + 1 - self.y, self.mine()], self.yv.at[at, k], self.snd.at[at, 1], self.yr.at[unit, k], self.r + 2 - 4 * self.y, self.t)

    def at_z(self, unit, z):
        return self.cv.at[self.ring(unit), z * 2 + self.y, self.mine()]

    def send_z(self, unit, target, up):
        at, entry = self.at_z(unit, target), target + (1 if up else 0)
        remote(at, self.zv.at[self.ring(unit), entry], self.snd.at[self.ring(unit), 2 if up else 3], self.zr.at[unit, entry], self.r + (4 if up else -4), self.t)

    def take_z(self, unit, target, below):
        at, entry = self.at_z(unit, target), target + (1 if below else 0)
        zv = self.zv.at[self.ring(unit), entry]
        landed(zv, self.zr.at[unit, entry])
        at[...] = (at[...].astype(jnp.float32) + zv[...].astype(jnp.float32)).astype(jnp.bfloat16)

    def sum_y(self, unit):
        for k in range(4):
            yv = self.yv.at[self.ring(unit), k]
            landed(yv, self.yr.at[unit, k])
            at = self.at_z(unit, k)
            at[...] = (at[...].astype(jnp.float32) + yv[...].astype(jnp.float32)).astype(jnp.bfloat16)

        @pl.when(self.z == 0)
        def _():
            self.granted(unit, 3)
            for target in (3, 2, 1):
                self.send_z(unit, target, True)

        @pl.when(self.z == 3)
        def _():
            self.granted(unit, 4)
            for target in (0, 1, 2):
                self.send_z(unit, target, False)

    def hop(self, unit, number):
        for z in range(4):
            @pl.when(self.z == z)
            def _(z=z):
                if number == z:
                    if z < 3:
                        self.granted(unit, 3)
                    for target in range(3, z - 1, -1):
                        self.take_z(unit, target, True)
                        if target > z:
                            self.send_z(unit, target, True)
                if number == 3 - z:
                    if z > 0:
                        self.granted(unit, 4)
                    for target in range(0, z + 1):
                        self.take_z(unit, target, False)
                        if target < z:
                            self.send_z(unit, target, False)

    def exchange(self, unit):
        at = self.ring(unit)
        remote(self.at_z(unit, self.z), self.fv.at[at], self.snd.at[at, 4], self.fr.at[unit], self.r, 1 - self.t)

    def store(self, unit):
        number, slot, first = self.number(unit), lax.rem(unit, 2), 0
        for out in self.out:
            rows, cols = out.shape
            count = rows * cols // (UNIT * 1024)

            @pl.when((number >= first) & (number < first + count))
            def _(out=out, first=first, rows=rows):
                at = number - first
                if rows == UNIT:
                    dst = out.at[:, pl.ds(pl.multiple_of(at * 1024, 1024), 1024)]
                else:
                    dst = out.at[pl.ds(pl.multiple_of(at * UNIT, UNIT), UNIT)]
                pltpu.make_async_copy(self.obuf.at[slot], dst, self.storing.at[slot]).start()
            first += count

    def stored(self, unit):
        slot = lax.rem(unit, 2) if not isinstance(unit, int) else unit % 2
        landed(self.obuf.at[slot], self.storing.at[slot])

    def conclude(self, unit):
        at = self.ring(unit)
        fv, cv = self.fv.at[at], self.cv.at[at, self.z * 2 + self.y]
        landed(fv, self.fr.at[unit])

        @pl.when(unit >= 2)
        def _():
            self.stored(unit)
        obuf = self.obuf.at[lax.rem(unit, 2)]
        middle = pl.ds(S_EDGE, S_MIDDLE)
        obuf[middle] = cv[middle].astype(jnp.float32) + fv[pl.ds(pl.multiple_of(self.t * S_EDGE, 16), S_MIDDLE)].astype(jnp.float32)
        obuf[self.edge(self.t)] = cv[self.edge(self.t)].astype(jnp.float32)
        obuf[self.edge(1 - self.t)] = fv[pl.ds(pl.multiple_of((1 - self.t) * S_MIDDLE, 16), S_EDGE)].astype(jnp.float32)
        self.store(unit)
        landed(self.xv.at[at], self.snd.at[at, 0])
        landed(self.yv.at[at], self.snd.at[at, 1])
        for z in range(4):
            @pl.when(self.z == z)
            def _(z=z):
                if z < 3:
                    landed(self.zv.at[at, 0:3 - z], self.snd.at[at, 2])
                if z > 0:
                    landed(self.zv.at[at, 0:z], self.snd.at[at, 3])
        landed(fv, self.snd.at[at, 4])
        more = unit + self.RING < self.units

        def free(kind, rows, tm):
            pl.semaphore_signal(self.free.at[kind], inc=1, device_id=(rows, tm), device_id_type=MESH)

        @pl.when(more)
        def _():
            free(0, self.r + 1 - 2 * self.c, self.t)
            free(1, self.r, 1 - self.t)
            free(2, self.r + 2 - 4 * self.y, self.t)

        @pl.when(more & (self.z > 0))
        def _():
            free(3, self.r - 4, self.t)

        @pl.when(more & (self.z < 3))
        def _():
            free(4, self.r + 4, self.t)

    def begin(self):
        for unit in range(min(2, self.units)):
            self.own_copy(unit).start()
        for unit in range(min(self.LEAD, self.units)):
            self.send_core(unit)

    def part(self, step, quarter):
        for name, lag, args in self.EVENTS[2 * quarter:2 * quarter + 2]:
            unit = step - lag

            @pl.when((unit >= 0) & (unit < self.units))
            def _(name=name, unit=unit, args=args):
                getattr(self, name)(unit, *args)
        if quarter == 3:
            unit = step + self.LEAD

            @pl.when(unit < self.units)
            def _():
                self.send_core(unit)

    def tick(self, step):
        for quarter in range(4):
            self.part(step, quarter)

    def run(self, first, last):
        loop(last, self.tick, first)

    def finish(self):
        for unit in range(max(0, self.units - 2), self.units):
            self.stored(unit)
        landed(self.grads.at[:, 0, 0:self.units * UNIT], self.core)


def spread(slots, landing, send, recv):
    r, t, R = lax.axis_index("rows"), lax.axis_index("tm"), lax.axis_size("rows")
    for d in range(1, R):
        to = lax.rem(r + d, R)
        remote(slots.at[to], landing.at[R - 1 - d], send, recv, to, t)


def gathered(slots, landing, pair, sems, send, recv):
    r, t, R = lax.axis_index("rows"), lax.axis_index("tm"), lax.axis_size("rows")
    landed(slots.at[0:R - 1], send)
    landed(landing.at[0:R - 1], recv)
    total = slots[r]
    for d in range(R - 1):
        total = total + landing[d]
    pair[0] = total
    remote(pair.at[0], pair.at[1], sems.at[0], sems.at[1], r, 1 - t)
    landed(pair.at[0], sems.at[0])
    landed(pair.at[1], sems.at[1])
    pair[0] = pair[0] + pair[1]


HALO = 384
FI1, FO1, QKV, ATT, GLU, CONV, FI2, FO2, UNITS = 0, 4, 8, 11, 12, 14, 15, 19, 23
GAIN, SHIFT, BIAS, TAPS, REL = 0, 6, 20, 28, 33
F32, BF16 = jnp.float32, jnp.bfloat16
TILE = 1024
NN = (((1,), (0,)), ((), ()))
NT = (((1,), (1,)), ((), ()))
TN = (((0,), (0,)), ((), ()))
VMEM_LIMIT = 67043328


def dot(a, b, dims=NN):
    return lax.dot_general(a, b, dims, preferred_element_type=F32)


def by_rows(count, size, fn):
    loop(count // size, lambda i: fn(pl.ds(pl.multiple_of(i * size, size), size)))


def by_cols(count, fn):
    loop(count // TILE, lambda i: fn(pl.ds(pl.multiple_of(i * TILE, TILE), TILE)))


def normalized(v):
    centred = v - jnp.mean(v, axis=-1, keepdims=True)
    rs = lax.rsqrt(jnp.mean(centred * centred, axis=-1, keepdims=True) + EPS)
    return centred * rs, rs


def norm_back(w, gain, vhat, rs):
    wg = w * gain
    return rs * (wg - jnp.mean(wg, axis=-1, keepdims=True) - vhat * jnp.mean(wg * vhat, axis=-1, keepdims=True))


def eight(v):
    return jnp.sum(v.reshape(v.shape[0] // 8, 8, v.shape[1]), axis=0)


def sigmoid(v):
    return 1.0 / (1.0 + jnp.exp(-v))


class Weights:
    def __init__(self, full, buf, sems, blocks):
        self.full, self.buf, self.sems, self.blocks = full, buf, sems, blocks
        self.R = full.shape[0]
        self.n = 1024 // self.R

    def copies(self, k):
        unit, kind, index = self.blocks[k]
        n, R = self.n, self.R
        if kind == "in":
            return [(self.full.at[s, (unit + index) * n:(unit + index + 1) * n], self.buf.at[k, s * n:(s + 1) * n]) for s in range(R)]
        return [(self.full.at[index * (R // 4) + s, unit * n:(unit + 4) * n], self.buf.at[k, s * 4 * n:(s + 1) * 4 * n]) for s in range(R // 4)]

    def start(self, *ks):
        for k in ks or range(len(self.blocks)):
            for src, dst in self.copies(k):
                pltpu.make_async_copy(src, dst, self.sems.at[k]).start()

    def wait(self, *ks):
        for k in ks:
            pltpu.make_async_copy(self.buf.at[k], self.buf.at[k], self.sems.at[k]).wait()


class Grads:
    def __init__(self, out, buf, sems):
        self.out, self.buf, self.sems, self.count = out, buf, sems, 0
        self.R = 2 * out.shape[0]
        self.n = 1024 // self.R

    def put(self, unit, kind, index, left, right, out=None):
        out = self.out if out is None else out
        slot = self.count % 2
        buf, n, R = self.buf.at[slot], self.n, self.R
        if self.count >= 2:
            self.wait(slot)

        def cols(c):
            buf[:, c] = dot(left, right(c), TN).astype(BF16)
        by_cols(1024, cols)
        if kind == "in":
            pairs = [(buf.at[s * n:(s + 1) * n], out.at[s // 2, s % 2, (unit + index) * n:(unit + index + 1) * n]) for s in range(R)]
        else:
            pairs = [(buf.at[s * 4 * n:(s + 1) * 4 * n], out.at[(index * (R // 4) + s) // 2, (index * (R // 4) + s) % 2, unit * n:(unit + 4) * n]) for s in range(R // 4)]
        for src, dst in pairs:
            pltpu.make_async_copy(src, dst, self.sems.at[slot]).start()
        self.count += 1

    def wait(self, slot):
        pltpu.make_async_copy(self.buf.at[slot], self.buf.at[slot], self.sems.at[slot]).wait()

    def finish(self):
        for slot in range(min(2, self.count)):
            self.wait(slot)


def flipped(x, size):
    m = size
    return x + m - 2 * m * lax.rem(x // m, 2)


def cube_peers():
    r, t = lax.axis_index("rows"), lax.axis_index("tm")
    peers, m = [], 1
    while m < lax.axis_size("rows"):
        peers.append((flipped(r, m), t))
        m *= 2
    m = 1
    while m < lax.axis_size("tm"):
        peers.append((r, flipped(t, m)))
        m *= 2
    return peers


def add_all(send, recv, ssem, rsem):
    for i, (rows, tm) in enumerate(cube_peers()):
        remote(send.at[i], recv.at[i], ssem.at[i], rsem.at[i], rows, tm)
        landed(send.at[i], ssem.at[i])
        landed(recv.at[i], rsem.at[i])
        send[i + 1] = send[i] + recv[i]
    return len(cube_peers())


def edge_peers():
    r, t, T = lax.axis_index("rows"), lax.axis_index("tm"), lax.axis_size("tm")
    return [(r, lax.rem(t + 1, T)), (r, lax.rem(t + T - 1, T))]


def swap_edges(pad, count, sems):
    r, t, T = lax.axis_index("rows"), lax.axis_index("tm"), lax.axis_size("tm")

    @pl.when(t < T - 1)
    def _():
        remote(pad.at[count:count + 8], pad.at[0:8], sems.at[0], sems.at[1], r, t + 1)

    @pl.when(t > 0)
    def _():
        remote(pad.at[8:16], pad.at[count + 8:count + 16], sems.at[2], sems.at[3], r, t - 1)

    @pl.when(t < T - 1)
    def _():
        landed(pad.at[0:8], sems.at[0])
        landed(pad.at[0:8], sems.at[3])

    @pl.when(t > 0)
    def _():
        landed(pad.at[0:8], sems.at[2])
        landed(pad.at[0:8], sems.at[1])


def whole():
    return pl.BlockSpec(memory_space=pltpu.VMEM)


def anywhere():
    return pl.BlockSpec(memory_space=ANY)


def shape(*dims, dtype=F32):
    return jax.ShapeDtypeStruct(dims, dtype)


BLOCKS_A = tuple([(FI1, "in", j) for j in range(4)] + [(FO1, "out", j) for j in range(4)] + [(QKV, "in", j) for j in range(3)])


def norm_tokens(tokens, params, a):
    def norm(rows):
        vhat, _ = normalized(tokens[rows].astype(F32))
        a[rows] = (vhat * params[GAIN:GAIN + 1] + params[SHIFT:SHIFT + 1]).astype(BF16)
    by_rows(tokens.shape[0], 256, norm)


def norm_resid(x1, params, a):
    def norm(rows):
        vhat, _ = normalized(x1[rows])
        a[rows] = (vhat * params[GAIN + 1:GAIN + 2] + params[SHIFT + 1:SHIFT + 2]).astype(BF16)
    by_rows(x1.shape[0], 256, norm)


class Front:
    def __init__(self, w, params, tokens, x1, z1, a, h, zbuf, zsem):
        self.w, self.params, self.tokens, self.x1, self.z1, self.a, self.h, self.zbuf, self.zsem = w, params, tokens, x1, z1, a, h, zbuf, zsem

    def stored(self, slot):
        pltpu.make_async_copy(self.zbuf.at[slot], self.zbuf.at[slot], self.zsem.at[slot]).wait()

    def hidden(self, j):
        slot = j % 2
        self.w.wait(j)
        if j >= 2:
            self.stored(slot)
        z = dot(self.a[...], self.w.buf[j]) + self.params[BIAS + j:BIAS + j + 1]
        self.zbuf[slot] = z
        self.h[j] = (z * sigmoid(z)).astype(BF16)
        pltpu.make_async_copy(self.zbuf.at[slot], self.z1.at[:, j * 1024:(j + 1) * 1024], self.zsem.at[slot]).start()

    def project(self, j):
        self.w.wait(4 + j)
        part = dot(self.h[j], self.w.buf[4 + j])
        if j > 0:
            part = self.x1[...] + part
        if j == 3:
            part = self.tokens[...].astype(F32) + 0.5 * (part + self.params[SHIFT + 6:SHIFT + 7])
        self.x1[...] = part

    def mix(self, block, source, shift, out, rows):
        value = dot(source[...], self.w.buf[8 + block])
        if shift is not None:
            value = value + self.params[shift:shift + 1]
        out[rows] = value.astype(BF16)


def front_kernel(blocks, *refs):
    small, *refs = refs
    ws, refs = refs[:8], refs[8:]
    (tokens, hot, segq, segrow, full, params, x1, z1, q, k, v, beside, o, lse, windows, segk, own, slab, slabs, table, strip, wbuf, a, h, zbuf,
     load, keep, ssend, srecv, wsem, zsem, esem, idsem, *sems) = refs
    r, t, c, y, z = place()
    units, R, count = len(blocks), lax.axis_size("rows"), tokens.shape[0]
    copies = []
    for unit, (w, row, col) in enumerate(blocks):
        cp = pltpu.make_async_copy(ws[w].at[row:row + UNIT, col:col + 1024], own.at[unit * UNIT:(unit + 1) * UNIT], load.at[unit])
        cp.start()
        copies.append(cp)
    cs = pltpu.make_async_copy(small, slab, keep)
    cs.start()
    greet([(lax.rem(r + d, R), t) for d in range(1, R)] + [(r, 1 - t)])
    ids = segrow.at[:, pl.ds(pl.multiple_of((1 - t) * (count - HALO), 128), HALO)]
    remote(ids, segk.at[:, pl.ds(pl.multiple_of(t * count, 128), HALO)], idsem.at[0], idsem.at[1], r, 1 - t)
    cs.wait()
    for d in range(1, R):
        remote(slab, slabs.at[r], ssend, srecv, lax.rem(r + d, R), t)
    stored = []
    for unit, cp in enumerate(copies):
        cp.wait()
        put = pltpu.make_async_copy(own.at[unit * UNIT:(unit + 1) * UNIT], full.at[r, unit * UNIT:(unit + 1) * UNIT], load.at[unit])
        put.start()
        stored.append(put)
    for put in stored:
        put.wait()
    g = Gather(full, 0, units, sems)
    g.begin()

    def take_rows():
        landed(slabs.at[0:R - 1], ssend)
        landed(slabs.at[0:R - 1], srecv)
        slabs[r] = slab[...]
        for pair in range(R // 2):
            params[:, pair * 128:(pair + 1) * 128] = (slabs[2 * pair].astype(F32) + slabs[2 * pair + 1].astype(F32))[0:40]
        for s in range(R):
            rows = slabs[s].astype(F32)
            for b in range(2):
                for part in range(2):
                    at = 40 + 2 * b + part
                    params[BIAS + 4 * b + s // 4:BIAS + 4 * b + s // 4 + 1, (s % 4) * 256 + part * 128:(s % 4) * 256 + (part + 1) * 128] = rows[at:at + 1]

    w = Weights(full, wbuf, wsem, BLOCKS_A)
    f = Front(w, params, tokens, x1, z1, a, h, zbuf, zsem)
    mine, other = pl.ds(pl.multiple_of(t * HALO, 128), count), pl.ds(pl.multiple_of((1 - t) * count, 128), HALO)

    def exchange():
        norm_resid(x1, params, a)
        first = pl.multiple_of((1 - t) * (count - HALO), 128)
        remote(a.at[pl.ds(first, HALO)], beside, esem.at[0], esem.at[1], r, 1 - t)

    def receive():
        landed(beside, esem.at[0])
        landed(beside, esem.at[1])
        f.mix(1, beside, None, k, other)

    def bias_rows():
        landed(segrow.at[:, pl.ds(0, HALO)], idsem.at[0])
        landed(segk.at[:, pl.ds(pl.multiple_of((1 - t) * count, 128), HALO)], idsem.at[1])
        segk[:, pl.ds(pl.multiple_of(t * HALO, 128), count)] = segrow[...]
        for head in range(HEADS):
            table[head:head + 1] = params[REL:REL + 1, head * NB:(head + 1) * NB].astype(BF16)
        windows[...] = dot(table[...], hot[...])

    def head_rows(head, b):
        cols, rows = pl.ds(pl.multiple_of(head * 128, 128), 128), pl.ds(b * QB, QB)
        if b == 0:
            strip[...] = strip_of(windows[pl.ds(head, 1)], windows.shape[-1])
        base = k.shape[0] + QB - t * HALO
        attend_rows(q[rows, cols], k[:, cols], v[:, cols], strip, base, b, segq[rows], segk[...], o.at[rows, cols], lse.at[head, rows])

    work = {(2, 1): take_rows, (3, 1): lambda: norm_tokens(tokens, params, a), (4, 1): bias_rows, (5, 1): lambda: f.hidden(0), (6, 1): lambda: f.hidden(1), (7, 1): lambda: f.hidden(2), (8, 1): lambda: f.hidden(3),
            (12, 0): lambda: f.project(0), (12, 2): lambda: f.project(1), (13, 0): lambda: f.project(2), (13, 1): lambda: f.project(3), (13, 2): exchange,
            (14, 1): lambda: (w.wait(8), f.mix(0, a, SHIFT + 7, q, slice(None))), (14, 3): lambda: (w.wait(9), f.mix(1, a, None, k, mine)),
            (15, 1): lambda: (w.wait(10), f.mix(2, a, SHIFT + 8, v, mine)), (16, 1): receive, (17, 1): lambda: f.mix(2, beside, SHIFT + 8, v, other)}
    for step in range(18):
        for quarter in range(4):
            g.part(step, quarter)
            if (step, quarter) in work:
                work[step, quarter]()
        unit = step - g.LAG
        if 0 <= unit < 11:
            g.arrived(unit)
            if unit == 7:
                w.start(4, 5, 6, 7)
            elif unit < 4 or unit > 7:
                w.start(unit)

    def heads(step):
        for quarter in range(4):
            g.part(step, quarter)
            head_rows(step - 18, quarter)
    loop(18 + HEADS, heads, 18)
    g.run(18 + HEADS, units + g.LAG)
    g.finish()
    for slot in range(2):
        f.stored(slot)


def front(small, weights, tokens, hot, segq, segrow, cid):
    length = hot.shape[1]
    count, R, blocks = tokens.shape[0], lax.axis_size("rows"), []
    near = count + HALO
    for i, weight in enumerate(weights):
        n, cols = weight.shape
        blocks += [(i, row, col) for col in range(0, cols, 1024) for row in range(0, n, UNIT)]
    units, sem = len(blocks), pltpu.SemaphoreType.DMA
    return pl.pallas_call(
        functools.partial(front_kernel, tuple(blocks)),
        out_shape=[shape(R, units * UNIT, 1024, dtype=BF16), shape(40, 1024), shape(count, 1024), shape(count, 4096), shape(count, 1024, dtype=BF16),
                   shape(near, 1024, dtype=BF16), shape(near, 1024, dtype=BF16), shape(HALO, 1024, dtype=BF16),
                   shape(count, 1024), shape(HEADS, count, 128), shape(HEADS, length), shape(1, near, dtype=jnp.int32)],
        in_specs=[anywhere()] * 9 + [whole()] * 4, out_specs=[anywhere(), whole(), whole(), anywhere()] + [whole()] * 8,
        scratch_shapes=[pltpu.VMEM((units * UNIT, 1024), BF16), pltpu.VMEM(small.shape, BF16), pltpu.VMEM((R,) + small.shape, BF16), pltpu.VMEM((HEADS, NB), BF16), pltpu.VMEM((QB, length), F32),
                        pltpu.VMEM((11, 1024, 1024), BF16), pltpu.VMEM((count, 1024), BF16), pltpu.VMEM((4, count, 1024), BF16), pltpu.VMEM((2, count, 1024), F32),
                        sem((units,)), sem, sem, sem, sem((11,)), sem((2,)), sem((2,)), sem((2,))] + Gather.scratch(units),
        compiler_params=pltpu.CompilerParams(vmem_limit_bytes=VMEM_LIMIT, collective_id=cid, has_side_effects=True),
        name="front",
    )(small, *weights, tokens, hot, segq, segrow)


def plain_front_kernel(tokens, params, full, x1, z1, q, k, v, wbuf, a, h, zbuf, wsem, zsem):
    w = Weights(full, wbuf, wsem, BLOCKS_A)
    w.start()
    f = Front(w, params, tokens, x1, z1, a, h, zbuf, zsem)
    norm_tokens(tokens, params, a)
    for j in range(4):
        f.hidden(j)
    for j in range(4):
        f.project(j)
    norm_resid(x1, params, a)
    w.wait(8, 9, 10)
    f.mix(0, a, SHIFT + 7, q, slice(None))
    f.mix(1, a, None, k, slice(None))
    f.mix(2, a, SHIFT + 8, v, slice(None))
    for slot in range(2):
        f.stored(slot)


def plain_front(tokens, params, full):
    count = tokens.shape[0]
    return pl.pallas_call(
        plain_front_kernel,
        out_shape=[shape(count, 1024), shape(count, 4096)] + [shape(count, 1024, dtype=BF16)] * 3,
        in_specs=[whole(), whole(), anywhere()], out_specs=[whole(), anywhere(), whole(), whole(), whole()],
        scratch_shapes=[pltpu.VMEM((11, 1024, 1024), BF16), pltpu.VMEM((count, 1024), BF16), pltpu.VMEM((4, count, 1024), BF16), pltpu.VMEM((2, count, 1024), F32),
                        pltpu.SemaphoreType.DMA((11,)), pltpu.SemaphoreType.DMA((2,))],
        compiler_params=pltpu.CompilerParams(vmem_limit_bytes=VMEM_LIMIT),
        name="front",
    )(tokens, params, full)


QB = 128


def strip_of(window, length):
    return pltpu.roll(jnp.broadcast_to(window, (QB, length)), 0, 1, stride=1, stride_axis=0)


def score_block(q, k, strip, base, b, near, segq, segk, scale):
    start = pl.multiple_of(base - b * QB, 128)
    s = dot(q, k, NT) * scale + strip[:, pl.ds(start, near)]
    return jnp.where(segq == segk, s, NEG), start


SCALE = 1.0 / math.sqrt(128)


def attend_rows(q, k, v, strip, base, b, segq, segk, o, lse):
    s, _ = score_block(q, k, strip, base, b, k.shape[0], segq, segk, SCALE)
    top = jnp.max(s, axis=-1, keepdims=True)
    p = jnp.exp(s - top)
    total = jnp.sum(p, axis=-1, keepdims=True)
    o[...] = dot(p.astype(BF16), v) / total
    lse[...] = jnp.broadcast_to(top + jnp.log(total), (QB, 128))


def attend_kernel(off, q, k, v, window, segq, segk, o, lse, strip):
    near = k.shape[0]
    strip[...] = strip_of(window[0], window.shape[-1])
    base = near + QB - off[0]

    def block(b):
        rows = pl.ds(pl.multiple_of(b * QB, QB), QB)
        attend_rows(q[rows], k[...], v[...], strip, base, b, segq[rows], segk[...], o.at[rows], lse.at[0, rows])
    loop(q.shape[0] // QB, block)


def head_block(n):
    return pl.BlockSpec((n, 128), lambda h, off: (0, h))


def attend(q, k, v, windows, segq, segk, off):
    count, near, length = q.shape[0], k.shape[0], windows.shape[-1]
    return pl.pallas_call(
        attend_kernel,
        out_shape=[shape(count, 1024), shape(HEADS, count, 128)],
        grid_spec=pltpu.PrefetchScalarGridSpec(
            num_scalar_prefetch=1, grid=(HEADS,),
            in_specs=[head_block(count), head_block(near), head_block(near), pl.BlockSpec((1, 1, length), lambda h, off: (h, 0, 0)),
                      pl.BlockSpec((count, 1), lambda h, off: (0, 0)), pl.BlockSpec((1, near), lambda h, off: (0, 0))],
            out_specs=[head_block(count), pl.BlockSpec((1, count, 128), lambda h, off: (h, 0, 0))],
            scratch_shapes=[pltpu.VMEM((QB, length), F32)]),
        compiler_params=pltpu.CompilerParams(vmem_limit_bytes=VMEM_LIMIT),
        name="attend",
    )(off, q, k, v, windows, segq, segk)


def attend_back_kernel(scale, off, q, k, v, window, segq, segk, o, lse, do, dq, dk, dv, dtable, strip, ds, pb, acc):
    near = k.shape[0]
    length = window.shape[-1]
    strip[...] = strip_of(window[0], length)
    acc[...] = jnp.zeros_like(acc)
    base = near + QB - off[0]

    def block(b):
        rows = pl.ds(pl.multiple_of(b * QB, QB), QB)
        s, start = score_block(q[rows], k[...], strip, base, b, near, segq[rows], segk[...], scale)
        p = jnp.exp(s - lse[0, rows, 0:1])
        delta = jnp.sum(do[rows].astype(F32) * o[rows], axis=-1, keepdims=True)
        d = (p * (dot(do[rows], v[...], NT) - delta)).astype(BF16)
        pb[rows] = p.astype(BF16)
        ds[rows] = d
        dq[rows] = (dot(d, k[...]) * scale).astype(BF16)
        acc[:, pl.ds(start, near)] += d.astype(F32)
    loop(q.shape[0] // QB, block)
    dims = (((0,), (0,)), ((), ()))
    dk[...] = (dot(ds[...], q[...], dims) * scale).astype(BF16)
    dv[...] = dot(pb[...], do[...], dims).astype(BF16)
    rows, size = acc[...], QB
    while size > 1:
        size //= 2
        rows = rows[:size] + pltpu.roll(rows[size:], length - size, 1)
    dtable[0] = rows


def attend_back(q, k, v, windows, segq, segk, off, o, lse, do):
    count, near, length = q.shape[0], k.shape[0], windows.shape[-1]
    return pl.pallas_call(
        functools.partial(attend_back_kernel, 1.0 / math.sqrt(128)),
        out_shape=[shape(count, 1024, dtype=BF16), shape(near, 1024, dtype=BF16), shape(near, 1024, dtype=BF16), shape(HEADS, 1, length)],
        grid_spec=pltpu.PrefetchScalarGridSpec(
            num_scalar_prefetch=1, grid=(HEADS,),
            in_specs=[head_block(count), head_block(near), head_block(near), pl.BlockSpec((1, 1, length), lambda h, off: (h, 0, 0)),
                      pl.BlockSpec((count, 1), lambda h, off: (0, 0)), pl.BlockSpec((1, near), lambda h, off: (0, 0)),
                      head_block(count), pl.BlockSpec((1, count, 128), lambda h, off: (h, 0, 0)), head_block(count)],
            out_specs=[head_block(count), head_block(near), head_block(near), pl.BlockSpec((1, 1, length), lambda h, off: (h, 0, 0))],
            scratch_shapes=[pltpu.VMEM((QB, length), F32), pltpu.VMEM((count, near), BF16), pltpu.VMEM((count, near), BF16), pltpu.VMEM((QB, length), F32)]),
        compiler_params=pltpu.CompilerParams(vmem_limit_bytes=VMEM_LIMIT),
        name="attend_back",
    )(off, q, k, v, windows, segq, segk, o, lse, do)


ROWS = 128


BLOCKS_C = ((ATT, "in", 0), (GLU, "in", 0), (GLU, "in", 1))


def convolve_kernel(x1, o, params, seg, full, x2, c1, c2, u, y, sums, wbuf, a, half, send, recv, wsem, esem, ssem, rsem):
    w = Weights(full, wbuf, wsem, BLOCKS_C)
    w.start()
    count = x1.shape[0]
    u[0:8] = jnp.zeros((8, 1024), F32)
    u[count + 8:count + 16] = jnp.zeros((8, 1024), F32)
    greet(cube_peers() + edge_peers())

    def cast(rows):
        a[rows] = o[rows].astype(BF16)
    by_rows(count, 256, cast)
    w.wait(0)

    def project(c):
        x2[:, c] = x1[:, c] + dot(a[...], wbuf[0, :, c]) + params[SHIFT + 9:SHIFT + 10, c]
    by_cols(1024, project)

    def norm(rows):
        vhat, _ = normalized(x2[rows])
        a[rows] = (vhat * params[GAIN + 2:GAIN + 3] + params[SHIFT + 2:SHIFT + 3]).astype(BF16)
    by_rows(count, 256, norm)
    w.wait(1, 2)

    def gate(c):
        value = dot(a[...], wbuf[1, :, c]) + params[SHIFT + 10:SHIFT + 11, c]
        other = dot(a[...], wbuf[2, :, c]) + params[SHIFT + 11:SHIFT + 12, c]
        c1[:, c] = value
        c2[:, c] = other
        u[8:count + 8, c] = (value * sigmoid(other)).astype(BF16).astype(F32)
    by_cols(1024, gate)
    swap_edges(u, count, esem)
    half[...] = jnp.zeros_like(half)

    def taps(i):
        first = pl.multiple_of(i * ROWS, ROWS)
        here = seg[pl.ds(first + 8, ROWS)]
        total = jnp.zeros((ROWS, 1024), F32)
        block = u[pl.ds(first, ROWS + 16)]
        segs = seg[pl.ds(first, ROWS + 16)]
        for tap in range(KSIZE):
            k = slice(6 + tap, 6 + tap + ROWS)
            total = total + params[TAPS + tap:TAPS + tap + 1] * jnp.where(segs[k] == here, block[k], 0.0)
        y[pl.ds(first, ROWS)] = total
        half[0:8] += eight(total)
        half[8:16] += eight(total * total)
    loop(count // ROWS, taps)
    fold(half, send)
    steps = add_all(send, recv, ssem, rsem)
    sums[...] = send[steps]


def fold(half, send):
    send[0, 0:1] = jnp.sum(half[0:8], axis=0, keepdims=True)
    send[0, 1:2] = jnp.sum(half[8:16], axis=0, keepdims=True)


def reduce_scratch(rows=2):
    steps = (lax.axis_size("rows").bit_length() - 1) + (lax.axis_size("tm").bit_length() - 1)
    return [pltpu.VMEM((steps + 1, rows, 1024), F32), pltpu.VMEM((steps, rows, 1024), F32)], [pltpu.SemaphoreType.DMA((steps,)), pltpu.SemaphoreType.DMA((steps,))]


def convolve(x1, o, params, seg, full, cid):
    count = x1.shape[0]
    bufs, sems = reduce_scratch()
    return pl.pallas_call(
        convolve_kernel,
        out_shape=[shape(count, 1024), shape(count, 1024), shape(count, 1024), shape(count + 16, 1024), shape(count, 1024), shape(2, 1024)],
        in_specs=[whole()] * 4 + [anywhere()], out_specs=[whole()] * 6,
        scratch_shapes=[pltpu.VMEM((3, 1024, 1024), BF16), pltpu.VMEM((count, 1024), BF16), pltpu.VMEM((16, 1024), F32)] + bufs + [pltpu.SemaphoreType.DMA((3,)), pltpu.SemaphoreType.DMA((4,))] + sems,
        compiler_params=pltpu.CompilerParams(vmem_limit_bytes=VMEM_LIMIT, collective_id=cid, has_side_effects=True),
        name="convolve",
    )(x1, o, params, seg, full)


def batch_stats(sums, frames):
    mean = sums[0:1] / frames
    square = sums[1:2] / frames
    return mean, lax.rsqrt(square - mean * mean + EPS)


BLOCKS_D = tuple([(CONV, "in", 0)] + [(FI2, "in", j) for j in range(4)] + [(FO2, "out", j) for j in range(4)])


def middle_kernel(frames, x2, y, sums, cot, params, full, out, g3, dn, totals, small, grads, grads_b,
                  wbuf, a, e, d, dz, h, z, stage, half, send, recv, wsem, gsem, ssem, rsem):
    w = Weights(full, wbuf, wsem, BLOCKS_D)
    w.start()
    greet(cube_peers())
    g = Grads(grads, stage, gsem)
    count = x2.shape[0]
    mean, inverse = batch_stats(sums, frames)
    small[...] = jnp.zeros_like(small)
    half[...] = jnp.zeros_like(half)

    def active(rows):
        n = (y[rows] - mean) * inverse * params[GAIN + 5:GAIN + 6] + params[SHIFT + 5:SHIFT + 6]
        e[rows] = (n * sigmoid(n)).astype(BF16)
    by_rows(count, 256, active)
    w.wait(0)
    x3 = g3

    def project(c):
        x3[:, c] = x2[:, c] + dot(e[...], wbuf[0, :, c]) + params[SHIFT + 12:SHIFT + 13, c]
    by_cols(1024, project)

    def norm(rows):
        vhat, _ = normalized(x3[rows])
        a[rows] = (vhat * params[GAIN + 3:GAIN + 4] + params[SHIFT + 3:SHIFT + 4]).astype(BF16)
    by_rows(count, 256, norm)
    for j in range(4):
        w.wait(1 + j)

    def hidden(j):
        def cols(c):
            v = dot(a[...], wbuf[1 + j, :, c]) + params[pl.ds(BIAS + 4 + j, 1), c]
            z[j, :, c] = v
            h[j, :, c] = (v * sigmoid(v)).astype(BF16)
        by_cols(1024, cols)
    loop(4, hidden)
    w.wait(5, 6, 7, 8)

    def outward(c):
        acc = dot(h[0], wbuf[5, :, c])
        for j in range(1, 4):
            acc = acc + dot(h[j], wbuf[5 + j, :, c])
        out[:, c] = x3[:, c] + 0.5 * (acc + params[SHIFT + 13:SHIFT + 14, c])
    by_cols(1024, outward)

    def last(rows):
        vhat, rs = normalized(out[rows])
        gain = params[GAIN + 4:GAIN + 5]
        out[rows] = vhat * gain + params[SHIFT + 4:SHIFT + 5]
        ct = cot[rows]
        small[0:8] += eight(ct * vhat)
        small[8:16] += eight(ct)
        g4 = norm_back(ct, gain, vhat, rs)
        dn[rows] = g4
        half = (0.5 * g4).astype(BF16)
        d[rows] = half
        small[16:24] += eight(half.astype(F32))
    by_rows(count, 256, last)

    def back(j):
        def cols(c):
            v = z[j, :, c]
            s = sigmoid(v)
            dh = dot(d[...], wbuf[5 + j, c, :], NT) * (s * (1.0 + v * (1.0 - s)))
            dh = dh.astype(BF16)
            dz[j, :, c] = dh
            small[pl.ds(pl.multiple_of(24 + 8 * j, 8), 8), c] += eight(dh.astype(F32))
        by_cols(1024, cols)
    loop(4, back)
    for j in range(4):
        g.put(0, "out", j, h[j], lambda c: d[:, c], grads_b)
    for j in range(4):
        g.put(FI2, "in", j, a[...], lambda c, j=j: dz[j, :, c])
    da = z.at[0]

    def inward(c):
        acc = dot(dz[0], wbuf[1, c, :], NT)
        for j in range(1, 4):
            acc = acc + dot(dz[j], wbuf[1 + j, c, :], NT)
        da[:, c] = acc
    by_cols(1024, inward)

    def resid(rows):
        vhat, rs = normalized(x3[rows])
        w3 = da[rows]
        small[56:64] += eight(w3 * vhat)
        small[64:72] += eight(w3)
        total = dn[rows] + norm_back(w3, params[GAIN + 3:GAIN + 4], vhat, rs)
        g3[rows] = total
        de = total.astype(BF16)
        d[rows] = de
        small[72:80] += eight(de.astype(F32))
    by_rows(count, 256, resid)
    g.put(CONV, "in", 0, e[...], lambda c: d[:, c])

    def dnorm(c):
        dn[:, c] = dot(d[...], wbuf[0, c, :], NT)
    by_cols(1024, dnorm)

    def finish(rows):
        yhat = (y[rows] - mean) * inverse
        n = yhat * params[GAIN + 5:GAIN + 6] + params[SHIFT + 5:SHIFT + 6]
        s = sigmoid(n)
        v = dn[rows] * (s * (1.0 + n * (1.0 - s)))
        dn[rows] = v
        half[0:8] += eight(v * yhat)
        half[8:16] += eight(v)
    by_rows(count, 256, finish)
    small[80:96] = half[...]
    fold(half, send)
    steps = add_all(send, recv, ssem, rsem)
    totals[...] = send[steps]
    g.finish()


def middle(x2, y, sums, cot, params, full, frames, cid):
    count = x2.shape[0]
    bufs, sems = reduce_scratch()
    return pl.pallas_call(
        functools.partial(middle_kernel, frames),
        out_shape=[shape(count, 1024), shape(count, 1024), shape(count, 1024), shape(2, 1024), shape(96, 1024), shape(full.shape[0] // 2, 2, FO2 * 1024 // full.shape[0], 1024, dtype=BF16), shape(full.shape[0] // 2, 2, 4096 // full.shape[0], 1024, dtype=BF16)],
        in_specs=[whole()] * 5 + [anywhere()], out_specs=[whole()] * 5 + [anywhere()] * 2,
        scratch_shapes=[pltpu.VMEM((9, 1024, 1024), BF16), pltpu.VMEM((count, 1024), BF16), pltpu.VMEM((count, 1024), BF16), pltpu.VMEM((count, 1024), BF16),
                        pltpu.VMEM((4, count, 1024), BF16), pltpu.VMEM((4, count, 1024), BF16), pltpu.VMEM((4, count, 1024), F32),
                        pltpu.VMEM((2, 1024, 1024), BF16), pltpu.VMEM((16, 1024), F32)] + bufs + [pltpu.SemaphoreType.DMA((9,)), pltpu.SemaphoreType.DMA((2,))] + sems,
        compiler_params=pltpu.CompilerParams(vmem_limit_bytes=VMEM_LIMIT, collective_id=cid, has_side_effects=True),
        name="middle",
    )(x2, y, sums, cot, params, full)


def convolve_back_kernel(frames, dn, y, sums, totals, c1, c2, u, x2, g3, o, params, seg, full, grads_in, g2, dob, small, grads,
                         wbuf, a, d, dc, pad, stage, wsem, gsem, esem):
    w = Weights(full, wbuf, wsem, BLOCKS_C)
    w.start()
    count = x2.shape[0]
    pad[0:8] = jnp.zeros((8, 1024), F32)
    pad[count + 8:count + 16] = jnp.zeros((8, 1024), F32)
    greet(edge_peers())
    g = Grads(grads, stage, gsem)
    mean, inverse = batch_stats(sums, frames)
    gain = params[GAIN + 5:GAIN + 6]
    product = totals[0:1] * gain / frames
    total = totals[1:2] * gain / frames
    small[...] = jnp.zeros_like(small)

    def dy(i):
        rows = pl.ds(pl.multiple_of(i * ROWS, ROWS), ROWS)
        yhat = (y[rows] - mean) * inverse
        v = inverse * (dn[rows] * gain - total - yhat * product)
        pad[pl.ds(pl.multiple_of(i * ROWS + 8, 8), ROWS)] = v.astype(BF16).astype(F32)
        vhat, _ = normalized(x2[rows])
        a[rows] = (vhat * params[GAIN + 2:GAIN + 3] + params[SHIFT + 2:SHIFT + 3]).astype(BF16)
    loop(count // ROWS, dy)
    swap_edges(pad, count, esem)

    def taps(i):
        first = pl.multiple_of(i * ROWS, ROWS)
        rows = pl.ds(first, ROWS)
        block, grad, segs = u[pl.ds(first, ROWS + 16)], pad[pl.ds(first, ROWS + 16)], seg[pl.ds(first, ROWS + 16)]
        here, own = segs[8:ROWS + 8], grad[8:ROWS + 8]
        du = jnp.zeros((ROWS, 1024), F32)
        for tap in range(KSIZE):
            k = slice(6 + tap, 6 + tap + ROWS)
            small[8 * tap:8 * tap + 8] += eight(own * jnp.where(segs[k] == here, block[k], 0.0))
            b = slice(10 - tap, 10 - tap + ROWS)
            du = du + params[TAPS + tap:TAPS + tap + 1] * jnp.where(segs[b] == here, grad[b], 0.0)
        s = sigmoid(c2[rows])
        left = (du * s).astype(BF16)
        right = (du * c1[rows] * s * (1.0 - s)).astype(BF16)
        dc[0, rows] = left
        dc[1, rows] = right
        small[40:48] += eight(left.astype(F32))
        small[48:56] += eight(right.astype(F32))
    loop(count // ROWS, taps)
    w.wait(0, 1, 2)
    da = pad.at[0:count]

    def inward(c):
        da[:, c] = dot(dc[0], wbuf[1, c, :], NT) + dot(dc[1], wbuf[2, c, :], NT)
    by_cols(1024, inward)

    def resid(rows):
        vhat, rs = normalized(x2[rows])
        v = da[rows]
        small[56:64] += eight(v * vhat)
        small[64:72] += eight(v)
        both = g3[rows] + norm_back(v, params[GAIN + 2:GAIN + 3], vhat, rs)
        g2[rows] = both
        dx = both.astype(BF16)
        d[rows] = dx
        small[72:80] += eight(dx.astype(F32))
    by_rows(count, 256, resid)

    def attended(c):
        dob[:, c] = dot(d[...], wbuf[0, c, :], NT).astype(BF16)
    by_cols(1024, attended)
    for j in range(2):
        g.put(GLU, "in", j, a[...], lambda c, j=j: dc[j, :, c])

    def cast(rows):
        a[rows] = o[rows].astype(BF16)
    by_rows(count, 256, cast)
    g.put(ATT, "in", 0, a[...], lambda c: d[:, c])
    g.finish()


def convolve_back(dn, y, sums, totals, c1, c2, u, x2, g3, o, params, seg, full, grads, frames, cid):
    count = x2.shape[0]
    return pl.pallas_call(
        functools.partial(convolve_back_kernel, frames),
        out_shape=[shape(count, 1024), shape(count, 1024, dtype=BF16), shape(80, 1024), shape(*grads.shape, dtype=BF16)],
        in_specs=[whole()] * 12 + [anywhere()] * 2, out_specs=[whole()] * 3 + [anywhere()],
        scratch_shapes=[pltpu.VMEM((3, 1024, 1024), BF16), pltpu.VMEM((count, 1024), BF16), pltpu.VMEM((count, 1024), BF16), pltpu.VMEM((2, count, 1024), BF16),
                        pltpu.VMEM((count + 16, 1024), F32), pltpu.VMEM((2, 1024, 1024), BF16),
                        pltpu.SemaphoreType.DMA((3,)), pltpu.SemaphoreType.DMA((2,)), pltpu.SemaphoreType.DMA((4,))],
        input_output_aliases={13: 3},
        compiler_params=pltpu.CompilerParams(vmem_limit_bytes=VMEM_LIMIT, collective_id=cid, has_side_effects=True),
        name="convolve_back",
    )(dn, y, sums, totals, c1, c2, u, x2, g3, o, params, seg, full, grads)


BLOCKS_E = tuple([(QKV, "in", j) for j in range(3)])
BLOCKS_F = tuple([(FO1, "out", j) for j in range(4)] + [(FI1, "in", j) for j in range(4)])


def rear_kernel(halo, x1, g2, dq, dk, dv, params, full, *refs):
    if halo:
        beside, grads_in, g1, small, grads, wbuf, a, stage, da, back, got, wsem, gsem, esem = refs
    else:
        grads_in, g1, small, grads, wbuf, a, stage, da, wsem, gsem = refs
    w = Weights(full, wbuf, wsem, BLOCKS_E)
    w.start()
    g = Grads(grads, stage, gsem)
    count = x1.shape[0]
    small[...] = jnp.zeros_like(small)
    own = 0
    if halo:
        r, t = lax.axis_index("rows"), lax.axis_index("tm")
        greet([(r, 1 - t)])
        own, other = pl.multiple_of(t * HALO, 128), pl.multiple_of((1 - t) * count, 128)
        w.wait(1, 2)

        def outside(c):
            back[:, c] = (dot(dk[pl.ds(other, HALO)], wbuf[1, c, :], NT) + dot(dv[pl.ds(other, HALO)], wbuf[2, c, :], NT)).astype(BF16)
        by_cols(1024, outside)
        remote(back, got, esem.at[0], esem.at[1], r, 1 - t)
        w.wait(0)
    else:
        w.wait(0, 1, 2)
    mine = pl.ds(own, count)

    def inside(c):
        da[:, c] = dot(dq[...], wbuf[0, c, :], NT) + dot(dk[mine], wbuf[1, c, :], NT) + dot(dv[mine], wbuf[2, c, :], NT)
    by_cols(1024, inside)

    def norm(rows):
        vhat, _ = normalized(x1[rows])
        a[rows] = (vhat * params[GAIN + 1:GAIN + 2] + params[SHIFT + 1:SHIFT + 2]).astype(BF16)
        small[0:8] += eight(dq[rows].astype(F32))
    by_rows(count, 256, norm)

    def values(rows):
        small[8:16] += eight(dv[rows].astype(F32))
    by_rows(dv.shape[0], 128, values)
    g.put(QKV, "in", 0, a[...], lambda c: dq[:, c])
    if halo:
        for j, grad in ((1, dk), (2, dv)):
            slot = g.count % 2
            buf, n, R = stage.at[slot], g.n, g.R
            if g.count >= 2:
                g.wait(slot)

            def cols(c, grad=grad, buf=buf):
                buf[:, c] = (dot(a[...], grad[mine, c], TN) + dot(beside[...], grad[pl.ds(other, HALO), c], TN)).astype(BF16)
            by_cols(1024, cols)
            for s in range(R):
                pltpu.make_async_copy(buf.at[s * n:(s + 1) * n], grads.at[s // 2, s % 2, (QKV + j) * n:(QKV + j + 1) * n], gsem.at[slot]).start()
            g.count += 1
        landed(back, esem.at[0])
        landed(got, esem.at[1])
        first = pl.multiple_of((1 - t) * (count - HALO), 128)

        def merge(i):
            rows = pl.ds(pl.multiple_of(first + i * 64, 64), 64)
            da[rows] += got[pl.ds(pl.multiple_of(i * 64, 64), 64)].astype(F32)
        loop(HALO // 64, merge)
    else:
        g.put(QKV, "in", 1, a[...], lambda c: dk[:, c])
        g.put(QKV, "in", 2, a[...], lambda c: dv[:, c])

    def resid(rows):
        vhat, rs = normalized(x1[rows])
        v = da[rows]
        small[16:24] += eight(v * vhat)
        small[24:32] += eight(v)
        g1[rows] = g2[rows] + norm_back(v, params[GAIN + 1:GAIN + 2], vhat, rs)
    by_rows(count, 256, resid)
    g.finish()


def rear(x1, g2, dq, dk, dv, params, full, beside, grads, cid):
    count = x1.shape[0]
    halo = beside is not None
    scratch = [pltpu.VMEM((3, 1024, 1024), BF16), pltpu.VMEM((count, 1024), BF16), pltpu.VMEM((2, 1024, 1024), BF16), pltpu.VMEM((count, 1024), F32)]
    if halo:
        scratch += [pltpu.VMEM((HALO, 1024), BF16), pltpu.VMEM((HALO, 1024), BF16)]
    scratch += [pltpu.SemaphoreType.DMA((3,)), pltpu.SemaphoreType.DMA((2,))]
    if halo:
        scratch.append(pltpu.SemaphoreType.DMA((2,)))
    specs = [whole()] * 6 + [anywhere()] + ([whole()] if halo else []) + [anywhere()]
    return pl.pallas_call(
        functools.partial(rear_kernel, halo),
        out_shape=[shape(count, 1024), shape(32, 1024), shape(*grads.shape, dtype=BF16)],
        in_specs=specs, out_specs=[whole(), whole(), anywhere()], scratch_shapes=scratch,
        input_output_aliases={len(specs) - 1: 2},
        compiler_params=pltpu.CompilerParams(vmem_limit_bytes=VMEM_LIMIT, **({"collective_id": cid, "has_side_effects": True} if halo else {})),
        name="rear",
    )(x1, g2, dq, dk, dv, params, full, *((beside,) if halo else ()), grads)


class Last:
    def __init__(self, full, params, tokens, g1, z1, dtok, small, grads, scratch):
        wbuf, self.a, self.d, self.dz, self.zbuf, self.hbuf, stage, self.da, wsem, self.zsem, gsem = scratch
        self.w = Weights(full, wbuf, wsem, BLOCKS_F[:4])
        self.w2 = Weights(full, wbuf, wsem, BLOCKS_F[4:])
        self.g = Grads(grads, stage, gsem)
        self.params, self.tokens, self.g1, self.z1, self.dtok, self.small = params, tokens, g1, z1, dtok, small

    @staticmethod
    def scratch(count):
        sem, vmem = pltpu.SemaphoreType.DMA, pltpu.VMEM
        return [vmem((4, 1024, 1024), BF16), vmem((count, 1024), BF16), vmem((count, 1024), BF16), vmem((4, count, 1024), BF16), vmem((2, count, 1024), F32),
                vmem((count, 1024), BF16), vmem((2, 1024, 1024), BF16), vmem((count, 1024), F32), sem((4,)), sem((2,)), sem((2,))]

    def z_copy(self, j):
        return pltpu.make_async_copy(self.z1.at[:, j * 1024:(j + 1) * 1024], self.zbuf.at[j % 2], self.zsem.at[j % 2])

    def start(self):
        self.w.start()
        self.z_copy(0).start()
        self.z_copy(1).start()

    def prepare(self):
        self.small[...] = jnp.zeros_like(self.small)

        def rows(rows):
            half = (0.5 * self.g1[rows]).astype(BF16)
            self.d[rows] = half
            self.small[0:8] += eight(half.astype(F32))
        by_rows(self.d.shape[0], 256, rows)
        norm_tokens(self.tokens, self.params, self.a)

    def hidden(self, j):
        self.w.wait(j)
        self.z_copy(j).wait()
        v = self.zbuf[j % 2]
        s = sigmoid(v)
        self.hbuf[...] = (v * s).astype(BF16)
        dh = (dot(self.d[...], self.w.buf[j], NT) * (s * (1.0 + v * (1.0 - s)))).astype(BF16)
        self.dz[j] = dh
        self.small[8 + 8 * j:16 + 8 * j] += eight(dh.astype(F32))
        self.w2.start(j)
        if j + 2 < 4:
            self.z_copy(j + 2).start()

    def outward(self, j):
        self.g.put(FO1, "out", j, self.hbuf[...], lambda c: self.d[:, c])

    def inward(self, j):
        self.g.put(FI1, "in", j, self.a[...], lambda c: self.dz[j, :, c])

    def through(self, j):
        self.w2.wait(j)
        part = dot(self.dz[j], self.w2.buf[j], NT)
        self.da[...] = part if j == 0 else self.da[...] + part

    def end(self):
        def rows(rows):
            vhat, rs = normalized(self.tokens[rows].astype(F32))
            v = self.da[rows]
            self.small[40:48] += eight(v * vhat)
            self.small[48:56] += eight(v)
            self.dtok[rows] = self.g1[rows] + norm_back(v, self.params[GAIN:GAIN + 1], vhat, rs)
        by_rows(self.d.shape[0], 256, rows)


def plain_last_kernel(tokens, g1, z1, params, full, grads_in, dtok, small, grads, *scratch):
    f = Last(full, params, tokens, g1, z1, dtok, small, grads, scratch)
    f.start()
    f.prepare()
    for j in range(4):
        f.hidden(j)
        f.outward(j)
    for j in range(4):
        f.inward(j)
    for j in range(4):
        f.through(j)
    f.end()
    f.g.finish()


def plain_last(tokens, g1, z1, params, full, grads):
    count = tokens.shape[0]
    return pl.pallas_call(
        plain_last_kernel,
        out_shape=[shape(count, 1024), shape(56, 1024), shape(*grads.shape, dtype=BF16)],
        in_specs=[whole(), whole(), anywhere(), whole(), anywhere(), anywhere()], out_specs=[whole(), whole(), anywhere()],
        scratch_shapes=Last.scratch(count), input_output_aliases={5: 2},
        compiler_params=pltpu.CompilerParams(vmem_limit_bytes=VMEM_LIMIT),
        name="last",
    )(tokens, g1, z1, params, full, grads)


def last_kernel(units, ready, first, tokens, g1, z1, params, full, rows_in, share, grads_in, dtok, *refs):
    out, refs = refs[:7], refs[7:]
    (rows_out, late_out, share_out, grads,
     small, lv, lout, sown, sv, sx, town, tv, tx, lsem, sload, ssend, srecv, sxsem, tsend, trecv, txsem, *scratch) = refs
    r, t, c, y, z = place()
    R = lax.axis_size("rows")
    n = len(Last.scratch(tokens.shape[0]))
    f = Last(full, params, tokens, g1, z1, dtok, small, grads, scratch[:n])
    f.start()
    cs = pltpu.make_async_copy(rows_in, sown, sload.at[0])
    cs.start()
    lc = pltpu.make_async_copy(share, lv.at[0], lsem.at[0])
    lc.start()
    greet([(lax.rem(r + d, R), t) for d in range(1, R)] + [(r, 1 - t)])
    s = Scatter(grads, out, units, ready, first, scratch[n:])
    s.begin()
    cs.wait()
    spread(sown, sv, ssend, srecv)
    lc.wait()
    pieces = share.shape[0] // 16

    def piece(i):
        @pl.when((i >= 2) & (i < pieces + 2))
        def _():
            rows = pl.ds(pl.multiple_of((i - 2) * 16, 16), 16)
            remote(lv.at[0, rows], lv.at[1, rows], lsem.at[1], lsem.at[2], r, 1 - t)

    def late_rows():
        town[...] = jnp.zeros_like(town)
        sums = [jnp.sum(small[8 * i:8 * i + 8], axis=0, keepdims=True) for i in range(7)]
        for to in range(R):
            pair = slice(to // 2 * 128, to // 2 * 128 + 128)
            for row, which in ((0, 0), (1, 5), (2, 6)):
                town[to, row:row + 1] = sums[which][:, pair]
            for half in range(2):
                at = (to % 4) * 256 + half * 128
                town[to, 3 + half:4 + half] = sums[1 + to // 4][:, at:at + 128]
        spread(town, tv, tsend, trecv)

    work = {(0, 2): f.prepare, (5, 0): lambda: f.inward(0), (5, 2): lambda: f.inward(1), (6, 0): lambda: f.inward(2), (6, 2): lambda: f.inward(3), (7, 0): f.g.finish,
            (7, 1): lambda: f.through(0), (7, 3): lambda: f.through(1), (8, 1): lambda: f.through(2), (8, 3): lambda: f.through(3), (9, 1): f.end, (10, 1): late_rows}
    for j in range(4):
        work[1 + j, 0] = lambda j=j: f.hidden(j)
        work[1 + j, 2] = lambda j=j: f.outward(j)
    for step in range(11):
        piece(step)
        for quarter in range(4):
            s.part(step, quarter)
            if (step, quarter) in work:
                work[step, quarter]()

    def rest(step):
        piece(step)
        s.tick(step)
    loop(units + s.LAG, rest, 11)
    gathered(sown, sv, sx, sxsem, ssend, srecv)
    gathered(town, tv, tx, txsem, tsend, trecv)
    done = [pltpu.make_async_copy(sx.at[0], rows_out, sload.at[0]), pltpu.make_async_copy(tx.at[0], late_out, sload.at[1])]
    landed(lv.at[0], lsem.at[1])
    landed(lv.at[1], lsem.at[2])
    lout[...] = lv[0].astype(F32) + lv[1].astype(F32)
    done.append(pltpu.make_async_copy(lout, share_out, lsem.at[0]))
    for copy in done:
        copy.start()
    s.finish()
    for copy in done:
        copy.wait()


def last(tokens, g1, z1, params, full, rows, share, grads, shapes, cid):
    count, R = tokens.shape[0], full.shape[0]
    units, ready = FO2, FO2 - QKV
    sem, vmem = pltpu.SemaphoreType.DMA, pltpu.VMEM
    late = (8, 128)
    return pl.pallas_call(
        functools.partial(last_kernel, units, ready, QKV),
        out_shape=[shape(count, 1024)] + [shape(*dims) for dims in shapes] + [shape(*rows.shape[1:]), shape(*late), shape(*share.shape), shape(*grads.shape, dtype=BF16)],
        in_specs=[whole(), whole(), anywhere(), whole()] + [anywhere()] * 4, out_specs=[whole()] + [anywhere()] * 11,
        scratch_shapes=[vmem((56, 1024), F32), vmem((2,) + share.shape, BF16), vmem(share.shape, F32),
                        vmem(rows.shape, F32), vmem((R - 1,) + rows.shape[1:], F32), vmem((2,) + rows.shape[1:], F32),
                        vmem((R,) + late, F32), vmem((R - 1,) + late, F32), vmem((2,) + late, F32),
                        sem((3,)), sem((2,)), sem, sem, sem((2,)), sem, sem, sem((2,))] + Last.scratch(count) + Scatter.scratch(units),
        input_output_aliases={7: 11},
        compiler_params=pltpu.CompilerParams(vmem_limit_bytes=VMEM_LIMIT, collective_id=cid, has_side_effects=True),
        name="last",
    )(tokens, g1, z1, params, full, rows, share, grads)


def pack_rows(gains, shifts, ffn_bias, conv_kernel, rel_table):
    n = rel_table.shape[0]
    rows = jnp.concatenate([gains, shifts, ffn_bias.reshape(2 * 4, n), conv_kernel, rel_table[None]], axis=0).reshape(-1)
    return jnp.pad(rows, (0, 8 * 384 - rows.shape[0])).reshape(8, 384)


def slab_rows(gains, shifts, ffn_bias, conv_kernel, rel_table):
    rows = jnp.concatenate([gains, shifts, jnp.zeros((8, 64), BF16), conv_kernel, rel_table[None], jnp.zeros((6, 64), BF16)], axis=0)
    zero = jnp.zeros_like(rows)
    odd = lax.rem(lax.axis_index("rows"), 2) == 1
    wide = jnp.concatenate([jnp.where(odd, zero, rows), jnp.where(odd, rows, zero)], axis=1)
    return jnp.concatenate([wide, ffn_bias.reshape(4, 128), jnp.zeros((4, 128), BF16)], axis=0)


def wide_rows(smalls):
    R = smalls.shape[0]
    n = 1024 // R
    rows = smalls.reshape(R, -1)[:, : 34 * n].reshape(R, 34, n).astype(F32)
    flat = rows.transpose(1, 0, 2).reshape(34, 1024)
    bias = rows[:, 20:28].reshape(R, 2, 4 * n).transpose(1, 0, 2).reshape(8, 1024)
    return jnp.concatenate([flat[:20], bias, flat[28:], jnp.zeros((6, 1024), F32)], axis=0)


def slot_rows(rows, R):
    n = 1024 // R
    flat = rows.reshape(34, R, n).transpose(1, 0, 2)
    bias = rows[20:28].reshape(2, R, 4, n).transpose(1, 0, 2, 3).reshape(R, 8, n)
    flat = jnp.concatenate([flat[:, :20], bias, flat[:, 28:]], axis=1).reshape(R, 34 * n)
    return jnp.pad(flat, ((0, 0), (0, 8 * 384 - 34 * n))).reshape(R, 8, 384)


def split_rows(rows):
    return (rows[:6], rows[6:20], rows[20:28].reshape(2, -1), rows[28:33], rows[33])


def pack_weights(weights):
    blocks = []
    for w in weights:
        rows, cols = w.shape
        blocks.append(w.reshape(rows, cols // 1024, 1024).transpose(1, 0, 2).reshape(-1, 1024))
    return jnp.concatenate(blocks, axis=0)


def unpack_shard(shard, weights):
    out, row = [], 0
    for w in weights:
        n, cols = w.shape
        count = n * cols // 1024
        out.append(shard[row : row + count].reshape(cols // 1024, n, 1024).transpose(1, 0, 2).reshape(n, cols))
        row += count
    return tuple(out)


def body(tokens, cotangent, segment_ids, rel_bucket, ffn1_in, ffn1_out, qkv_weight, attn_out, glu_in, conv_out, ffn2_in, ffn2_out,
         gains, shifts, ffn_bias, conv_kernel, rel_table):
    packed_rows, count, width = tokens.shape
    R, T = lax.axis_size("rows"), lax.axis_size("tm")
    t = lax.axis_index("tm")
    links = R == 16 and T == 2 and count == 512
    frames = R * T * count * packed_rows
    weights = (ffn1_in, ffn1_out, qkv_weight, attn_out, glu_in, conv_out, ffn2_in, ffn2_out)
    segq = segment_ids.reshape(count, 1)
    if links:
        near, off = count + HALO, t * HALO
    else:
        near, off = T * count, t * count
        segk = lax.all_gather(segment_ids, "tm", axis=1, tiled=True)
    length = 2 * near + QB
    places = np.clip(np.arange(length) - (near + QB), -MAXD, MAXD) + MAXD
    before, after = int(np.argmax(places > 0)), int(np.argmax(places >= 2 * MAXD))
    buckets = jnp.concatenate([jnp.broadcast_to(rel_bucket[:1], (before,)), rel_bucket[1 : 2 * MAXD], jnp.broadcast_to(rel_bucket[2 * MAXD :], (length - after,))])
    hot = (buckets[None, :] == jnp.arange(NB, dtype=jnp.int32)[:, None]).astype(F32)
    off = off.astype(jnp.int32).reshape(1)
    tok = tokens.reshape(count, width)
    if links:
        full, params, x1, z1, q, k, v, beside, o, lse, windows, segk = front(slab_rows(gains, shifts, ffn_bias, conv_kernel, rel_table), weights, tok, hot.astype(BF16), segq, segment_ids, 0)
        windows = windows.reshape(HEADS, 1, length)
    else:
        full = lax.all_gather(pack_weights(weights), "rows", axis=0)
        params = wide_rows(lax.all_gather(pack_rows(gains, shifts, ffn_bias, conv_kernel, rel_table), "rows", axis=0))

        windows = jnp.dot(params[REL].reshape(HEADS, NB), hot, precision=HIGH).reshape(HEADS, 1, length)

    if not links:
        x1, z1, q, k, v = plain_front(tok, params, full)
        beside = None
        k = lax.all_gather(k, "tm", axis=0, tiled=True)
        v = lax.all_gather(v, "tm", axis=0, tiled=True)
        o, lse = attend(q, k, v, windows, segq, segk, off)
    segx = lax.dynamic_slice_in_dim(jnp.pad(segk[0], (8, 8), constant_values=-1), off[0], count + 16)[:, None]
    x2, c1, c2, u, y, sums = convolve(x1, o, params, segx, full, 3)
    output, g3, dn, totals, small_d, grads, grads_b = middle(x2, y, sums, cotangent.reshape(count, width), params, full, frames, 4)
    share = lax.psum_scatter(grads_b.reshape(R, -1, 1024), "rows", scatter_dimension=0, tiled=False)
    g2, dob, small_c, grads = convolve_back(dn, y, sums, totals, c1, c2, u, x2, g3, o, params, segx, full, grads, frames, 5)
    dq, dk, dv, dtable = attend_back(q, k, v, windows, segq, segk, off, o, lse, dob)
    if not links:
        dk = lax.psum_scatter(dk, "tm", scatter_dimension=0, tiled=True)
        dv = lax.psum_scatter(dv, "tm", scatter_dimension=0, tiled=True)
    g1, small_e, grads = rear(x1, g2, dq, dk, dv, params, full, beside, grads, 6)

    rel = lax.dot_general(dtable.reshape(HEADS, length), hot, (((1,), (1,)), ((), ())), precision=HIGH).reshape(1, 1024)
    d = jnp.sum(small_d.reshape(12, 8, 1024), axis=1)
    c = jnp.sum(small_c.reshape(10, 8, 1024), axis=1)
    e = jnp.sum(small_e.reshape(4, 8, 1024), axis=1)
    if links:
        l = jnp.zeros((7, 1024), F32)
    else:
        dtok, small_l, grads = plain_last(tok, g1, z1, params, full, grads)
        l = jnp.sum(small_l.reshape(7, 8, 1024), axis=1)
    rows = jnp.concatenate([
        l[5:6], e[2:3], c[7:8], d[7:8], d[0:1], d[10:11],
        l[6:7], e[3:4], c[8:9], d[8:9], d[1:2], d[11:12], l[0:1], e[0:2], c[9:10], c[5:7], d[9:10], d[2:3],
        l[1:5], d[3:7], c[0:5], rel])
    slots = slot_rows(rows, R)
    if links:
        dtok, *shards, small, late, share, _ = last(tok, g1, z1, params, full, slots, share, grads, [w.shape for w in weights[:7]], 1)
        shards = tuple(shards)
    else:
        shard = lax.psum(lax.psum_scatter(grads.reshape(R, -1, 1024), "rows", scatter_dimension=0, tiled=False), "tm").astype(F32)
        shards = unpack_shard(shard, weights[:7])
        small = lax.psum(lax.psum_scatter(slots, "rows", scatter_dimension=0, tiled=False), "tm")
        share = lax.psum(share, "tm").astype(F32)
    rows = small.reshape(-1)[: 34 * (1024 // R)].reshape(34, 1024 // R)
    if links:
        odd = lax.rem(lax.axis_index("rows"), 2) == 1
        mine = jnp.where(odd, late[0:3, 64:], late[0:3, :64])
        rows = jnp.concatenate([mine[1:2], rows[1:6], mine[2:3], rows[7:12], mine[0:1], rows[13:20], late[3:5].reshape(4, 64), rows[24:]])
    return (output.reshape(tokens.shape), dtok.reshape(tokens.shape)) + shards + (share,) + split_rows(rows)


def solution(mesh):
    return jax.shard_map(
        body,
        mesh=mesh,
        in_specs=(
            P("rows", "tm", None),
            P("rows", "tm", None),
            P("rows", "tm"),
            P(),
            P("rows", None),
            P("rows", None),
            P("rows", None),
            P("rows", None),
            P("rows", None),
            P("rows", None),
            P("rows", None),
            P("rows", None),
            P(None, "rows"),
            P(None, "rows"),
            P(None, "rows"),
            P(None, "rows"),
            P("rows"),
        ),
        out_specs=(
            P("rows", "tm", None),
            P("rows", "tm", None),
            P("rows", None),
            P("rows", None),
            P("rows", None),
            P("rows", None),
            P("rows", None),
            P("rows", None),
            P("rows", None),
            P("rows", None),
            P(None, "rows"),
            P(None, "rows"),
            P(None, "rows"),
            P(None, "rows"),
            P("rows"),
        ),
        check_vma=False,
    )
```

```python
import functools
import math

import jax
import jax.numpy as jnp
import numpy as np
from jax import lax
from jax.experimental import pallas as pl
from jax.experimental.pallas import tpu as pltpu
from jax.sharding import PartitionSpec as P

HEADS = 8
KSIZE = 5
NB = 128
MAXD = 256


EPS = 1e-05
NEG = -1e30
HIGH = lax.Precision.HIGHEST


MESH = pl.DeviceIdType.MESH
ANY = pl.ANY


def place():
    r = lax.axis_index("rows")
    t = lax.axis_index("tm")
    return r, t, lax.rem(r, 2), lax.rem(r // 2, 2), r // 4


def remote(src, dst, send, recv, rows, tm):
    pltpu.make_async_remote_copy(
        src_ref=src, dst_ref=dst, send_sem=send, recv_sem=recv,
        device_id=(rows, tm), device_id_type=MESH,
    ).start()


def landed(ref, sem):
    pltpu.make_async_copy(ref, ref, sem).wait()


def greet(peers):
    barrier = pltpu.get_barrier_semaphore()
    for rows, tm in peers:
        pl.semaphore_signal(barrier, inc=1, device_id=(rows, tm), device_id_type=MESH)
    pl.semaphore_wait(barrier, len(peers))


def link_peers():
    r, t, c, y, z = place()
    return [(r + 1 - 2 * c, t), (r + 2 - 4 * y, t), (lax.rem(r + 4, 16), t), (lax.rem(r + 12, 16), t), (r, 1 - t)]


def loop(n, fn, first=0):
    def one(i, carry):
        fn(i)
        return carry
    lax.fori_loop(first, n, one, 0)


UNIT = 64
EDGE = 24
MIDDLE = UNIT - 2 * EDGE
PLANE = EDGE + MIDDLE


class Gather:
    LEAD = 3
    EVENTS = (("from_z", 1, 0), ("from_y", 0, 0), ("from_z", 2, 1), ("from_y", 1, 1), ("from_x", 0, 1), ("from_z", 3, 2),
              ("from_y", 2, 2), ("from_x", 1, 2), ("from_y", 3, 3), ("from_x", 2, 3), ("from_x", 3, 4))
    LAG = 4

    def __init__(self, full, first, units, sems):
        self.full, self.first, self.units = full, first, units
        self.zr, self.yr, self.xr, self.cr, self.snd = sems
        self.r, self.t, self.c, self.y, self.z = place()
        self.taken = set()

    @staticmethod
    def scratch(units):
        sem = pltpu.SemaphoreType.DMA
        return [sem((units, 4)), sem((units, 4)), sem((units, 8)), sem((units,)), sem((5,))]

    def slot(self, z, y):
        return z * 4 + y * 2 + self.c

    def rows_of(self, unit, start, size):
        return pl.ds(pl.multiple_of((unit + self.first) * UNIT + start, 8), size)

    def inplane(self, slot, unit):
        return self.full.at[slot, self.rows_of(unit, self.t * EDGE, PLANE)]

    def edge(self, slot, unit, tm):
        return self.full.at[slot, self.rows_of(unit, tm * PLANE, EDGE)]

    def to_core(self, ref, unit):
        remote(ref, ref, self.snd.at[4], self.cr.at[unit], self.r + 1 - 2 * self.c, self.t)

    def send_own(self, unit):
        r, t, z = self.r, self.t, self.z
        plane = self.inplane(r, unit)

        @pl.when(z < 3)
        def _():
            remote(plane, plane, self.snd.at[0], self.zr.at[unit, z], r + 4, t)

        @pl.when(z > 0)
        def _():
            remote(plane, plane, self.snd.at[1], self.zr.at[unit, z], r - 4, t)

        remote(plane, plane, self.snd.at[2], self.yr.at[unit, z], self.slot(z, 1 - self.y), t)
        self.to_core(self.full.at[r, self.rows_of(unit, 0, UNIT)], unit)

    def pass_on(self, unit, z, y):
        s = self.slot(z, y)
        part = self.edge(s, unit, self.t)
        remote(part, part, self.snd.at[3], self.xr.at[unit, z * 2 + y], self.r, 1 - self.t)
        self.to_core(self.inplane(s, unit), unit)

    def from_z(self, unit, distance):
        for sign in (-1, 1):
            z = self.z + sign * distance

            @pl.when((z >= 0) & (z <= 3))
            def _(z=z, sign=sign):
                plane = self.inplane(self.slot(z, self.y), unit)
                landed(plane, self.zr.at[unit, z])
                onward = self.z - sign

                @pl.when((onward >= 0) & (onward <= 3))
                def _():
                    remote(plane, plane, self.snd.at[0 if sign < 0 else 1], self.zr.at[unit, z], self.slot(onward, self.y), self.t)

                remote(plane, plane, self.snd.at[2], self.yr.at[unit, z], self.slot(self.z, 1 - self.y), self.t)
                self.pass_on(unit, z, self.y)

    def from_y(self, unit, distance):
        for sign in (-1, 1) if distance else (1,):
            z = self.z + sign * distance

            @pl.when((z >= 0) & (z <= 3))
            def _(z=z):
                landed(self.inplane(self.slot(z, 1 - self.y), unit), self.yr.at[unit, z])
                self.pass_on(unit, z, 1 - self.y)

    def from_x(self, unit, distance):
        for other in (False, True) if distance else (True,):
            y = 1 - self.y if other else self.y
            for sign in (-1, 1) if distance else (1,):
                z = self.z + sign * distance

                @pl.when((z >= 0) & (z <= 3))
                def _(z=z, y=y):
                    part = self.edge(self.slot(z, y), unit, 1 - self.t)
                    landed(part, self.xr.at[unit, z * 2 + y])
                    self.to_core(part, unit)

    def begin(self):
        for unit in range(min(self.LEAD, self.units)):
            self.send_own(unit)

    def part(self, step, quarter):
        bounds = (0, 3, 6, 9, len(self.EVENTS))
        for name, distance, lag in self.EVENTS[bounds[quarter]:bounds[quarter + 1]]:
            unit = step - lag

            @pl.when((unit >= 0) & (unit < self.units))
            def _(name=name, distance=distance, unit=unit):
                getattr(self, name)(unit, distance)
        if quarter == 3:
            unit = step + self.LEAD

            @pl.when(unit < self.units)
            def _():
                self.send_own(unit)

    def tick(self, step):
        for quarter in range(4):
            self.part(step, quarter)

    def run(self, first, last):
        loop(last, self.tick, first)

    def arrived(self, unit):
        self.taken.add(unit)
        landed(self.full.at[0:8, self.rows_of(unit, 0, UNIT)], self.cr.at[unit])

    def finish(self):
        full, units, z = self.full, self.units, self.z
        for unit in range(units):
            if unit not in self.taken:
                self.arrived(unit)
        plane = units * PLANE
        for k in range(4):
            @pl.when(z == k)
            def _(k=k):
                if k < 3:
                    landed(full.at[0:k + 1, 0:plane], self.snd.at[0])
                if k > 0:
                    landed(full.at[0:4 - k, 0:plane], self.snd.at[1])
        landed(full.at[0:4, 0:plane], self.snd.at[2])
        landed(full.at[0:7, 0:units * EDGE], self.snd.at[3])
        landed(full.at[0:8, 0:units * UNIT], self.snd.at[4])


S_EDGE = 16
S_MIDDLE = UNIT - 2 * S_EDGE
S_PLANE = S_EDGE + S_MIDDLE


class Scatter:
    LEAD = 3
    RING = 10
    EVENTS = (("sum_core", 0, ()), ("sum_x", 1, ()), ("sum_y", 2, ()), ("hop", 3, (1,)), ("hop", 4, (2,)), ("hop", 5, (3,)), ("exchange", 5, ()), ("conclude", 6, ()))
    LAG = 6

    def __init__(self, grads, out, units, ready, first, scratch):
        self.grads, self.out, self.units, self.ready, self.first = grads, out, units, ready, first
        (self.own, self.obuf, self.cv, self.xv, self.yv, self.zv, self.fv,
         self.load, self.storing, self.cr, self.xr, self.yr, self.zr, self.fr, self.core, self.snd, self.free) = scratch
        self.r, self.t, self.c, self.y, self.z = place()

    @classmethod
    def scratch(cls, units):
        sem, vmem, n, bf = pltpu.SemaphoreType.DMA, pltpu.VMEM, cls.RING, jnp.bfloat16
        return [vmem((2, 8, UNIT, 1024), bf), vmem((2, UNIT, 1024), jnp.float32), vmem((n, 8, UNIT, 1024), bf), vmem((n, 8, S_EDGE, 1024), bf),
                vmem((n, 4, S_PLANE, 1024), bf), vmem((n, 5, S_PLANE, 1024), bf), vmem((n, S_PLANE, 1024), bf),
                sem((2,)), sem((2,)), sem((units,)), sem((units,)), sem((units, 4)), sem((units, 5)), sem((units,)), sem, sem((cls.RING, 5)), pltpu.SemaphoreType.REGULAR((5,))]

    def ring(self, unit):
        return lax.rem(unit, self.RING)

    def number(self, unit):
        late = self.units - self.ready
        after = unit - self.ready
        late_unit = after + late // 2 - jnp.where(after >= late // 2, late, 0)
        return jnp.where(unit < self.ready, unit + self.first, late_unit)

    def rows_of(self, unit):
        return pl.ds(pl.multiple_of(self.number(unit) * UNIT, UNIT), UNIT)

    def mine(self):
        return pl.ds(pl.multiple_of(self.t * S_EDGE, 16), S_PLANE)

    def edge(self, tm):
        return pl.ds(pl.multiple_of(tm * S_PLANE, 16), S_EDGE)

    def granted(self, unit, kind):
        @pl.when(unit >= self.RING)
        def _():
            pl.semaphore_wait(self.free.at[kind], 1)

    def own_copy(self, unit):
        return pltpu.make_async_copy(self.grads.at[:, self.c, self.rows_of(unit)], self.own.at[lax.rem(unit, 2)], self.load.at[lax.rem(unit, 2)])

    def send_core(self, unit):
        self.granted(unit, 0)
        remote(self.grads.at[:, 1 - self.c, self.rows_of(unit)], self.cv.at[self.ring(unit)], self.core, self.cr.at[unit], self.r + 1 - 2 * self.c, self.t)

    def add(self, a, b, n):
        def one(i):
            a[i] = (a[i].astype(jnp.float32) + b[i].astype(jnp.float32)).astype(jnp.bfloat16)
        loop(n, one)

    def sum_core(self, unit):
        at = self.ring(unit)
        cv = self.cv.at[at]
        landed(cv, self.cr.at[unit])
        self.own_copy(unit).wait()
        self.add(cv, self.own.at[lax.rem(unit, 2)], 8)

        @pl.when(unit + 2 < self.units)
        def _():
            self.own_copy(unit + 2).start()
        self.granted(unit, 1)
        remote(cv.at[:, self.edge(1 - self.t)], self.xv.at[at], self.snd.at[at, 0], self.xr.at[unit], self.r, 1 - self.t)

    def sum_x(self, unit):
        at = self.ring(unit)
        xv, cv = self.xv.at[at], self.cv.at[at]
        landed(xv, self.xr.at[unit])
        self.add(cv.at[:, self.edge(self.t)], xv, 8)
        self.granted(unit, 2)
        for k in range(4):
            remote(cv.at[k * 2 + 1 - self.y, self.mine()], self.yv.at[at, k], self.snd.at[at, 1], self.yr.at[unit, k], self.r + 2 - 4 * self.y, self.t)

    def at_z(self, unit, z):
        return self.cv.at[self.ring(unit), z * 2 + self.y, self.mine()]

    def send_z(self, unit, target, up):
        at, entry = self.at_z(unit, target), target + (1 if up else 0)
        remote(at, self.zv.at[self.ring(unit), entry], self.snd.at[self.ring(unit), 2 if up else 3], self.zr.at[unit, entry], self.r + (4 if up else -4), self.t)

    def take_z(self, unit, target, below):
        at, entry = self.at_z(unit, target), target + (1 if below else 0)
        zv = self.zv.at[self.ring(unit), entry]
        landed(zv, self.zr.at[unit, entry])
        at[...] = (at[...].astype(jnp.float32) + zv[...].astype(jnp.float32)).astype(jnp.bfloat16)

    def sum_y(self, unit):
        for k in range(4):
            yv = self.yv.at[self.ring(unit), k]
            landed(yv, self.yr.at[unit, k])
            at = self.at_z(unit, k)
            at[...] = (at[...].astype(jnp.float32) + yv[...].astype(jnp.float32)).astype(jnp.bfloat16)

        @pl.when(self.z == 0)
        def _():
            self.granted(unit, 3)
            for target in (3, 2, 1):
                self.send_z(unit, target, True)

        @pl.when(self.z == 3)
        def _():
            self.granted(unit, 4)
            for target in (0, 1, 2):
                self.send_z(unit, target, False)

    def hop(self, unit, number):
        for z in range(4):
            @pl.when(self.z == z)
            def _(z=z):
                if number == z:
                    if z < 3:
                        self.granted(unit, 3)
                    for target in range(3, z - 1, -1):
                        self.take_z(unit, target, True)
                        if target > z:
                            self.send_z(unit, target, True)
                if number == 3 - z:
                    if z > 0:
                        self.granted(unit, 4)
                    for target in range(0, z + 1):
                        self.take_z(unit, target, False)
                        if target < z:
                            self.send_z(unit, target, False)

    def exchange(self, unit):
        at = self.ring(unit)
        remote(self.at_z(unit, self.z), self.fv.at[at], self.snd.at[at, 4], self.fr.at[unit], self.r, 1 - self.t)

    def store(self, unit):
        number, slot, first = self.number(unit), lax.rem(unit, 2), 0
        for out in self.out:
            rows, cols = out.shape
            count = rows * cols // (UNIT * 1024)

            @pl.when((number >= first) & (number < first + count))
            def _(out=out, first=first, rows=rows):
                at = number - first
                if rows == UNIT:
                    dst = out.at[:, pl.ds(pl.multiple_of(at * 1024, 1024), 1024)]
                else:
                    dst = out.at[pl.ds(pl.multiple_of(at * UNIT, UNIT), UNIT)]
                pltpu.make_async_copy(self.obuf.at[slot], dst, self.storing.at[slot]).start()
            first += count

    def stored(self, unit):
        slot = lax.rem(unit, 2) if not isinstance(unit, int) else unit % 2
        landed(self.obuf.at[slot], self.storing.at[slot])

    def conclude(self, unit):
        at = self.ring(unit)
        fv, cv = self.fv.at[at], self.cv.at[at, self.z * 2 + self.y]
        landed(fv, self.fr.at[unit])

        @pl.when(unit >= 2)
        def _():
            self.stored(unit)
        obuf = self.obuf.at[lax.rem(unit, 2)]
        middle = pl.ds(S_EDGE, S_MIDDLE)
        obuf[middle] = cv[middle].astype(jnp.float32) + fv[pl.ds(pl.multiple_of(self.t * S_EDGE, 16), S_MIDDLE)].astype(jnp.float32)
        obuf[self.edge(self.t)] = cv[self.edge(self.t)].astype(jnp.float32)
        obuf[self.edge(1 - self.t)] = fv[pl.ds(pl.multiple_of((1 - self.t) * S_MIDDLE, 16), S_EDGE)].astype(jnp.float32)
        self.store(unit)
        landed(self.xv.at[at], self.snd.at[at, 0])
        landed(self.yv.at[at], self.snd.at[at, 1])
        for z in range(4):
            @pl.when(self.z == z)
            def _(z=z):
                if z < 3:
                    landed(self.zv.at[at, 0:3 - z], self.snd.at[at, 2])
                if z > 0:
                    landed(self.zv.at[at, 0:z], self.snd.at[at, 3])
        landed(fv, self.snd.at[at, 4])
        more = unit + self.RING < self.units

        def free(kind, rows, tm):
            pl.semaphore_signal(self.free.at[kind], inc=1, device_id=(rows, tm), device_id_type=MESH)

        @pl.when(more)
        def _():
            free(0, self.r + 1 - 2 * self.c, self.t)
            free(1, self.r, 1 - self.t)
            free(2, self.r + 2 - 4 * self.y, self.t)

        @pl.when(more & (self.z > 0))
        def _():
            free(3, self.r - 4, self.t)

        @pl.when(more & (self.z < 3))
        def _():
            free(4, self.r + 4, self.t)

    def begin(self):
        for unit in range(min(2, self.units)):
            self.own_copy(unit).start()
        for unit in range(min(self.LEAD, self.units)):
            self.send_core(unit)

    def part(self, step, quarter):
        for name, lag, args in self.EVENTS[2 * quarter:2 * quarter + 2]:
            unit = step - lag

            @pl.when((unit >= 0) & (unit < self.units))
            def _(name=name, unit=unit, args=args):
                getattr(self, name)(unit, *args)
        if quarter == 3:
            unit = step + self.LEAD

            @pl.when(unit < self.units)
            def _():
                self.send_core(unit)

    def tick(self, step):
        for quarter in range(4):
            self.part(step, quarter)

    def run(self, first, last):
        loop(last, self.tick, first)

    def finish(self):
        for unit in range(max(0, self.units - 2), self.units):
            self.stored(unit)
        landed(self.grads.at[:, 0, 0:self.units * UNIT], self.core)


def spread(slots, landing, send, recv):
    r, t, R = lax.axis_index("rows"), lax.axis_index("tm"), lax.axis_size("rows")
    for d in range(1, R):
        to = lax.rem(r + d, R)
        remote(slots.at[to], landing.at[R - 1 - d], send, recv, to, t)


def gathered(slots, landing, pair, sems, send, recv):
    r, t, R = lax.axis_index("rows"), lax.axis_index("tm"), lax.axis_size("rows")
    landed(slots.at[0:R - 1], send)
    landed(landing.at[0:R - 1], recv)
    total = slots[r]
    for d in range(R - 1):
        total = total + landing[d]
    pair[0] = total
    remote(pair.at[0], pair.at[1], sems.at[0], sems.at[1], r, 1 - t)
    landed(pair.at[0], sems.at[0])
    landed(pair.at[1], sems.at[1])
    pair[0] = pair[0] + pair[1]


HALO = 384
FI1, FO1, QKV, ATT, GLU, CONV, FI2, FO2, UNITS = 0, 4, 8, 11, 12, 14, 15, 19, 23
GAIN, SHIFT, BIAS, TAPS, REL = 0, 6, 20, 28, 33
F32, BF16 = jnp.float32, jnp.bfloat16
TILE = 1024
NN = (((1,), (0,)), ((), ()))
NT = (((1,), (1,)), ((), ()))
TN = (((0,), (0,)), ((), ()))
VMEM_LIMIT = 67043328


def dot(a, b, dims=NN):
    return lax.dot_general(a, b, dims, preferred_element_type=F32)


def by_rows(count, size, fn):
    loop(count // size, lambda i: fn(pl.ds(pl.multiple_of(i * size, size), size)))


def by_cols(count, fn):
    loop(count // TILE, lambda i: fn(pl.ds(pl.multiple_of(i * TILE, TILE), TILE)))


def normalized(v):
    centred = v - jnp.mean(v, axis=-1, keepdims=True)
    rs = lax.rsqrt(jnp.mean(centred * centred, axis=-1, keepdims=True) + EPS)
    return centred * rs, rs


def norm_back(w, gain, vhat, rs):
    wg = w * gain
    return rs * (wg - jnp.mean(wg, axis=-1, keepdims=True) - vhat * jnp.mean(wg * vhat, axis=-1, keepdims=True))


def eight(v):
    return jnp.sum(v.reshape(v.shape[0] // 8, 8, v.shape[1]), axis=0)


def sigmoid(v):
    return 1.0 / (1.0 + jnp.exp(-v))


class Weights:
    def __init__(self, full, buf, sems, blocks):
        self.full, self.buf, self.sems, self.blocks = full, buf, sems, blocks
        self.R = full.shape[0]
        self.n = 1024 // self.R

    def copies(self, k):
        unit, kind, index = self.blocks[k]
        n, R = self.n, self.R
        if kind == "in":
            return [(self.full.at[s, (unit + index) * n:(unit + index + 1) * n], self.buf.at[k, s * n:(s + 1) * n]) for s in range(R)]
        return [(self.full.at[index * (R // 4) + s, unit * n:(unit + 4) * n], self.buf.at[k, s * 4 * n:(s + 1) * 4 * n]) for s in range(R // 4)]

    def start(self, *ks):
        for k in ks or range(len(self.blocks)):
            for src, dst in self.copies(k):
                pltpu.make_async_copy(src, dst, self.sems.at[k]).start()

    def wait(self, *ks):
        for k in ks:
            pltpu.make_async_copy(self.buf.at[k], self.buf.at[k], self.sems.at[k]).wait()


class Grads:
    def __init__(self, out, buf, sems):
        self.out, self.buf, self.sems, self.count = out, buf, sems, 0
        self.R = 2 * out.shape[0]
        self.n = 1024 // self.R

    def put(self, unit, kind, index, left, right, out=None):
        out = self.out if out is None else out
        slot = self.count % 2
        buf, n, R = self.buf.at[slot], self.n, self.R
        if self.count >= 2:
            self.wait(slot)

        def cols(c):
            buf[:, c] = dot(left, right(c), TN).astype(BF16)
        by_cols(1024, cols)
        if kind == "in":
            pairs = [(buf.at[s * n:(s + 1) * n], out.at[s // 2, s % 2, (unit + index) * n:(unit + index + 1) * n]) for s in range(R)]
        else:
            pairs = [(buf.at[s * 4 * n:(s + 1) * 4 * n], out.at[(index * (R // 4) + s) // 2, (index * (R // 4) + s) % 2, unit * n:(unit + 4) * n]) for s in range(R // 4)]
        for src, dst in pairs:
            pltpu.make_async_copy(src, dst, self.sems.at[slot]).start()
        self.count += 1

    def wait(self, slot):
        pltpu.make_async_copy(self.buf.at[slot], self.buf.at[slot], self.sems.at[slot]).wait()

    def finish(self):
        for slot in range(min(2, self.count)):
            self.wait(slot)


def flipped(x, size):
    m = size
    return x + m - 2 * m * lax.rem(x // m, 2)


def cube_peers():
    r, t = lax.axis_index("rows"), lax.axis_index("tm")
    peers, m = [], 1
    while m < lax.axis_size("rows"):
        peers.append((flipped(r, m), t))
        m *= 2
    m = 1
    while m < lax.axis_size("tm"):
        peers.append((r, flipped(t, m)))
        m *= 2
    return peers


def add_all(send, recv, ssem, rsem):
    for i, (rows, tm) in enumerate(cube_peers()):
        remote(send.at[i], recv.at[i], ssem.at[i], rsem.at[i], rows, tm)
        landed(send.at[i], ssem.at[i])
        landed(recv.at[i], rsem.at[i])
        send[i + 1] = send[i] + recv[i]
    return len(cube_peers())


def edge_peers():
    r, t, T = lax.axis_index("rows"), lax.axis_index("tm"), lax.axis_size("tm")
    return [(r, lax.rem(t + 1, T)), (r, lax.rem(t + T - 1, T))]


def swap_edges(pad, count, sems):
    r, t, T = lax.axis_index("rows"), lax.axis_index("tm"), lax.axis_size("tm")

    @pl.when(t < T - 1)
    def _():
        remote(pad.at[count:count + 8], pad.at[0:8], sems.at[0], sems.at[1], r, t + 1)

    @pl.when(t > 0)
    def _():
        remote(pad.at[8:16], pad.at[count + 8:count + 16], sems.at[2], sems.at[3], r, t - 1)

    @pl.when(t < T - 1)
    def _():
        landed(pad.at[0:8], sems.at[0])
        landed(pad.at[0:8], sems.at[3])

    @pl.when(t > 0)
    def _():
        landed(pad.at[0:8], sems.at[2])
        landed(pad.at[0:8], sems.at[1])


def whole():
    return pl.BlockSpec(memory_space=pltpu.VMEM)


def anywhere():
    return pl.BlockSpec(memory_space=ANY)


def shape(*dims, dtype=F32):
    return jax.ShapeDtypeStruct(dims, dtype)


BLOCKS_A = tuple([(FI1, "in", j) for j in range(4)] + [(FO1, "out", j) for j in range(4)] + [(QKV, "in", j) for j in range(3)])


def norm_tokens(tokens, params, a):
    def norm(rows):
        vhat, _ = normalized(tokens[rows].astype(F32))
        a[rows] = (vhat * params[GAIN:GAIN + 1] + params[SHIFT:SHIFT + 1]).astype(BF16)
    by_rows(tokens.shape[0], 256, norm)


def norm_resid(x1, params, a):
    def norm(rows):
        vhat, _ = normalized(x1[rows])
        a[rows] = (vhat * params[GAIN + 1:GAIN + 2] + params[SHIFT + 1:SHIFT + 2]).astype(BF16)
    by_rows(x1.shape[0], 256, norm)


class Front:
    def __init__(self, w, params, tokens, x1, z1, a, h, zbuf, zsem):
        self.w, self.params, self.tokens, self.x1, self.z1, self.a, self.h, self.zbuf, self.zsem = w, params, tokens, x1, z1, a, h, zbuf, zsem

    def stored(self, slot):
        pltpu.make_async_copy(self.zbuf.at[slot], self.zbuf.at[slot], self.zsem.at[slot]).wait()

    def hidden(self, j):
        slot = j % 2
        self.w.wait(j)
        if j >= 2:
            self.stored(slot)
        z = dot(self.a[...], self.w.buf[j]) + self.params[BIAS + j:BIAS + j + 1]
        self.zbuf[slot] = z
        self.h[j] = (z * sigmoid(z)).astype(BF16)
        pltpu.make_async_copy(self.zbuf.at[slot], self.z1.at[:, j * 1024:(j + 1) * 1024], self.zsem.at[slot]).start()

    def project(self, j):
        self.w.wait(4 + j)
        part = dot(self.h[j], self.w.buf[4 + j])
        if j > 0:
            part = self.x1[...] + part
        if j == 3:
            part = self.tokens[...].astype(F32) + 0.5 * (part + self.params[SHIFT + 6:SHIFT + 7])
        self.x1[...] = part

    def mix(self, block, source, shift, out, rows):
        value = dot(source[...], self.w.buf[8 + block])
        if shift is not None:
            value = value + self.params[shift:shift + 1]
        out[rows] = value.astype(BF16)


def front_kernel(blocks, *refs):
    small, *refs = refs
    ws, refs = refs[:8], refs[8:]
    (tokens, hot, segq, segrow, full, params, x1, z1, q, k, v, beside, o, lse, windows, segk, own, slab, slabs, table, strip, wbuf, a, h, zbuf,
     load, keep, ssend, srecv, wsem, zsem, esem, idsem, *sems) = refs
    r, t, c, y, z = place()
    units, R, count = len(blocks), lax.axis_size("rows"), tokens.shape[0]
    copies = []
    for unit, (w, row, col) in enumerate(blocks):
        cp = pltpu.make_async_copy(ws[w].at[row:row + UNIT, col:col + 1024], own.at[unit * UNIT:(unit + 1) * UNIT], load.at[unit])
        cp.start()
        copies.append(cp)
    cs = pltpu.make_async_copy(small, slab, keep)
    cs.start()
    greet([(lax.rem(r + d, R), t) for d in range(1, R)] + [(r, 1 - t)])
    ids = segrow.at[:, pl.ds(pl.multiple_of((1 - t) * (count - HALO), 128), HALO)]
    remote(ids, segk.at[:, pl.ds(pl.multiple_of(t * count, 128), HALO)], idsem.at[0], idsem.at[1], r, 1 - t)
    cs.wait()
    for d in range(1, R):
        remote(slab, slabs.at[r], ssend, srecv, lax.rem(r + d, R), t)
    stored = []
    for unit, cp in enumerate(copies):
        cp.wait()
        put = pltpu.make_async_copy(own.at[unit * UNIT:(unit + 1) * UNIT], full.at[r, unit * UNIT:(unit + 1) * UNIT], load.at[unit])
        put.start()
        stored.append(put)
    for put in stored:
        put.wait()
    g = Gather(full, 0, units, sems)
    g.begin()

    def take_rows():
        landed(slabs.at[0:R - 1], ssend)
        landed(slabs.at[0:R - 1], srecv)
        slabs[r] = slab[...]
        for pair in range(R // 2):
            params[:, pair * 128:(pair + 1) * 128] = (slabs[2 * pair].astype(F32) + slabs[2 * pair + 1].astype(F32))[0:40]
        for s in range(R):
            rows = slabs[s].astype(F32)
            for b in range(2):
                for part in range(2):
                    at = 40 + 2 * b + part
                    params[BIAS + 4 * b + s // 4:BIAS + 4 * b + s // 4 + 1, (s % 4) * 256 + part * 128:(s % 4) * 256 + (part + 1) * 128] = rows[at:at + 1]

    w = Weights(full, wbuf, wsem, BLOCKS_A)
    f = Front(w, params, tokens, x1, z1, a, h, zbuf, zsem)
    mine, other = pl.ds(pl.multiple_of(t * HALO, 128), count), pl.ds(pl.multiple_of((1 - t) * count, 128), HALO)

    def exchange():
        norm_resid(x1, params, a)
        first = pl.multiple_of((1 - t) * (count - HALO), 128)
        remote(a.at[pl.ds(first, HALO)], beside, esem.at[0], esem.at[1], r, 1 - t)

    def receive():
        landed(beside, esem.at[0])
        landed(beside, esem.at[1])
        f.mix(1, beside, None, k, other)

    def bias_rows():
        landed(segrow.at[:, pl.ds(0, HALO)], idsem.at[0])
        landed(segk.at[:, pl.ds(pl.multiple_of((1 - t) * count, 128), HALO)], idsem.at[1])
        segk[:, pl.ds(pl.multiple_of(t * HALO, 128), count)] = segrow[...]
        for head in range(HEADS):
            table[head:head + 1] = params[REL:REL + 1, head * NB:(head + 1) * NB].astype(BF16)
        windows[...] = dot(table[...], hot[...])

    def head_rows(head, b):
        cols, rows = pl.ds(pl.multiple_of(head * 128, 128), 128), pl.ds(b * QB, QB)
        if b == 0:
            strip[...] = strip_of(windows[pl.ds(head, 1)], windows.shape[-1])
        base = k.shape[0] + QB - t * HALO
        attend_rows(q[rows, cols], k[:, cols], v[:, cols], strip, base, b, segq[rows], segk[...], o.at[rows, cols], lse.at[head, rows])

    work = {(2, 1): take_rows, (3, 1): lambda: norm_tokens(tokens, params, a), (4, 1): bias_rows, (5, 1): lambda: f.hidden(0), (6, 1): lambda: f.hidden(1), (7, 1): lambda: f.hidden(2), (8, 1): lambda: f.hidden(3),
            (12, 0): lambda: f.project(0), (12, 2): lambda: f.project(1), (13, 0): lambda: f.project(2), (13, 1): lambda: f.project(3), (13, 2): exchange,
            (14, 1): lambda: (w.wait(8), f.mix(0, a, SHIFT + 7, q, slice(None))), (14, 3): lambda: (w.wait(9), f.mix(1, a, None, k, mine)),
            (15, 1): lambda: (w.wait(10), f.mix(2, a, SHIFT + 8, v, mine)), (16, 1): receive, (17, 1): lambda: f.mix(2, beside, SHIFT + 8, v, other)}
    for step in range(18):
        for quarter in range(4):
            g.part(step, quarter)
            if (step, quarter) in work:
                work[step, quarter]()
        unit = step - g.LAG
        if 0 <= unit < 11:
            g.arrived(unit)
            if unit == 7:
                w.start(4, 5, 6, 7)
            elif unit < 4 or unit > 7:
                w.start(unit)

    def heads(step):
        for quarter in range(4):
            g.part(step, quarter)
            head_rows(step - 18, quarter)
    loop(18 + HEADS, heads, 18)
    g.run(18 + HEADS, units + g.LAG)
    g.finish()
    for slot in range(2):
        f.stored(slot)


def front(small, weights, tokens, hot, segq, segrow, cid):
    length = hot.shape[1]
    count, R, blocks = tokens.shape[0], lax.axis_size("rows"), []
    near = count + HALO
    for i, weight in enumerate(weights):
        n, cols = weight.shape
        blocks += [(i, row, col) for col in range(0, cols, 1024) for row in range(0, n, UNIT)]
    units, sem = len(blocks), pltpu.SemaphoreType.DMA
    return pl.pallas_call(
        functools.partial(front_kernel, tuple(blocks)),
        out_shape=[shape(R, units * UNIT, 1024, dtype=BF16), shape(40, 1024), shape(count, 1024), shape(count, 4096), shape(count, 1024, dtype=BF16),
                   shape(near, 1024, dtype=BF16), shape(near, 1024, dtype=BF16), shape(HALO, 1024, dtype=BF16),
                   shape(count, 1024), shape(HEADS, count, 128), shape(HEADS, length), shape(1, near, dtype=jnp.int32)],
        in_specs=[anywhere()] * 9 + [whole()] * 4, out_specs=[anywhere(), whole(), whole(), anywhere()] + [whole()] * 8,
        scratch_shapes=[pltpu.VMEM((units * UNIT, 1024), BF16), pltpu.VMEM(small.shape, BF16), pltpu.VMEM((R,) + small.shape, BF16), pltpu.VMEM((HEADS, NB), BF16), pltpu.VMEM((QB, length), F32),
                        pltpu.VMEM((11, 1024, 1024), BF16), pltpu.VMEM((count, 1024), BF16), pltpu.VMEM((4, count, 1024), BF16), pltpu.VMEM((2, count, 1024), F32),
                        sem((units,)), sem, sem, sem, sem((11,)), sem((2,)), sem((2,)), sem((2,))] + Gather.scratch(units),
        compiler_params=pltpu.CompilerParams(vmem_limit_bytes=VMEM_LIMIT, collective_id=cid, has_side_effects=True),
        name="front",
    )(small, *weights, tokens, hot, segq, segrow)


def plain_front_kernel(tokens, params, full, x1, z1, q, k, v, wbuf, a, h, zbuf, wsem, zsem):
    w = Weights(full, wbuf, wsem, BLOCKS_A)
    w.start()
    f = Front(w, params, tokens, x1, z1, a, h, zbuf, zsem)
    norm_tokens(tokens, params, a)
    for j in range(4):
        f.hidden(j)
    for j in range(4):
        f.project(j)
    norm_resid(x1, params, a)
    w.wait(8, 9, 10)
    f.mix(0, a, SHIFT + 7, q, slice(None))
    f.mix(1, a, None, k, slice(None))
    f.mix(2, a, SHIFT + 8, v, slice(None))
    for slot in range(2):
        f.stored(slot)


def plain_front(tokens, params, full):
    count = tokens.shape[0]
    return pl.pallas_call(
        plain_front_kernel,
        out_shape=[shape(count, 1024), shape(count, 4096)] + [shape(count, 1024, dtype=BF16)] * 3,
        in_specs=[whole(), whole(), anywhere()], out_specs=[whole(), anywhere(), whole(), whole(), whole()],
        scratch_shapes=[pltpu.VMEM((11, 1024, 1024), BF16), pltpu.VMEM((count, 1024), BF16), pltpu.VMEM((4, count, 1024), BF16), pltpu.VMEM((2, count, 1024), F32),
                        pltpu.SemaphoreType.DMA((11,)), pltpu.SemaphoreType.DMA((2,))],
        compiler_params=pltpu.CompilerParams(vmem_limit_bytes=VMEM_LIMIT),
        name="front",
    )(tokens, params, full)


QB = 128


def strip_of(window, length):
    return pltpu.roll(jnp.broadcast_to(window, (QB, length)), 0, 1, stride=1, stride_axis=0)


def score_block(q, k, strip, base, b, near, segq, segk, scale):
    start = pl.multiple_of(base - b * QB, 128)
    s = dot(q, k, NT) * scale + strip[:, pl.ds(start, near)]
    return jnp.where(segq == segk, s, NEG), start


SCALE = 1.0 / math.sqrt(128)


def attend_rows(q, k, v, strip, base, b, segq, segk, o, lse):
    s, _ = score_block(q, k, strip, base, b, k.shape[0], segq, segk, SCALE)
    top = jnp.max(s, axis=-1, keepdims=True)
    p = jnp.exp(s - top)
    total = jnp.sum(p, axis=-1, keepdims=True)
    o[...] = dot(p.astype(BF16), v) / total
    lse[...] = jnp.broadcast_to(top + jnp.log(total), (QB, 128))


def attend_kernel(off, q, k, v, window, segq, segk, o, lse, strip):
    near = k.shape[0]
    strip[...] = strip_of(window[0], window.shape[-1])
    base = near + QB - off[0]

    def block(b):
        rows = pl.ds(pl.multiple_of(b * QB, QB), QB)
        attend_rows(q[rows], k[...], v[...], strip, base, b, segq[rows], segk[...], o.at[rows], lse.at[0, rows])
    loop(q.shape[0] // QB, block)


def head_block(n):
    return pl.BlockSpec((n, 128), lambda h, off: (0, h))


def attend(q, k, v, windows, segq, segk, off):
    count, near, length = q.shape[0], k.shape[0], windows.shape[-1]
    return pl.pallas_call(
        attend_kernel,
        out_shape=[shape(count, 1024), shape(HEADS, count, 128)],
        grid_spec=pltpu.PrefetchScalarGridSpec(
            num_scalar_prefetch=1, grid=(HEADS,),
            in_specs=[head_block(count), head_block(near), head_block(near), pl.BlockSpec((1, 1, length), lambda h, off: (h, 0, 0)),
                      pl.BlockSpec((count, 1), lambda h, off: (0, 0)), pl.BlockSpec((1, near), lambda h, off: (0, 0))],
            out_specs=[head_block(count), pl.BlockSpec((1, count, 128), lambda h, off: (h, 0, 0))],
            scratch_shapes=[pltpu.VMEM((QB, length), F32)]),
        compiler_params=pltpu.CompilerParams(vmem_limit_bytes=VMEM_LIMIT),
        name="attend",
    )(off, q, k, v, windows, segq, segk)


def attend_back_kernel(scale, off, q, k, v, window, segq, segk, o, lse, do, dq, dk, dv, dtable, strip, ds, pb, acc):
    near = k.shape[0]
    length = window.shape[-1]
    strip[...] = strip_of(window[0], length)
    acc[...] = jnp.zeros_like(acc)
    base = near + QB - off[0]

    def block(b):
        rows = pl.ds(pl.multiple_of(b * QB, QB), QB)
        s, start = score_block(q[rows], k[...], strip, base, b, near, segq[rows], segk[...], scale)
        p = jnp.exp(s - lse[0, rows, 0:1])
        delta = jnp.sum(do[rows].astype(F32) * o[rows], axis=-1, keepdims=True)
        d = (p * (dot(do[rows], v[...], NT) - delta)).astype(BF16)
        pb[rows] = p.astype(BF16)
        ds[rows] = d
        dq[rows] = (dot(d, k[...]) * scale).astype(BF16)
        acc[:, pl.ds(start, near)] += d.astype(F32)
    loop(q.shape[0] // QB, block)
    dims = (((0,), (0,)), ((), ()))
    dk[...] = (dot(ds[...], q[...], dims) * scale).astype(BF16)
    dv[...] = dot(pb[...], do[...], dims).astype(BF16)
    rows, size = acc[...], QB
    while size > 1:
        size //= 2
        rows = rows[:size] + pltpu.roll(rows[size:], length - size, 1)
    dtable[0] = rows


def attend_back(q, k, v, windows, segq, segk, off, o, lse, do):
    count, near, length = q.shape[0], k.shape[0], windows.shape[-1]
    return pl.pallas_call(
        functools.partial(attend_back_kernel, 1.0 / math.sqrt(128)),
        out_shape=[shape(count, 1024, dtype=BF16), shape(near, 1024, dtype=BF16), shape(near, 1024, dtype=BF16), shape(HEADS, 1, length)],
        grid_spec=pltpu.PrefetchScalarGridSpec(
            num_scalar_prefetch=1, grid=(HEADS,),
            in_specs=[head_block(count), head_block(near), head_block(near), pl.BlockSpec((1, 1, length), lambda h, off: (h, 0, 0)),
                      pl.BlockSpec((count, 1), lambda h, off: (0, 0)), pl.BlockSpec((1, near), lambda h, off: (0, 0)),
                      head_block(count), pl.BlockSpec((1, count, 128), lambda h, off: (h, 0, 0)), head_block(count)],
            out_specs=[head_block(count), head_block(near), head_block(near), pl.BlockSpec((1, 1, length), lambda h, off: (h, 0, 0))],
            scratch_shapes=[pltpu.VMEM((QB, length), F32), pltpu.VMEM((count, near), BF16), pltpu.VMEM((count, near), BF16), pltpu.VMEM((QB, length), F32)]),
        compiler_params=pltpu.CompilerParams(vmem_limit_bytes=VMEM_LIMIT),
        name="attend_back",
    )(off, q, k, v, windows, segq, segk, o, lse, do)


ROWS = 128


BLOCKS_C = ((ATT, "in", 0), (GLU, "in", 0), (GLU, "in", 1))


def convolve_kernel(x1, o, params, seg, full, x2, c1, c2, u, y, sums, wbuf, a, half, send, recv, wsem, esem, ssem, rsem):
    w = Weights(full, wbuf, wsem, BLOCKS_C)
    w.start()
    count = x1.shape[0]
    u[0:8] = jnp.zeros((8, 1024), F32)
    u[count + 8:count + 16] = jnp.zeros((8, 1024), F32)
    greet(cube_peers() + edge_peers())

    def cast(rows):
        a[rows] = o[rows].astype(BF16)
    by_rows(count, 256, cast)
    w.wait(0)

    def project(c):
        x2[:, c] = x1[:, c] + dot(a[...], wbuf[0, :, c]) + params[SHIFT + 9:SHIFT + 10, c]
    by_cols(1024, project)

    def norm(rows):
        vhat, _ = normalized(x2[rows])
        a[rows] = (vhat * params[GAIN + 2:GAIN + 3] + params[SHIFT + 2:SHIFT + 3]).astype(BF16)
    by_rows(count, 256, norm)
    w.wait(1, 2)

    def gate(c):
        value = dot(a[...], wbuf[1, :, c]) + params[SHIFT + 10:SHIFT + 11, c]
        other = dot(a[...], wbuf[2, :, c]) + params[SHIFT + 11:SHIFT + 12, c]
        c1[:, c] = value
        c2[:, c] = other
        u[8:count + 8, c] = (value * sigmoid(other)).astype(BF16).astype(F32)
    by_cols(1024, gate)
    swap_edges(u, count, esem)
    half[...] = jnp.zeros_like(half)

    def taps(i):
        first = pl.multiple_of(i * ROWS, ROWS)
        here = seg[pl.ds(first + 8, ROWS)]
        total = jnp.zeros((ROWS, 1024), F32)
        block = u[pl.ds(first, ROWS + 16)]
        segs = seg[pl.ds(first, ROWS + 16)]
        for tap in range(KSIZE):
            k = slice(6 + tap, 6 + tap + ROWS)
            total = total + params[TAPS + tap:TAPS + tap + 1] * jnp.where(segs[k] == here, block[k], 0.0)
        y[pl.ds(first, ROWS)] = total
        half[0:8] += eight(total)
        half[8:16] += eight(total * total)
    loop(count // ROWS, taps)
    fold(half, send)
    steps = add_all(send, recv, ssem, rsem)
    sums[...] = send[steps]


def fold(half, send):
    send[0, 0:1] = jnp.sum(half[0:8], axis=0, keepdims=True)
    send[0, 1:2] = jnp.sum(half[8:16], axis=0, keepdims=True)


def reduce_scratch(rows=2):
    steps = (lax.axis_size("rows").bit_length() - 1) + (lax.axis_size("tm").bit_length() - 1)
    return [pltpu.VMEM((steps + 1, rows, 1024), F32), pltpu.VMEM((steps, rows, 1024), F32)], [pltpu.SemaphoreType.DMA((steps,)), pltpu.SemaphoreType.DMA((steps,))]


def convolve(x1, o, params, seg, full, cid):
    count = x1.shape[0]
    bufs, sems = reduce_scratch()
    return pl.pallas_call(
        convolve_kernel,
        out_shape=[shape(count, 1024), shape(count, 1024), shape(count, 1024), shape(count + 16, 1024), shape(count, 1024), shape(2, 1024)],
        in_specs=[whole()] * 4 + [anywhere()], out_specs=[whole()] * 6,
        scratch_shapes=[pltpu.VMEM((3, 1024, 1024), BF16), pltpu.VMEM((count, 1024), BF16), pltpu.VMEM((16, 1024), F32)] + bufs + [pltpu.SemaphoreType.DMA((3,)), pltpu.SemaphoreType.DMA((4,))] + sems,
        compiler_params=pltpu.CompilerParams(vmem_limit_bytes=VMEM_LIMIT, collective_id=cid, has_side_effects=True),
        name="convolve",
    )(x1, o, params, seg, full)


def batch_stats(sums, frames):
    mean = sums[0:1] / frames
    square = sums[1:2] / frames
    return mean, lax.rsqrt(square - mean * mean + EPS)


BLOCKS_D = tuple([(CONV, "in", 0)] + [(FI2, "in", j) for j in range(4)] + [(FO2, "out", j) for j in range(4)])


def middle_kernel(frames, x2, y, sums, cot, params, full, out, g3, dn, totals, small, grads, grads_b,
                  wbuf, a, e, d, dz, h, z, stage, half, send, recv, wsem, gsem, ssem, rsem):
    w = Weights(full, wbuf, wsem, BLOCKS_D)
    w.start()
    greet(cube_peers())
    g = Grads(grads, stage, gsem)
    count = x2.shape[0]
    mean, inverse = batch_stats(sums, frames)
    small[...] = jnp.zeros_like(small)
    half[...] = jnp.zeros_like(half)

    def active(rows):
        n = (y[rows] - mean) * inverse * params[GAIN + 5:GAIN + 6] + params[SHIFT + 5:SHIFT + 6]
        e[rows] = (n * sigmoid(n)).astype(BF16)
    by_rows(count, 256, active)
    w.wait(0)
    x3 = g3

    def project(c):
        x3[:, c] = x2[:, c] + dot(e[...], wbuf[0, :, c]) + params[SHIFT + 12:SHIFT + 13, c]
    by_cols(1024, project)

    def norm(rows):
        vhat, _ = normalized(x3[rows])
        a[rows] = (vhat * params[GAIN + 3:GAIN + 4] + params[SHIFT + 3:SHIFT + 4]).astype(BF16)
    by_rows(count, 256, norm)
    for j in range(4):
        w.wait(1 + j)

    def hidden(j):
        def cols(c):
            v = dot(a[...], wbuf[1 + j, :, c]) + params[pl.ds(BIAS + 4 + j, 1), c]
            z[j, :, c] = v
            h[j, :, c] = (v * sigmoid(v)).astype(BF16)
        by_cols(1024, cols)
    loop(4, hidden)
    w.wait(5, 6, 7, 8)

    def outward(c):
        acc = dot(h[0], wbuf[5, :, c])
        for j in range(1, 4):
            acc = acc + dot(h[j], wbuf[5 + j, :, c])
        out[:, c] = x3[:, c] + 0.5 * (acc + params[SHIFT + 13:SHIFT + 14, c])
    by_cols(1024, outward)

    def last(rows):
        vhat, rs = normalized(out[rows])
        gain = params[GAIN + 4:GAIN + 5]
        out[rows] = vhat * gain + params[SHIFT + 4:SHIFT + 5]
        ct = cot[rows]
        small[0:8] += eight(ct * vhat)
        small[8:16] += eight(ct)
        g4 = norm_back(ct, gain, vhat, rs)
        dn[rows] = g4
        half = (0.5 * g4).astype(BF16)
        d[rows] = half
        small[16:24] += eight(half.astype(F32))
    by_rows(count, 256, last)

    def back(j):
        def cols(c):
            v = z[j, :, c]
            s = sigmoid(v)
            dh = dot(d[...], wbuf[5 + j, c, :], NT) * (s * (1.0 + v * (1.0 - s)))
            dh = dh.astype(BF16)
            dz[j, :, c] = dh
            small[pl.ds(pl.multiple_of(24 + 8 * j, 8), 8), c] += eight(dh.astype(F32))
        by_cols(1024, cols)
    loop(4, back)
    for j in range(4):
        g.put(0, "out", j, h[j], lambda c: d[:, c], grads_b)
    for j in range(4):
        g.put(FI2, "in", j, a[...], lambda c, j=j: dz[j, :, c])
    da = z.at[0]

    def inward(c):
        acc = dot(dz[0], wbuf[1, c, :], NT)
        for j in range(1, 4):
            acc = acc + dot(dz[j], wbuf[1 + j, c, :], NT)
        da[:, c] = acc
    by_cols(1024, inward)

    def resid(rows):
        vhat, rs = normalized(x3[rows])
        w3 = da[rows]
        small[56:64] += eight(w3 * vhat)
        small[64:72] += eight(w3)
        total = dn[rows] + norm_back(w3, params[GAIN + 3:GAIN + 4], vhat, rs)
        g3[rows] = total
        de = total.astype(BF16)
        d[rows] = de
        small[72:80] += eight(de.astype(F32))
    by_rows(count, 256, resid)
    g.put(CONV, "in", 0, e[...], lambda c: d[:, c])

    def dnorm(c):
        dn[:, c] = dot(d[...], wbuf[0, c, :], NT)
    by_cols(1024, dnorm)

    def finish(rows):
        yhat = (y[rows] - mean) * inverse
        n = yhat * params[GAIN + 5:GAIN + 6] + params[SHIFT + 5:SHIFT + 6]
        s = sigmoid(n)
        v = dn[rows] * (s * (1.0 + n * (1.0 - s)))
        dn[rows] = v
        half[0:8] += eight(v * yhat)
        half[8:16] += eight(v)
    by_rows(count, 256, finish)
    small[80:96] = half[...]
    fold(half, send)
    steps = add_all(send, recv, ssem, rsem)
    totals[...] = send[steps]
    g.finish()


def middle(x2, y, sums, cot, params, full, frames, cid):
    count = x2.shape[0]
    bufs, sems = reduce_scratch()
    return pl.pallas_call(
        functools.partial(middle_kernel, frames),
        out_shape=[shape(count, 1024), shape(count, 1024), shape(count, 1024), shape(2, 1024), shape(96, 1024), shape(full.shape[0] // 2, 2, FO2 * 1024 // full.shape[0], 1024, dtype=BF16), shape(full.shape[0] // 2, 2, 4096 // full.shape[0], 1024, dtype=BF16)],
        in_specs=[whole()] * 5 + [anywhere()], out_specs=[whole()] * 5 + [anywhere()] * 2,
        scratch_shapes=[pltpu.VMEM((9, 1024, 1024), BF16), pltpu.VMEM((count, 1024), BF16), pltpu.VMEM((count, 1024), BF16), pltpu.VMEM((count, 1024), BF16),
                        pltpu.VMEM((4, count, 1024), BF16), pltpu.VMEM((4, count, 1024), BF16), pltpu.VMEM((4, count, 1024), F32),
                        pltpu.VMEM((2, 1024, 1024), BF16), pltpu.VMEM((16, 1024), F32)] + bufs + [pltpu.SemaphoreType.DMA((9,)), pltpu.SemaphoreType.DMA((2,))] + sems,
        compiler_params=pltpu.CompilerParams(vmem_limit_bytes=VMEM_LIMIT, collective_id=cid, has_side_effects=True),
        name="middle",
    )(x2, y, sums, cot, params, full)


def convolve_back_kernel(frames, dn, y, sums, totals, c1, c2, u, x2, g3, o, params, seg, full, grads_in, g2, dob, small, grads,
                         wbuf, a, d, dc, pad, stage, wsem, gsem, esem):
    w = Weights(full, wbuf, wsem, BLOCKS_C)
    w.start()
    count = x2.shape[0]
    pad[0:8] = jnp.zeros((8, 1024), F32)
    pad[count + 8:count + 16] = jnp.zeros((8, 1024), F32)
    greet(edge_peers())
    g = Grads(grads, stage, gsem)
    mean, inverse = batch_stats(sums, frames)
    gain = params[GAIN + 5:GAIN + 6]
    product = totals[0:1] * gain / frames
    total = totals[1:2] * gain / frames
    small[...] = jnp.zeros_like(small)

    def dy(i):
        rows = pl.ds(pl.multiple_of(i * ROWS, ROWS), ROWS)
        yhat = (y[rows] - mean) * inverse
        v = inverse * (dn[rows] * gain - total - yhat * product)
        pad[pl.ds(pl.multiple_of(i * ROWS + 8, 8), ROWS)] = v.astype(BF16).astype(F32)
        vhat, _ = normalized(x2[rows])
        a[rows] = (vhat * params[GAIN + 2:GAIN + 3] + params[SHIFT + 2:SHIFT + 3]).astype(BF16)
    loop(count // ROWS, dy)
    swap_edges(pad, count, esem)

    def taps(i):
        first = pl.multiple_of(i * ROWS, ROWS)
        rows = pl.ds(first, ROWS)
        block, grad, segs = u[pl.ds(first, ROWS + 16)], pad[pl.ds(first, ROWS + 16)], seg[pl.ds(first, ROWS + 16)]
        here, own = segs[8:ROWS + 8], grad[8:ROWS + 8]
        du = jnp.zeros((ROWS, 1024), F32)
        for tap in range(KSIZE):
            k = slice(6 + tap, 6 + tap + ROWS)
            small[8 * tap:8 * tap + 8] += eight(own * jnp.where(segs[k] == here, block[k], 0.0))
            b = slice(10 - tap, 10 - tap + ROWS)
            du = du + params[TAPS + tap:TAPS + tap + 1] * jnp.where(segs[b] == here, grad[b], 0.0)
        s = sigmoid(c2[rows])
        left = (du * s).astype(BF16)
        right = (du * c1[rows] * s * (1.0 - s)).astype(BF16)
        dc[0, rows] = left
        dc[1, rows] = right
        small[40:48] += eight(left.astype(F32))
        small[48:56] += eight(right.astype(F32))
    loop(count // ROWS, taps)
    w.wait(0, 1, 2)
    da = pad.at[0:count]

    def inward(c):
        da[:, c] = dot(dc[0], wbuf[1, c, :], NT) + dot(dc[1], wbuf[2, c, :], NT)
    by_cols(1024, inward)

    def resid(rows):
        vhat, rs = normalized(x2[rows])
        v = da[rows]
        small[56:64] += eight(v * vhat)
        small[64:72] += eight(v)
        both = g3[rows] + norm_back(v, params[GAIN + 2:GAIN + 3], vhat, rs)
        g2[rows] = both
        dx = both.astype(BF16)
        d[rows] = dx
        small[72:80] += eight(dx.astype(F32))
    by_rows(count, 256, resid)

    def attended(c):
        dob[:, c] = dot(d[...], wbuf[0, c, :], NT).astype(BF16)
    by_cols(1024, attended)
    for j in range(2):
        g.put(GLU, "in", j, a[...], lambda c, j=j: dc[j, :, c])

    def cast(rows):
        a[rows] = o[rows].astype(BF16)
    by_rows(count, 256, cast)
    g.put(ATT, "in", 0, a[...], lambda c: d[:, c])
    g.finish()


def convolve_back(dn, y, sums, totals, c1, c2, u, x2, g3, o, params, seg, full, grads, frames, cid):
    count = x2.shape[0]
    return pl.pallas_call(
        functools.partial(convolve_back_kernel, frames),
        out_shape=[shape(count, 1024), shape(count, 1024, dtype=BF16), shape(80, 1024), shape(*grads.shape, dtype=BF16)],
        in_specs=[whole()] * 12 + [anywhere()] * 2, out_specs=[whole()] * 3 + [anywhere()],
        scratch_shapes=[pltpu.VMEM((3, 1024, 1024), BF16), pltpu.VMEM((count, 1024), BF16), pltpu.VMEM((count, 1024), BF16), pltpu.VMEM((2, count, 1024), BF16),
                        pltpu.VMEM((count + 16, 1024), F32), pltpu.VMEM((2, 1024, 1024), BF16),
                        pltpu.SemaphoreType.DMA((3,)), pltpu.SemaphoreType.DMA((2,)), pltpu.SemaphoreType.DMA((4,))],
        input_output_aliases={13: 3},
        compiler_params=pltpu.CompilerParams(vmem_limit_bytes=VMEM_LIMIT, collective_id=cid, has_side_effects=True),
        name="convolve_back",
    )(dn, y, sums, totals, c1, c2, u, x2, g3, o, params, seg, full, grads)


BLOCKS_E = tuple([(QKV, "in", j) for j in range(3)])
BLOCKS_F = tuple([(FO1, "out", j) for j in range(4)] + [(FI1, "in", j) for j in range(4)])


def rear_kernel(halo, x1, g2, dq, dk, dv, params, full, *refs):
    if halo:
        beside, grads_in, g1, small, grads, wbuf, a, stage, da, back, got, wsem, gsem, esem = refs
    else:
        grads_in, g1, small, grads, wbuf, a, stage, da, wsem, gsem = refs
    w = Weights(full, wbuf, wsem, BLOCKS_E)
    w.start()
    g = Grads(grads, stage, gsem)
    count = x1.shape[0]
    small[...] = jnp.zeros_like(small)
    own = 0
    if halo:
        r, t = lax.axis_index("rows"), lax.axis_index("tm")
        greet([(r, 1 - t)])
        own, other = pl.multiple_of(t * HALO, 128), pl.multiple_of((1 - t) * count, 128)
        w.wait(1, 2)

        def outside(c):
            back[:, c] = (dot(dk[pl.ds(other, HALO)], wbuf[1, c, :], NT) + dot(dv[pl.ds(other, HALO)], wbuf[2, c, :], NT)).astype(BF16)
        by_cols(1024, outside)
        remote(back, got, esem.at[0], esem.at[1], r, 1 - t)
        w.wait(0)
    else:
        w.wait(0, 1, 2)
    mine = pl.ds(own, count)

    def inside(c):
        da[:, c] = dot(dq[...], wbuf[0, c, :], NT) + dot(dk[mine], wbuf[1, c, :], NT) + dot(dv[mine], wbuf[2, c, :], NT)
    by_cols(1024, inside)

    def norm(rows):
        vhat, _ = normalized(x1[rows])
        a[rows] = (vhat * params[GAIN + 1:GAIN + 2] + params[SHIFT + 1:SHIFT + 2]).astype(BF16)
        small[0:8] += eight(dq[rows].astype(F32))
    by_rows(count, 256, norm)

    def values(rows):
        small[8:16] += eight(dv[rows].astype(F32))
    by_rows(dv.shape[0], 128, values)
    g.put(QKV, "in", 0, a[...], lambda c: dq[:, c])
    if halo:
        for j, grad in ((1, dk), (2, dv)):
            slot = g.count % 2
            buf, n, R = stage.at[slot], g.n, g.R
            if g.count >= 2:
                g.wait(slot)

            def cols(c, grad=grad, buf=buf):
                buf[:, c] = (dot(a[...], grad[mine, c], TN) + dot(beside[...], grad[pl.ds(other, HALO), c], TN)).astype(BF16)
            by_cols(1024, cols)
            for s in range(R):
                pltpu.make_async_copy(buf.at[s * n:(s + 1) * n], grads.at[s // 2, s % 2, (QKV + j) * n:(QKV + j + 1) * n], gsem.at[slot]).start()
            g.count += 1
        landed(back, esem.at[0])
        landed(got, esem.at[1])
        first = pl.multiple_of((1 - t) * (count - HALO), 128)

        def merge(i):
            rows = pl.ds(pl.multiple_of(first + i * 64, 64), 64)
            da[rows] += got[pl.ds(pl.multiple_of(i * 64, 64), 64)].astype(F32)
        loop(HALO // 64, merge)
    else:
        g.put(QKV, "in", 1, a[...], lambda c: dk[:, c])
        g.put(QKV, "in", 2, a[...], lambda c: dv[:, c])

    def resid(rows):
        vhat, rs = normalized(x1[rows])
        v = da[rows]
        small[16:24] += eight(v * vhat)
        small[24:32] += eight(v)
        g1[rows] = g2[rows] + norm_back(v, params[GAIN + 1:GAIN + 2], vhat, rs)
    by_rows(count, 256, resid)
    g.finish()


def rear(x1, g2, dq, dk, dv, params, full, beside, grads, cid):
    count = x1.shape[0]
    halo = beside is not None
    scratch = [pltpu.VMEM((3, 1024, 1024), BF16), pltpu.VMEM((count, 1024), BF16), pltpu.VMEM((2, 1024, 1024), BF16), pltpu.VMEM((count, 1024), F32)]
    if halo:
        scratch += [pltpu.VMEM((HALO, 1024), BF16), pltpu.VMEM((HALO, 1024), BF16)]
    scratch += [pltpu.SemaphoreType.DMA((3,)), pltpu.SemaphoreType.DMA((2,))]
    if halo:
        scratch.append(pltpu.SemaphoreType.DMA((2,)))
    specs = [whole()] * 6 + [anywhere()] + ([whole()] if halo else []) + [anywhere()]
    return pl.pallas_call(
        functools.partial(rear_kernel, halo),
        out_shape=[shape(count, 1024), shape(32, 1024), shape(*grads.shape, dtype=BF16)],
        in_specs=specs, out_specs=[whole(), whole(), anywhere()], scratch_shapes=scratch,
        input_output_aliases={len(specs) - 1: 2},
        compiler_params=pltpu.CompilerParams(vmem_limit_bytes=VMEM_LIMIT, **({"collective_id": cid, "has_side_effects": True} if halo else {})),
        name="rear",
    )(x1, g2, dq, dk, dv, params, full, *((beside,) if halo else ()), grads)


class Last:
    def __init__(self, full, params, tokens, g1, z1, dtok, small, grads, scratch):
        wbuf, self.a, self.d, self.dz, self.zbuf, self.hbuf, stage, self.da, wsem, self.zsem, gsem = scratch
        self.w = Weights(full, wbuf, wsem, BLOCKS_F[:4])
        self.w2 = Weights(full, wbuf, wsem, BLOCKS_F[4:])
        self.g = Grads(grads, stage, gsem)
        self.params, self.tokens, self.g1, self.z1, self.dtok, self.small = params, tokens, g1, z1, dtok, small

    @staticmethod
    def scratch(count):
        sem, vmem = pltpu.SemaphoreType.DMA, pltpu.VMEM
        return [vmem((4, 1024, 1024), BF16), vmem((count, 1024), BF16), vmem((count, 1024), BF16), vmem((4, count, 1024), BF16), vmem((2, count, 1024), F32),
                vmem((count, 1024), BF16), vmem((2, 1024, 1024), BF16), vmem((count, 1024), F32), sem((4,)), sem((2,)), sem((2,))]

    def z_copy(self, j):
        return pltpu.make_async_copy(self.z1.at[:, j * 1024:(j + 1) * 1024], self.zbuf.at[j % 2], self.zsem.at[j % 2])

    def start(self):
        self.w.start()
        self.z_copy(0).start()
        self.z_copy(1).start()

    def prepare(self):
        self.small[...] = jnp.zeros_like(self.small)

        def rows(rows):
            half = (0.5 * self.g1[rows]).astype(BF16)
            self.d[rows] = half
            self.small[0:8] += eight(half.astype(F32))
        by_rows(self.d.shape[0], 256, rows)
        norm_tokens(self.tokens, self.params, self.a)

    def hidden(self, j):
        self.w.wait(j)
        self.z_copy(j).wait()
        v = self.zbuf[j % 2]
        s = sigmoid(v)
        self.hbuf[...] = (v * s).astype(BF16)
        dh = (dot(self.d[...], self.w.buf[j], NT) * (s * (1.0 + v * (1.0 - s)))).astype(BF16)
        self.dz[j] = dh
        self.small[8 + 8 * j:16 + 8 * j] += eight(dh.astype(F32))
        self.w2.start(j)
        if j + 2 < 4:
            self.z_copy(j + 2).start()

    def outward(self, j):
        self.g.put(FO1, "out", j, self.hbuf[...], lambda c: self.d[:, c])

    def inward(self, j):
        self.g.put(FI1, "in", j, self.a[...], lambda c: self.dz[j, :, c])

    def through(self, j):
        self.w2.wait(j)
        part = dot(self.dz[j], self.w2.buf[j], NT)
        self.da[...] = part if j == 0 else self.da[...] + part

    def end(self):
        def rows(rows):
            vhat, rs = normalized(self.tokens[rows].astype(F32))
            v = self.da[rows]
            self.small[40:48] += eight(v * vhat)
            self.small[48:56] += eight(v)
            self.dtok[rows] = self.g1[rows] + norm_back(v, self.params[GAIN:GAIN + 1], vhat, rs)
        by_rows(self.d.shape[0], 256, rows)


def plain_last_kernel(tokens, g1, z1, params, full, grads_in, dtok, small, grads, *scratch):
    f = Last(full, params, tokens, g1, z1, dtok, small, grads, scratch)
    f.start()
    f.prepare()
    for j in range(4):
        f.hidden(j)
        f.outward(j)
    for j in range(4):
        f.inward(j)
    for j in range(4):
        f.through(j)
    f.end()
    f.g.finish()


def plain_last(tokens, g1, z1, params, full, grads):
    count = tokens.shape[0]
    return pl.pallas_call(
        plain_last_kernel,
        out_shape=[shape(count, 1024), shape(56, 1024), shape(*grads.shape, dtype=BF16)],
        in_specs=[whole(), whole(), anywhere(), whole(), anywhere(), anywhere()], out_specs=[whole(), whole(), anywhere()],
        scratch_shapes=Last.scratch(count), input_output_aliases={5: 2},
        compiler_params=pltpu.CompilerParams(vmem_limit_bytes=VMEM_LIMIT),
        name="last",
    )(tokens, g1, z1, params, full, grads)


def last_kernel(units, ready, first, tokens, g1, z1, params, full, rows_in, share, grads_in, dtok, *refs):
    out, refs = refs[:7], refs[7:]
    (rows_out, late_out, share_out, grads,
     small, lv, lout, sown, sv, sx, town, tv, tx, lsem, sload, ssend, srecv, sxsem, tsend, trecv, txsem, *scratch) = refs
    r, t, c, y, z = place()
    R = lax.axis_size("rows")
    n = len(Last.scratch(tokens.shape[0]))
    f = Last(full, params, tokens, g1, z1, dtok, small, grads, scratch[:n])
    f.start()
    cs = pltpu.make_async_copy(rows_in, sown, sload.at[0])
    cs.start()
    lc = pltpu.make_async_copy(share, lv.at[0], lsem.at[0])
    lc.start()
    greet([(lax.rem(r + d, R), t) for d in range(1, R)] + [(r, 1 - t)])
    s = Scatter(grads, out, units, ready, first, scratch[n:])
    s.begin()
    cs.wait()
    spread(sown, sv, ssend, srecv)
    lc.wait()
    pieces = share.shape[0] // 16

    def piece(i):
        @pl.when((i >= 2) & (i < pieces + 2))
        def _():
            rows = pl.ds(pl.multiple_of((i - 2) * 16, 16), 16)
            remote(lv.at[0, rows], lv.at[1, rows], lsem.at[1], lsem.at[2], r, 1 - t)

    def late_rows():
        town[...] = jnp.zeros_like(town)
        sums = [jnp.sum(small[8 * i:8 * i + 8], axis=0, keepdims=True) for i in range(7)]
        for to in range(R):
            pair = slice(to // 2 * 128, to // 2 * 128 + 128)
            for row, which in ((0, 0), (1, 5), (2, 6)):
                town[to, row:row + 1] = sums[which][:, pair]
            for half in range(2):
                at = (to % 4) * 256 + half * 128
                town[to, 3 + half:4 + half] = sums[1 + to // 4][:, at:at + 128]
        spread(town, tv, tsend, trecv)

    work = {(0, 2): f.prepare, (5, 0): lambda: f.inward(0), (5, 2): lambda: f.inward(1), (6, 0): lambda: f.inward(2), (6, 2): lambda: f.inward(3), (7, 0): f.g.finish,
            (7, 1): lambda: f.through(0), (7, 3): lambda: f.through(1), (8, 1): lambda: f.through(2), (8, 3): lambda: f.through(3), (9, 1): f.end, (10, 1): late_rows}
    for j in range(4):
        work[1 + j, 0] = lambda j=j: f.hidden(j)
        work[1 + j, 2] = lambda j=j: f.outward(j)
    for step in range(11):
        piece(step)
        for quarter in range(4):
            s.part(step, quarter)
            if (step, quarter) in work:
                work[step, quarter]()

    def rest(step):
        piece(step)
        s.tick(step)
    loop(units + s.LAG, rest, 11)
    gathered(sown, sv, sx, sxsem, ssend, srecv)
    gathered(town, tv, tx, txsem, tsend, trecv)
    done = [pltpu.make_async_copy(sx.at[0], rows_out, sload.at[0]), pltpu.make_async_copy(tx.at[0], late_out, sload.at[1])]
    landed(lv.at[0], lsem.at[1])
    landed(lv.at[1], lsem.at[2])
    lout[...] = lv[0].astype(F32) + lv[1].astype(F32)
    done.append(pltpu.make_async_copy(lout, share_out, lsem.at[0]))
    for copy in done:
        copy.start()
    s.finish()
    for copy in done:
        copy.wait()


def last(tokens, g1, z1, params, full, rows, share, grads, shapes, cid):
    count, R = tokens.shape[0], full.shape[0]
    units, ready = FO2, FO2 - QKV
    sem, vmem = pltpu.SemaphoreType.DMA, pltpu.VMEM
    late = (8, 128)
    return pl.pallas_call(
        functools.partial(last_kernel, units, ready, QKV),
        out_shape=[shape(count, 1024)] + [shape(*dims) for dims in shapes] + [shape(*rows.shape[1:]), shape(*late), shape(*share.shape), shape(*grads.shape, dtype=BF16)],
        in_specs=[whole(), whole(), anywhere(), whole()] + [anywhere()] * 4, out_specs=[whole()] + [anywhere()] * 11,
        scratch_shapes=[vmem((56, 1024), F32), vmem((2,) + share.shape, BF16), vmem(share.shape, F32),
                        vmem(rows.shape, F32), vmem((R - 1,) + rows.shape[1:], F32), vmem((2,) + rows.shape[1:], F32),
                        vmem((R,) + late, F32), vmem((R - 1,) + late, F32), vmem((2,) + late, F32),
                        sem((3,)), sem((2,)), sem, sem, sem((2,)), sem, sem, sem((2,))] + Last.scratch(count) + Scatter.scratch(units),
        input_output_aliases={7: 11},
        compiler_params=pltpu.CompilerParams(vmem_limit_bytes=VMEM_LIMIT, collective_id=cid, has_side_effects=True),
        name="last",
    )(tokens, g1, z1, params, full, rows, share, grads)


def pack_rows(gains, shifts, ffn_bias, conv_kernel, rel_table):
    n = rel_table.shape[0]
    rows = jnp.concatenate([gains, shifts, ffn_bias.reshape(2 * 4, n), conv_kernel, rel_table[None]], axis=0).reshape(-1)
    return jnp.pad(rows, (0, 8 * 384 - rows.shape[0])).reshape(8, 384)


def slab_rows(gains, shifts, ffn_bias, conv_kernel, rel_table):
    parts = ((0, gains), (6, shifts), (28, conv_kernel), (33, rel_table[None]))
    rows = sum(jnp.pad(part, ((at, 48 - at - part.shape[0]), (0, 0))) for at, part in parts)
    odd = lax.rem(lax.axis_index("rows"), 2) == 1
    wide = jnp.tile(rows, (1, 2))
    keep = (lax.broadcasted_iota(jnp.int32, wide.shape, 1) >= 64) == odd
    return jnp.where(keep, wide, jnp.zeros_like(wide)) + jnp.pad(ffn_bias.reshape(4, 128), ((40, 4), (0, 0)))


def wide_rows(smalls):
    R = smalls.shape[0]
    n = 1024 // R
    rows = smalls.reshape(R, -1)[:, : 34 * n].reshape(R, 34, n).astype(F32)
    flat = rows.transpose(1, 0, 2).reshape(34, 1024)
    bias = rows[:, 20:28].reshape(R, 2, 4 * n).transpose(1, 0, 2).reshape(8, 1024)
    return jnp.concatenate([flat[:20], bias, flat[28:], jnp.zeros((6, 1024), F32)], axis=0)


def slot_rows(rows, R):
    n = 1024 // R
    flat = rows.reshape(34, R, n).transpose(1, 0, 2)
    bias = rows[20:28].reshape(2, R, 4, n).transpose(1, 0, 2, 3).reshape(R, 8, n)
    flat = jnp.concatenate([flat[:, :20], bias, flat[:, 28:]], axis=1).reshape(R, 34 * n)
    return jnp.pad(flat, ((0, 0), (0, 8 * 384 - 34 * n))).reshape(R, 8, 384)


def split_rows(rows):
    return (rows[:6], rows[6:20], rows[20:28].reshape(2, -1), rows[28:33], rows[33])


def pack_weights(weights):
    blocks = []
    for w in weights:
        rows, cols = w.shape
        blocks.append(w.reshape(rows, cols // 1024, 1024).transpose(1, 0, 2).reshape(-1, 1024))
    return jnp.concatenate(blocks, axis=0)


def unpack_shard(shard, weights):
    out, row = [], 0
    for w in weights:
        n, cols = w.shape
        count = n * cols // 1024
        out.append(shard[row : row + count].reshape(cols // 1024, n, 1024).transpose(1, 0, 2).reshape(n, cols))
        row += count
    return tuple(out)


def body(tokens, cotangent, segment_ids, rel_bucket, ffn1_in, ffn1_out, qkv_weight, attn_out, glu_in, conv_out, ffn2_in, ffn2_out,
         gains, shifts, ffn_bias, conv_kernel, rel_table):
    packed_rows, count, width = tokens.shape
    R, T = lax.axis_size("rows"), lax.axis_size("tm")
    t = lax.axis_index("tm")
    links = R == 16 and T == 2 and count == 512
    frames = R * T * count * packed_rows
    weights = (ffn1_in, ffn1_out, qkv_weight, attn_out, glu_in, conv_out, ffn2_in, ffn2_out)
    segq = segment_ids.reshape(count, 1)
    if links:
        near, off = count + HALO, t * HALO
    else:
        near, off = T * count, t * count
        segk = lax.all_gather(segment_ids, "tm", axis=1, tiled=True)
    length = 2 * near + QB
    places = np.clip(np.arange(length) - (near + QB), -MAXD, MAXD) + MAXD
    before, after = int(np.argmax(places > 0)), int(np.argmax(places >= 2 * MAXD))
    buckets = jnp.concatenate([jnp.broadcast_to(rel_bucket[:1], (before,)), rel_bucket[1 : 2 * MAXD], jnp.broadcast_to(rel_bucket[2 * MAXD :], (length - after,))])
    hot = (buckets[None, :] == jnp.arange(NB, dtype=jnp.int32)[:, None]).astype(F32)
    off = off.astype(jnp.int32).reshape(1)
    tok = tokens.reshape(count, width)
    if links:
        full, params, x1, z1, q, k, v, beside, o, lse, windows, segk = front(slab_rows(gains, shifts, ffn_bias, conv_kernel, rel_table), weights, tok, hot.astype(BF16), segq, segment_ids, 0)
        windows = windows.reshape(HEADS, 1, length)
    else:
        full = lax.all_gather(pack_weights(weights), "rows", axis=0)
        params = wide_rows(lax.all_gather(pack_rows(gains, shifts, ffn_bias, conv_kernel, rel_table), "rows", axis=0))

        windows = jnp.dot(params[REL].reshape(HEADS, NB), hot, precision=HIGH).reshape(HEADS, 1, length)

    if not links:
        x1, z1, q, k, v = plain_front(tok, params, full)
        beside = None
        k = lax.all_gather(k, "tm", axis=0, tiled=True)
        v = lax.all_gather(v, "tm", axis=0, tiled=True)
        o, lse = attend(q, k, v, windows, segq, segk, off)
    segx = lax.dynamic_slice_in_dim(jnp.pad(segk[0], (8, 8), constant_values=-1), off[0], count + 16)[:, None]
    x2, c1, c2, u, y, sums = convolve(x1, o, params, segx, full, 3)
    output, g3, dn, totals, small_d, grads, grads_b = middle(x2, y, sums, cotangent.reshape(count, width), params, full, frames, 4)
    share = lax.psum_scatter(grads_b.reshape(R, -1, 1024), "rows", scatter_dimension=0, tiled=False)
    g2, dob, small_c, grads = convolve_back(dn, y, sums, totals, c1, c2, u, x2, g3, o, params, segx, full, grads, frames, 5)
    dq, dk, dv, dtable = attend_back(q, k, v, windows, segq, segk, off, o, lse, dob)
    if not links:
        dk = lax.psum_scatter(dk, "tm", scatter_dimension=0, tiled=True)
        dv = lax.psum_scatter(dv, "tm", scatter_dimension=0, tiled=True)
    g1, small_e, grads = rear(x1, g2, dq, dk, dv, params, full, beside, grads, 6)

    rel = lax.dot_general(dtable.reshape(HEADS, length), hot, (((1,), (1,)), ((), ())), precision=HIGH).reshape(1, 1024)
    d = jnp.sum(small_d.reshape(12, 8, 1024), axis=1)
    c = jnp.sum(small_c.reshape(10, 8, 1024), axis=1)
    e = jnp.sum(small_e.reshape(4, 8, 1024), axis=1)
    if links:
        l = jnp.zeros((7, 1024), F32)
    else:
        dtok, small_l, grads = plain_last(tok, g1, z1, params, full, grads)
        l = jnp.sum(small_l.reshape(7, 8, 1024), axis=1)
    rows = jnp.concatenate([
        l[5:6], e[2:3], c[7:8], d[7:8], d[0:1], d[10:11],
        l[6:7], e[3:4], c[8:9], d[8:9], d[1:2], d[11:12], l[0:1], e[0:2], c[9:10], c[5:7], d[9:10], d[2:3],
        l[1:5], d[3:7], c[0:5], rel])
    slots = slot_rows(rows, R)
    if links:
        dtok, *shards, small, late, share, _ = last(tok, g1, z1, params, full, slots, share, grads, [w.shape for w in weights[:7]], 1)
        shards = tuple(shards)
    else:
        shard = lax.psum(lax.psum_scatter(grads.reshape(R, -1, 1024), "rows", scatter_dimension=0, tiled=False), "tm").astype(F32)
        shards = unpack_shard(shard, weights[:7])
        small = lax.psum(lax.psum_scatter(slots, "rows", scatter_dimension=0, tiled=False), "tm")
        share = lax.psum(share, "tm").astype(F32)
    rows = small.reshape(-1)[: 34 * (1024 // R)].reshape(34, 1024 // R)
    if links:
        odd = lax.rem(lax.axis_index("rows"), 2) == 1
        mine = jnp.where(odd, late[0:3, 64:], late[0:3, :64])
        rows = jnp.concatenate([mine[1:2], rows[1:6], mine[2:3], rows[7:12], mine[0:1], rows[13:20], late[3:5].reshape(4, 64), rows[24:]])
    return (output.reshape(tokens.shape), dtok.reshape(tokens.shape)) + shards + (share,) + split_rows(rows)


def solution(mesh):
    return jax.shard_map(
        body,
        mesh=mesh,
        in_specs=(
            P("rows", "tm", None),
            P("rows", "tm", None),
            P("rows", "tm"),
            P(),
            P("rows", None),
            P("rows", None),
            P("rows", None),
            P("rows", None),
            P("rows", None),
            P("rows", None),
            P("rows", None),
            P("rows", None),
            P(None, "rows"),
            P(None, "rows"),
            P(None, "rows"),
            P(None, "rows"),
            P("rows"),
        ),
        out_specs=(
            P("rows", "tm", None),
            P("rows", "tm", None),
            P("rows", None),
            P("rows", None),
            P("rows", None),
            P("rows", None),
            P("rows", None),
            P("rows", None),
            P("rows", None),
            P("rows", None),
            P(None, "rows"),
            P(None, "rows"),
            P(None, "rows"),
            P(None, "rows"),
            P("rows"),
        ),
        check_vma=False,
    )
```
